32 devices in a mesh: shot: 4 (over y, x), dom: 8 (over z, core).
Axes of the slice: x: 2, y: 2, z: 4, core: 2. Of those that a mesh axis runs over, the one named last changes fastest.
Arguments:
- velocity: float32 [256, 32, 128], P('dom'), may hold values from 1.5 to 3
- noise_field: float32 [256, 32, 128], P('dom'), may hold values from -6 to 6
- step_size: float32 [1], replicated, may hold values from 0.05 to 0.5
- field_prev: float32 [8, 256, 32, 128], P('shot', 'dom'), may hold values from -6 to 6
- field_now: float32 [8, 256, 32, 128], P('shot', 'dom'), may hold values from -6 to 6
- adjoint_next: float32 [8, 256, 32, 128], P('shot', 'dom'), may hold values from -6 to 6
- adjoint_now: float32 [8, 256, 32, 128], P('shot', 'dom'), may hold values from -6 to 6
- wavelet: float32 [8, 4], P('shot'), may hold values from -8 to 8
- source_cells: int32 [8, 8], P('shot'), may hold values from 0 to 1048575
- source_signs: int32 [8, 8], P('shot'), may hold values from 0 to 1
- record_cells: int32 [8, 256], P('shot'), may hold values from 0 to 1048575
- observed: float32 [8, 4, 256], P('shot'), may hold values from -6 to 6
Outputs:
- new_velocity: float32 [256, 32, 128], P('dom', None, 'shot')
The draws below stay inside these ranges and needn't reach their ends.
Inputs may be any that keep to these rules, and one draw needn't show every extreme that they name: `source_signs`: 0 stands for a negative sign, 1 for a positive one. `source_cells`: cells flattened as x 32 * 128 + z * 128 + y. `record_cells`: cells flattened as x 32 * 128 + z * 128 + y.
All inputs are finite; a program needn't handle non-finite values.
Results may differ from the reference program's by a relative error of at most 0.00009.
Values sent between devices are 32-bit elements; how exact they have to be, the bound alone decides.
A program may use at most 128 MiB of HBM per device.

```python
import math
import jax
import jax.numpy as jnp
from jax import lax

NZ = 32
NY = 128
STEPS = 4
NSRC = 8
NREC = 256
NX = 256
SHOTS = 8
KC = 8


def draw_noise_field(key, part):
    sample = jax.random.normal(key, (NX, NZ, NY), jnp.float32)
    return jnp.clip(sample, -5.0, 5.0)


def touch_ends(result, rng, least, largest):
    longest = result.shape.index(max(result.shape))
    spots = []
    for shift in (0, 1):
        where = [jax.random.randint(jax.random.fold_in(rng, axis), (), 0, length) for axis, length in enumerate(result.shape)]
        where[longest] = (where[longest] + shift) % result.shape[longest]
        spots.append(tuple(where))
    return result.at[spots[0]].set(least).at[spots[1]].set(largest)


def shard_levels(key, dims, pieces, smallest, top_value):
    factor_of, own = 1.0, jax.random.fold_in(key, 6)
    for dim, shards_of in pieces:
        draws = jnp.exp(jax.random.uniform(jax.random.fold_in(own, dim), (shards_of,), jnp.float32, smallest / len(pieces), top_value / len(pieces)))
        factor_of = factor_of * jnp.repeat(draws, dims[dim] // shards_of).reshape([-1 if axis == dim else 1 for axis in range(len(dims))])
    return factor_of


def centred(stream_key, extent, width, reach, cuts=(), kind=jnp.bfloat16):
    values = width * jax.random.normal(stream_key, extent, jnp.float32)
    if cuts:
        values = values * shard_levels(stream_key, extent, cuts, -0.22, 0.18)
    return jnp.clip(values, -reach, reach).astype(kind)


def setup_inputs(seed: int = 0) -> dict:
    key_of = jax.random.split(jax.random.key(seed), 13)
    return {
        "velocity": jnp.clip(1.5 + 1.5 * jax.random.uniform(key_of[0], (NX, NZ, NY), jnp.float32) ** shard_levels(key_of[0], (NX, NZ, NY), ((0, 8),), -0.2, 0.2), 1.5, 3.0),
        "noise_field": draw_noise_field(jax.random.fold_in(key_of[12], 71), 0),
        "step_size": jnp.clip(jnp.exp(jax.random.uniform(key_of[2], (1,), jnp.float32, math.log(0.05), math.log(0.5))), 0.05, 0.5),
        "field_prev": centred(key_of[3], (SHOTS, NX, NZ, NY), 1.0, 6.0, ((0, 4), (1, 8)), jnp.float32),
        "field_now": centred(key_of[4], (SHOTS, NX, NZ, NY), 1.0, 6.0, ((0, 4), (1, 8)), jnp.float32),
        "adjoint_next": centred(key_of[5], (SHOTS, NX, NZ, NY), 1.0, 6.0, ((0, 4), (1, 8)), jnp.float32),
        "adjoint_now": centred(key_of[6], (SHOTS, NX, NZ, NY), 1.0, 6.0, ((0, 4), (1, 8)), jnp.float32),
        "wavelet": centred(key_of[7], (SHOTS, STEPS), 2.0, 8.0, ((0, 4),), jnp.float32),
        "source_cells": touch_ends(jax.random.randint(key_of[8], (SHOTS, NSRC), 0, NX * NY * NZ), jax.random.fold_in(key_of[8], 1), 0, (NX * NY * NZ) - 1).astype(jnp.int32),
        "source_signs": touch_ends(jax.random.randint(key_of[9], (SHOTS, NSRC), 0, 2), jax.random.fold_in(key_of[9], 1), 0, 1).astype(jnp.int32),
        "record_cells": touch_ends(jax.random.randint(key_of[10], (SHOTS, NREC), 0, NX * NY * NZ), jax.random.fold_in(key_of[10], 1), 0, (NX * NY * NZ) - 1).astype(jnp.int32),
        "observed": centred(key_of[11], (SHOTS, STEPS, NREC), 1.0, 6.0, ((0, 4),), jnp.float32),
    }


COEFFS = (-205.0 / 72.0, 8.0 / 5.0, -1.0 / 5.0, 8.0 / 315.0, -1.0 / 560.0)
COURANT = 0.02

def stencil(padded):
    margin = 4
    rank = padded.ndim
    lengths = [padded.shape[rank - 3 + place] - 2 * margin for place in range(3)]

    def window(offsets):
        sliced = padded
        for place in range(3):
            begin = margin + offsets[place]
            sliced = lax.slice_in_dim(sliced, begin, begin + lengths[place], axis=rank - 3 + place)
        return sliced
    summed = 3.0 * COEFFS[0] * window((0, 0, 0))
    for distance in range(1, 5):
        beside_all = window((distance, 0, 0)) + window((-distance, 0, 0))
        beside_all = beside_all + window((0, distance, 0)) + window((0, -distance, 0))
        beside_all = beside_all + window((0, 0, distance)) + window((0, 0, -distance))
        summed = summed + COEFFS[distance] * beside_all
    return summed

def cosine_basis(length):
    wave_index = jnp.arange(length, dtype=jnp.int32)[:, None]
    position = jnp.arange(length, dtype=jnp.int32)[None, :]
    phase = wave_index * (2 * position + 1) % (4 * length)
    angle = math.pi / (2.0 * length) * phase.astype(jnp.float32)
    factor = jnp.where(wave_index == 0, math.sqrt(1.0 / length), math.sqrt(2.0 / length)).astype(jnp.float32)
    return factor * jnp.cos(angle)

def prior_gain(length, cutoff):
    scaled = jnp.arange(length, dtype=jnp.float32) / float(cutoff)
    return 1.0 / jnp.sqrt(1.0 + scaled)

def reference(velocity, noise_field, step_size, field_prev, field_now, adjoint_next, adjoint_now, wavelet, source_cells, source_signs, record_cells, observed):
    speed_sq = COURANT * velocity * velocity
    grid_shape = velocity.shape

    def one_shot(carry, inputs):
        prior, current, adj_later, adj_current, pulse, sources, signs, records, measured = inputs
        amplitude = (2 * signs - 1).astype(jnp.float32)
        laplacians = []
        samples = []
        for moment in range(STEPS):
            spread = stencil(jnp.pad(current, 4))
            laplacians.append(spread)
            advanced = 2.0 * current - prior + speed_sq * spread
            advanced = advanced.reshape(-1).at[sources].add(amplitude * pulse[moment]).reshape(grid_shape)
            samples.append(advanced.reshape(-1)[records])
            prior, current = (current, advanced)
        summed = jnp.zeros(grid_shape, jnp.float32)
        for moment in range(STEPS, 0, -1):
            misfit = samples[moment - 1] - measured[moment - 1]
            spread = stencil(jnp.pad(adj_current, 4))
            earlier = 2.0 * adj_current - adj_later + speed_sq * spread
            earlier = earlier.reshape(-1).at[records].add(misfit).reshape(grid_shape)
            adj_later, adj_current = (adj_current, earlier)
            summed = summed + adj_current * laplacians[moment - 1]
        return (carry + summed, None)
    start_total = jnp.zeros(grid_shape, jnp.float32)
    total = lax.scan(one_shot, start_total, (field_prev, field_now, adjoint_next, adjoint_now, wavelet, source_cells, source_signs, record_cells, observed))[0]
    gradient = 2.0 * COURANT * velocity * total
    basis = cosine_basis(NX)
    spectrum = prior_gain(NX, KC)[:, None]
    columns = NY * NZ
    highest = lax.Precision.HIGHEST
    grad_hat = jnp.dot(basis, gradient.reshape(NX, columns), precision=highest)
    noise_hat = jnp.dot(basis, noise_field.reshape(NX, columns), precision=highest)
    rate = step_size[0]
    weights = spectrum * (-0.5 * rate * spectrum * grad_hat + jnp.sqrt(rate) * noise_hat)
    update = lax.dot_general(basis, weights, (((0,), (0,)), ((), ())), precision=highest)
    return velocity + update.reshape(NX, NZ, NY)
```

```python
import functools
import math

import jax
import jax.numpy as jnp
import numpy as np
from jax import lax
from jax.experimental import pallas as pl
from jax.experimental.pallas import tpu as pltpu
from jax.sharding import PartitionSpec as P

STEPS = 4


COEFFS = (-205.0 / 72.0, 8.0 / 5.0, -1.0 / 5.0, 8.0 / 315.0, -1.0 / 560.0)
COURANT = 0.02


MARGIN = 4
MESH = pl.DeviceIdType.MESH


REACH = 2 * MARGIN
BORDER = 3 * MARGIN
WEIGHTS = (-43050.0, 8064.0, -1008.0, 128.0, -9.0)
SCALE = 5040.0


def split_two(value):
    high = value.astype(jnp.bfloat16)
    low = (value - high.astype(jnp.float32)).astype(jnp.bfloat16)
    return high, low


def banded(size, block, centre):
    down = lax.broadcasted_iota(jnp.int32, (size, size), 0)
    over = lax.broadcasted_iota(jnp.int32, (size, size), 1)
    apart = jnp.abs(down - over)
    band = jnp.where(apart == 0, centre, 0.0)
    for r in range(1, MARGIN + 1):
        band = jnp.where(apart == r, WEIGHTS[r], band)
    if block < size:
        band = jnp.where(down // block == over // block, band, 0.0)
    return band.astype(jnp.bfloat16)


def wave_kernel(
    doms,
    now_hbm,
    adj_hbm,
    prev_hbm,
    later_hbm,
    speed_hbm,
    pulse,
    src_cells,
    src_signs,
    record_cells,
    observed,
    out,
    f0,
    f1,
    f2,
    f3,
    f4,
    a4,
    a3,
    a2,
    a1,
    prev,
    later,
    speed,
    squares,
    laps,
    mf0,
    mf1,
    ma0,
    ma1,
    hf0,
    hf1,
    ha,
    across_y,
    across_z,
    spread_src,
    landed,
    pick,
    put,
    hot,
    columns,
    measured,
    found,
    beside,
    values,
    total,
    load_sem,
    send_sem,
    recv_sem,
):
    fields = (f0, f1, f2, f3, f4)
    mf, hf, ma = (mf0, mf1), (hf0, hf1), (ma0, ma1)
    shots, rows, depth, width = prev.shape
    here = lax.axis_index("dom")
    left = jnp.maximum(here - 1, 0)
    right = jnp.minimum(here + 1, doms - 1)
    has_left = here > 0
    has_right = here < doms - 1
    group = MARGIN
    groups = rows // group
    half = 16
    halves = depth // half
    f32 = jnp.float32

    loads = [
        pltpu.make_async_copy(now_hbm, f0.at[:, pl.ds(MARGIN, rows)], load_sem.at[0]),
        pltpu.make_async_copy(speed_hbm, speed.at[pl.ds(REACH, rows)], load_sem.at[1]),
        pltpu.make_async_copy(prev_hbm, prev, load_sem.at[2]),
        pltpu.make_async_copy(adj_hbm, a4.at[:, pl.ds(BORDER, rows)], load_sem.at[3]),
        pltpu.make_async_copy(later_hbm, later, load_sem.at[4]),
    ]
    for load in loads:
        load.start()

    barrier = pltpu.get_barrier_semaphore()

    @pl.when(has_left)
    def _():
        pl.semaphore_signal(barrier, inc=1, device_id={"dom": left}, device_id_type=MESH)

    @pl.when(has_right)
    def _():
        pl.semaphore_signal(barrier, inc=1, device_id={"dom": right}, device_id_type=MESH)

    pl.semaphore_wait(barrier, has_left.astype(jnp.int32) + has_right.astype(jnp.int32))

    pairs = []

    def pair(low_source, high_target, high_source, low_target):
        index = len(pairs)
        to_left = pltpu.make_async_remote_copy(
            src_ref=low_source,
            dst_ref=high_target,
            send_sem=send_sem.at[index, 0],
            recv_sem=recv_sem.at[index, 1],
            device_id={"dom": left},
            device_id_type=MESH,
        )
        to_right = pltpu.make_async_remote_copy(
            src_ref=high_source,
            dst_ref=low_target,
            send_sem=send_sem.at[index, 1],
            recv_sem=recv_sem.at[index, 0],
            device_id={"dom": right},
            device_id_type=MESH,
        )
        pairs.append((to_left, to_right))
        return pairs[-1]

    def send(copies):
        @pl.when(has_left)
        def _():
            copies[0].start()

        @pl.when(has_right)
        def _():
            copies[1].start()

    def receive(copies):
        @pl.when(has_left)
        def _():
            copies[1].wait_recv()

        @pl.when(has_right)
        def _():
            copies[0].wait_recv()

    def sent(copies):
        @pl.when(has_left)
        def _():
            copies[0].wait_send()

        @pl.when(has_right)
        def _():
            copies[1].wait_send()

    halos = []
    for k in range(STEPS):
        halos.append([])
        for s in range(shots):
            field = fields[k]
            source = now_hbm if k == 0 else field
            base = 0 if k == 0 else MARGIN
            halos[k].append(
                pair(
                    source.at[s, pl.ds(base, MARGIN)],
                    field.at[s, pl.ds(MARGIN + rows, MARGIN)],
                    source.at[s, pl.ds(base + rows - MARGIN, MARGIN)],
                    field.at[s, pl.ds(0, MARGIN)],
                )
            )
    adj_halo = pair(
        adj_hbm.at[:, pl.ds(0, REACH)],
        a4.at[:, pl.ds(BORDER + rows, REACH)],
        adj_hbm.at[:, pl.ds(rows - REACH, REACH)],
        a4.at[:, pl.ds(BORDER - REACH, REACH)],
    )
    speed_halo = pair(
        speed_hbm.at[pl.ds(0, REACH)],
        speed.at[pl.ds(REACH + rows, REACH)],
        speed_hbm.at[pl.ds(rows - REACH, REACH)],
        speed.at[pl.ds(0, REACH)],
    )
    border_halo = pair(
        a3.at[:, pl.ds(BORDER, BORDER)],
        a3.at[:, pl.ds(BORDER + rows, BORDER)],
        a3.at[:, pl.ds(rows, BORDER)],
        a3.at[:, pl.ds(0, BORDER)],
    )
    samples = [
        pair(found.at[k], beside.at[k, 1], found.at[k], beside.at[k, 0]) for k in range(STEPS)
    ]

    for s in range(shots):
        send(halos[0][s])
    send(adj_halo)
    send(speed_halo)

    def clear(first_field, first_adj, first_border, first_speed, side):
        for k in range(STEPS):
            for s in range(shots):
                fields[k][s, pl.ds(first_field, MARGIN)] = jnp.zeros((MARGIN, depth, width), f32)
        for s in range(shots):
            a4[s, pl.ds(first_adj, REACH)] = jnp.zeros((REACH, depth, width), f32)
            a3[s, pl.ds(first_border, BORDER)] = jnp.zeros((BORDER, depth, width), f32)
        speed[pl.ds(first_speed, REACH)] = jnp.zeros((REACH, depth, width), f32)
        for k in range(STEPS):
            beside[k, side] = jnp.zeros(beside.shape[2:], f32)

    @pl.when(jnp.logical_not(has_left))
    def _():
        clear(0, BORDER - REACH, 0, 0, 0)

    @pl.when(jnp.logical_not(has_right))
    def _():
        clear(MARGIN + rows, BORDER + rows, BORDER + rows, REACH + rows, 1)

    across_y[...] = jnp.concatenate([banded(width, width, -43008.0)] * 2, axis=0)
    across_z[...] = jnp.concatenate([banded(group * depth, depth, -42.0)] * 2, axis=1)

    receivers = record_cells.shape[1]
    tiles = receivers // 8
    lane = lax.broadcasted_iota(jnp.int32, (8, width), 1)
    first = here * (rows * depth)
    row_of = lambda cell: lax.div(cell, jnp.int32(width))
    lane_of = lambda cell: lax.rem(cell, jnp.int32(width))
    tile = (width, receivers)
    place = lax.broadcasted_iota(jnp.int32, tile, 0)
    span = 8 * depth
    compact = [jnp.zeros((8, width), f32) for _ in range(STEPS)]
    for s in range(shots):
        cells = record_cells[s : s + 1, :]
        rec_rows = row_of(cells) - first
        table = jnp.where(
            place == STEPS,
            jnp.broadcast_to(rec_rows.astype(f32), tile),
            jnp.broadcast_to(lane_of(cells).astype(f32), tile),
        )
        for k in range(STEPS):
            table = jnp.where(place == k, jnp.broadcast_to(observed[s, k : k + 1, :], tile), table)
        columns[s] = jnp.transpose(table)
        rec_col = columns[s, :, STEPS : STEPS + 1].astype(jnp.int32)
        rec_lane = columns[s, :, STEPS + 1 : STEPS + 2].astype(jnp.int32)
        hot[s] = (lax.broadcasted_iota(jnp.int32, (receivers, width), 1) == rec_lane).astype(f32)
        for k in range(STEPS):
            for j in range(tiles):
                column = columns[s, pl.ds(j * 8, 8), k : k + 1]
                compact[k] = jnp.where(lane == s * tiles + j, column, compact[k])
        count = src_cells.shape[1]
        padded = count + (-count) % 128
        order = lax.broadcasted_iota(jnp.int32, (padded, width), 0)
        across = lax.broadcasted_iota(jnp.int32, (padded, width), 1)
        along = lax.broadcasted_iota(jnp.int32, (1, padded), 1)
        tall = jnp.zeros((padded, width), f32)
        src_rows = jnp.full((1, padded), -1, jnp.int32)
        for j in range(count):
            cell = src_cells[s, j]
            sign = (2 * src_signs[s, j] - 1).astype(f32)
            tall = jnp.where((order == j) & (across == lane_of(cell)), sign, tall)
            src_rows = jnp.where(along == j, row_of(cell) - first, src_rows)
        tall = tall.astype(jnp.bfloat16)

        for c in range(rows * depth // span):
            cell = lax.broadcasted_iota(jnp.int32, (receivers, span), 1) + c * span
            pick[s, :, c * span : (c + 1) * span] = (
                (cell == rec_col).astype(f32).astype(jnp.bfloat16)
            )

        @pl.loop(0, rows * depth // span)
        def _(c):
            cell = lax.broadcasted_iota(jnp.int32, (span, padded), 0) + c * span
            wide = (cell == src_rows).astype(f32).astype(jnp.bfloat16)
            spots = jnp.dot(wide, tall, preferred_element_type=f32)
            spread_src[s, pl.ds(c * 8, 8)] = spots.reshape(8, depth, width)

        @pl.loop(0, (rows + 2 * BORDER) // 8)
        def _(c):
            cell = lax.broadcasted_iota(jnp.int32, (span, receivers), 0)
            cell = cell + (c * span - BORDER * depth)
            put[s, pl.ds(pl.multiple_of(c * span, span), span)] = (
                (cell == rec_rows).astype(f32).astype(jnp.bfloat16)
            )

    for k in range(STEPS):
        measured[k] = compact[k]

    def keep_split(ref, s, row, part, value):
        high, low = split_two(value)
        ref[s, row, part, 0:width] = high
        ref[s, row, part, width : 2 * width] = low

    def product(split, split_row, target, target_row):
        lines = [
            split[s, pl.ds(split_row, group)].reshape(group * depth, 2 * width)
            for s in range(shots)
        ]
        highs = jnp.concatenate([line[:, :width] for line in lines], axis=1)
        lows = jnp.concatenate([line[:, width:] for line in lines], axis=1)
        down = jnp.dot(
            across_z[...], jnp.concatenate([highs, lows], axis=0), preferred_element_type=f32
        )
        for s in range(shots):
            over = jnp.dot(lines[s], across_y[...], preferred_element_type=f32)
            both = over + down[:, s * width : (s + 1) * width]
            target[s, pl.ds(target_row, group)] = both.reshape(group, depth, width)

    def beside_x(window, i):
        summed = WEIGHTS[1] * (window[i + 3] + window[i + 5])
        for r in range(2, MARGIN + 1):
            summed += WEIGHTS[r] * (window[i + MARGIN + r] + window[i + MARGIN - r])
        return summed

    def sweep(first, last, point, product_of):
        point(first)

        @pl.loop(first + 1, last)
        def _(g):
            product_of(g - 1)
            point(g)

        product_of(last - 1)

    def square(first, last):
        @pl.loop(first, last)
        def _(x):
            squares[x] = (COURANT / SCALE) * speed[x] * speed[x]

    parts = [pl.ds(h * half, half) for h in range(halves)]

    def prepare(field, margin, split, split_margin, target, target_margin):
        def point(g):
            for s in range(shots):
                for i in range(group):
                    for part in parts:
                        x = g * group + i
                        keep_split(split, s, x + split_margin, part, field[s, x + margin, part])

        sweep(
            0,
            groups,
            point,
            lambda g: product(split, g * group + split_margin, target, g * group + target_margin),
        )

    def forward_point(k, g, which):
        x = g * group
        field, target, split = fields[k], fields[k + 1], hf[(k + 1) % 2]
        for part in parts:
            for s in which:
                window = [field[s, x + i, part] for i in range(group + 2 * MARGIN)]
                for i in range(group):
                    lap = mf[k % 2][s, x + i, part] + beside_x(window, i)
                    laps[k, s, x + i, part] = lap
                    if k == 0:
                        before = prev[s, x + i, part]
                    else:
                        before = fields[k - 1][s, x + i + MARGIN, part]
                    fresh = 2.0 * window[i + MARGIN] - before
                    fresh = fresh + pulse[s, k] * spread_src[s, x + i, part]
                    fresh = fresh + squares[x + i + REACH, part] * lap
                    target[s, x + i + MARGIN, part] = fresh
                    keep_split(split, s, x + i, part, fresh)

    def forward_product(k, g):
        product(hf[(k + 1) % 2], g * group, mf[(k + 1) % 2], g * group)

    def forward_inside(k):
        sweep(
            1,
            groups - 1,
            lambda g: forward_point(k, g, range(shots)),
            lambda g: forward_product(k, g) if k + 1 < STEPS else None,
        )

    def sample(k):
        split = hf[(k + 1) % 2]
        gathered = jnp.zeros((8, width), f32)
        for s in range(shots):
            both = jnp.dot(
                pick[s],
                split[s].reshape(rows * depth, 2 * width),
                preferred_element_type=f32,
            )
            chosen = (both[:, :width] + both[:, width:]) * hot[s]
            column = jnp.sum(chosen, axis=1, keepdims=True)
            for j in range(tiles):
                gathered = jnp.where(
                    lane == s * tiles + j, column[j * 8 : (j + 1) * 8], gathered
                )
        found[k] = gathered

    def misfits(k, everywhere):
        missed = found[k] - measured[k]
        if everywhere:
            missed = missed + (beside[k, 0] + beside[k, 1])
        for s in range(shots):
            for j in range(0, tiles, 2):
                block = []
                for t in (j, j + 1):
                    at = s * tiles + t
                    block.append(missed[:, at : at + 1] * hot[s, pl.ds(t * 8, 8)])
                high, low = split_two(jnp.concatenate(block, axis=0))
                values[s, pl.ds(j * 8, 16), 0:width] = high
                values[s, pl.ds(j * 8, 16), width : 2 * width] = low

    def dropped(s, x, count):
        at = pl.multiple_of((x + BORDER) * depth, group * depth)
        both = jnp.dot(put[s, pl.ds(at, count * depth)], values[s], preferred_element_type=f32)
        return (both[:, :width] + both[:, width:]).reshape(count, depth, width)

    def land(k, extra):
        @pl.loop(-extra // 8, (rows + extra) // 8)
        def _(c):
            for s in range(shots):
                landed[k, s, pl.ds(c * 8 + REACH, 8)] = dropped(s, c * 8, 8)

    def free_point(g):
        x = g * group
        for part in parts:
            for s in range(shots):
                window = [
                    a4[s, x + BORDER - MARGIN + i, part] for i in range(group + 2 * MARGIN)
                ]
                for i in range(group):
                    lap = ma0[s, x + i + BORDER, part] + beside_x(window, i)
                    fresh = 2.0 * window[i + MARGIN] - later[s, x + i, part]
                    a3[s, x + i + BORDER, part] = fresh + squares[x + i + REACH, part] * lap

    def drop_point(g, inside):
        x = g * group
        gathered = None
        for s in range(shots):
            fresh = a3[s, pl.ds(x + BORDER, group)] + dropped(s, x, group)
            a3[s, pl.ds(x + BORDER, group)] = fresh
            high, low = split_two(fresh)
            ha[s, pl.ds(x + BORDER, group), :, 0:width] = high
            ha[s, pl.ds(x + BORDER, group), :, width : 2 * width] = low
            if inside:
                term = fresh * laps[STEPS - 1, s, pl.ds(x, group)]
                gathered = term if gathered is None else gathered + term
        if inside:
            total[pl.ds(x, group)] = gathered

    adj = {4: a4, 3: a3, 2: a2, 1: a1}
    adj_mix = {4: ma0, 3: ma1, 2: ma0, 1: ma1}

    def adj_product(m, g):
        product(ha, g * group + BORDER, adj_mix[m], g * group + BORDER)

    def backward_point(m, g, inside):
        x = g * group
        field, after = adj[m], adj[m + 1]
        for part in parts:
            gathered = [None] * group
            for s in range(shots):
                window = [
                    field[s, x + BORDER - MARGIN + i, part] for i in range(group + 2 * MARGIN)
                ]
                for i in range(group):
                    lap = adj_mix[m][s, x + i + BORDER, part] + beside_x(window, i)
                    fresh = 2.0 * window[i + MARGIN] - after[s, x + i + BORDER, part]
                    fresh = fresh + landed[m - 1, s, x + i + REACH, part]
                    fresh = fresh + squares[x + i + REACH, part] * lap
                    if m > 1:
                        adj[m - 1][s, x + i + BORDER, part] = fresh
                        keep_split(ha, s, x + i + BORDER, part, fresh)
                    if inside:
                        term = fresh * laps[m - 1, s, x + i, part]
                        gathered[i] = term if gathered[i] is None else gathered[i] + term
            if inside:
                for i in range(group):
                    summed = total[x + i, part] + gathered[i]
                    if m > 1:
                        total[x + i, part] = summed
                    else:
                        factor = (2.0 * COURANT / SCALE) * speed[x + i + REACH, part]
                        out[x + i, part] = factor * summed

    def backward(m, first, last, inside):
        sweep(
            first,
            last,
            lambda g: backward_point(m, g, inside),
            lambda g: adj_product(m - 1, g) if m > 1 else None,
        )

    for load in loads[:3]:
        load.wait()
    square(REACH, REACH + rows)
    prepare(f0, MARGIN, hf0, 0, mf0, 0)
    forward_inside(0)
    for k in range(STEPS):
        for s in range(shots):
            receive(halos[k][s])
            forward_point(k, 0, (s,))
            forward_point(k, groups - 1, (s,))
            if k + 1 < STEPS:
                send(halos[k + 1][s])
        if k + 1 < STEPS:
            forward_product(k, 0)
            forward_product(k, groups - 1)
            forward_inside(k + 1)
        sample(k)
        send(samples[k])
        if k == 0:
            for load in loads[3:]:
                load.wait()
            prepare(a4, BORDER, ha, BORDER, ma0, BORDER)
            receive(adj_halo)

            @pl.loop(0, groups)
            def _(g):
                free_point(g)

            send(border_halo)
            receive(speed_halo)
            square(0, REACH)
            square(REACH + rows, 2 * REACH + rows)
        if k > 0:
            receive(samples[k - 1])
            misfits(k - 1, True)
            land(k - 1, {1: 0, 2: REACH, 3: REACH}[k])

    sent(border_halo)
    misfits(STEPS - 1, False)
    sweep(0, groups, lambda g: drop_point(g, True), lambda g: adj_product(3, g))
    backward(3, 1, groups - 1, True)
    receive(samples[STEPS - 1])
    misfits(STEPS - 1, True)
    receive(border_halo)
    edge = BORDER // group
    sweep(-edge, 0, lambda g: drop_point(g, False), lambda g: adj_product(3, g))
    sweep(
        groups,
        groups + edge,
        lambda g: drop_point(g, False),
        lambda g: adj_product(3, g),
    )
    edge -= 1
    backward(3, -edge, 0, False)
    backward(3, groups, groups + edge, False)
    for g in (0, groups - 1):
        backward_point(3, g, True)
        adj_product(2, g)
    edge -= 1
    for g in (-1, groups):
        backward_point(2, g, False)
        adj_product(1, g)
    backward(2, 0, groups, True)
    backward(1, 0, groups, True)
    for copies in pairs:
        if copies is not border_halo:
            sent(copies)


def shot_gradient(
    velocity, prev, now, later, adjoint, wavelet, source_cells, signs, record_cells, observed
):
    shots, rows, depth, width = now.shape
    receivers = record_cells.shape[1]
    hbm = pl.BlockSpec(memory_space=pl.ANY)
    vmem = pl.BlockSpec(memory_space=pltpu.VMEM)
    smem = pl.BlockSpec(memory_space=pltpu.SMEM)
    f32, bf16 = jnp.float32, jnp.bfloat16
    group = MARGIN
    wide = rows + 2 * REACH
    widest = rows + 2 * BORDER
    exchanges = STEPS * shots + 3 + STEPS
    return pl.pallas_call(
        functools.partial(wave_kernel, lax.axis_size("dom")),
        out_shape=jax.ShapeDtypeStruct((rows, depth, width), f32),
        in_specs=[hbm] * 5 + [smem] * 3 + [vmem] * 2,
        out_specs=vmem,
        scratch_shapes=[pltpu.VMEM((shots, rows + 2 * MARGIN, depth, width), f32)] * (STEPS + 1)
        + [pltpu.VMEM((shots, widest, depth, width), f32)] * STEPS
        + [
            pltpu.VMEM((shots, rows, depth, width), f32),
            pltpu.VMEM((shots, rows, depth, width), f32),
            pltpu.VMEM((wide, depth, width), f32),
            pltpu.VMEM((wide, depth, width), f32),
            pltpu.VMEM((STEPS, shots, rows, depth, width), f32),
            pltpu.VMEM((shots, rows, depth, width), f32),
            pltpu.VMEM((shots, rows, depth, width), f32),
            pltpu.VMEM((shots, widest, depth, width), f32),
            pltpu.VMEM((shots, widest, depth, width), f32),
            pltpu.VMEM((shots, rows, depth, 2 * width), bf16),
            pltpu.VMEM((shots, rows, depth, 2 * width), bf16),
            pltpu.VMEM((shots, widest, depth, 2 * width), bf16),
            pltpu.VMEM((2 * width, width), bf16),
            pltpu.VMEM((group * depth, 2 * group * depth), bf16),
            pltpu.VMEM((shots, rows, depth, width), f32),
            pltpu.VMEM((STEPS - 1, shots, wide, depth, width), f32),
            pltpu.VMEM((shots, receivers, rows * depth), bf16),
            pltpu.VMEM((shots, widest * depth, receivers), bf16),
            pltpu.VMEM((shots, receivers, width), f32),
            pltpu.VMEM((shots, receivers, width), f32),
            pltpu.VMEM((STEPS, 8, width), f32),
            pltpu.VMEM((STEPS, 8, width), f32),
            pltpu.VMEM((STEPS, 2, 8, width), f32),
            pltpu.VMEM((shots, receivers, 2 * width), bf16),
            pltpu.VMEM((rows, depth, width), f32),
            pltpu.SemaphoreType.DMA((5,)),
            pltpu.SemaphoreType.DMA((exchanges, 2)),
            pltpu.SemaphoreType.DMA((exchanges, 2)),
        ],
        compiler_params=pltpu.CompilerParams(
            collective_id=0, has_side_effects=True, vmem_limit_bytes=56 * 1024 * 1024
        ),
    )(
        now,
        adjoint,
        prev,
        later,
        velocity,
        wavelet,
        source_cells,
        signs,
        record_cells,
        observed,
    )


def cosine_basis(length):
    wave_index = jnp.arange(length, dtype=jnp.int32)[:, None]
    position = jnp.arange(length, dtype=jnp.int32)[None, :]
    phase = wave_index * (2 * position + 1) % (4 * length)
    angle = math.pi / (2.0 * length) * phase.astype(jnp.float32)
    factor = jnp.where(wave_index == 0, math.sqrt(1.0 / length), math.sqrt(2.0 / length)).astype(
        jnp.float32
    )
    return factor * jnp.cos(angle)


def prior_gain(length, cutoff):
    scaled = jnp.arange(length, dtype=jnp.float32) / float(cutoff)
    return 1.0 / jnp.sqrt(1.0 + scaled)


def precondition(gradient, noise_cols, rate):
    length = gradient.shape[0]
    basis = cosine_basis(length)
    spectrum = prior_gain(length, length // 32)[:, None]
    highest = lax.Precision.HIGHEST
    grad_hat = jnp.dot(basis, gradient.reshape(length, -1), precision=highest)
    noise_hat = jnp.dot(basis, noise_cols.reshape(length, -1), precision=highest)
    weights = spectrum * (-0.5 * rate * spectrum * grad_hat + jnp.sqrt(rate) * noise_hat)
    update = lax.dot_general(basis, weights, (((0,), (0,)), ((), ())), precision=highest)
    return update.reshape(gradient.shape)


def shared_kernel(
    shots,
    doms,
    partial,
    noise,
    basis,
    basis_t,
    gain,
    step_size,
    out,
    folded,
    noise_fold,
    sums,
    own,
    noise_lines,
    grad_lines,
    update,
    returned,
    send_sem,
    recv_sem,
    shot_send,
    shot_recv,
):
    depth, rows, width = shots * folded.shape[1], folded.shape[2], folded.shape[3]
    fold = folded.shape[1]
    lot = fold // doms
    lane_share = width // shots
    me = lax.axis_index("shot")
    here = lax.axis_index("dom")
    dom_peer = [lax.rem(here + o, doms) for o in range(doms)]
    shot_peer = [lax.rem(me + o, shots) for o in range(shots)]

    barrier = pltpu.get_barrier_semaphore()
    for o in range(1, doms):
        pl.semaphore_signal(barrier, inc=1, device_id={"dom": dom_peer[o]}, device_id_type=MESH)
    for o in range(1, shots):
        pl.semaphore_signal(barrier, inc=1, device_id={"shot": shot_peer[o]}, device_id_type=MESH)

    group = lax.broadcasted_iota(jnp.int32, (rows, width), 1) // lane_share

    def fold_lanes(source, target):
        @pl.loop(0, fold)
        def _(level):
            slabs = [
                source[pl.ds(block * fold + level, rows, stride=depth), :]
                for block in range(shots)
            ]
            for share in range(shots):
                merged = None
                for block in range(shots):
                    shift = (block - share) * lane_share % width
                    turned = pltpu.roll(slabs[block], shift, 1) if shift else slabs[block]
                    merged = turned if merged is None else jnp.where(group == block, turned, merged)
                target[share, level] = merged

    def exchange(phase, source_of, target):
        moves = []
        for o in range(1, doms):
            moves.append(
                pltpu.make_async_remote_copy(
                    src_ref=source_of(dom_peer[o]),
                    dst_ref=target.at[here],
                    send_sem=send_sem.at[phase, o],
                    recv_sem=recv_sem.at[phase, o],
                    device_id={"dom": dom_peer[o]},
                    device_id_type=MESH,
                )
            )
        return moves

    fold_lanes(partial, folded)
    pl.semaphore_wait(barrier, doms + shots - 2)
    sharing = []
    for o in range(1, shots):
        move = pltpu.make_async_remote_copy(
            src_ref=folded.at[shot_peer[o]],
            dst_ref=sums.at[o],
            send_sem=shot_send.at[o],
            recv_sem=shot_recv.at[o],
            device_id={"shot": shot_peer[o]},
            device_id_type=MESH,
        )
        move.start()
        sharing.append(move)
    fold_lanes(noise, noise_fold)
    noise_moves = exchange(0, lambda d: noise_fold.at[me, pl.ds(d * lot, lot)], noise_lines)
    for move in noise_moves:
        move.start()
    noise_lines[here] = noise_fold[me, pl.ds(here * lot, lot)]
    for move in noise_moves:
        move.wait_recv()
    rate = step_size[0]
    highest = lax.Precision.HIGHEST
    lines = doms * rows
    noise_hats = [
        jnp.dot(
            basis[...],
            noise_lines[:, i].reshape(lines, width),
            precision=highest,
            preferred_element_type=jnp.float32,
        )
        for i in range(lot)
    ]
    root = jnp.sqrt(jnp.full((1, 1), rate, jnp.float32))
    for move in sharing:
        move.wait_recv()
    gathered = folded[me]
    for o in range(1, shots):
        gathered = gathered + sums[o]
    own[...] = gathered
    grad_moves = exchange(1, lambda d: own.at[pl.ds(d * lot, lot)], grad_lines)
    for move in grad_moves:
        move.start()
    grad_lines[here] = own[pl.ds(here * lot, lot)]
    for move in grad_moves:
        move.wait_recv()
    for i in range(lot):
        grad_hat = jnp.dot(
            basis[...],
            grad_lines[:, i].reshape(lines, width),
            precision=highest,
            preferred_element_type=jnp.float32,
        )
        weights = gain[...] * (-0.5 * rate * gain[...] * grad_hat + root * noise_hats[i])
        update[:, i] = jnp.dot(
            basis_t[...], weights, precision=highest, preferred_element_type=jnp.float32
        ).reshape(doms, rows, width)
    back_moves = exchange(2, lambda d: update.at[d], returned)
    for move in back_moves:
        move.start()
    returned[here] = update[here]
    for move in back_moves:
        move.wait_recv()
    for d in range(doms):
        for i in range(lot):
            line = returned[d, i]
            for block in range(shots):
                shift = -block * lane_share % width
                turned = pltpu.roll(line, shift, 1) if shift else line
                out[pl.ds(block * fold + d * lot + i, rows, stride=depth), :] = turned
    for move in sharing + noise_moves + grad_moves + back_moves:
        move.wait_send()


def shared_update(partial_value, noise_field, step_size):
    rows, depth, width = partial_value.shape
    shots, doms = lax.axis_size("shot"), lax.axis_size("dom")
    length = rows * doms
    fold = depth // shots
    lot = fold // doms
    wave = np.arange(length)[:, None]
    phase = wave * (2 * np.arange(length)[None, :] + 1) % (4 * length)
    factor = np.where(wave == 0, math.sqrt(1.0 / length), math.sqrt(2.0 / length))
    basis = (factor * np.cos(math.pi / (2.0 * length) * phase)).astype(np.float32)
    gain = (1.0 / np.sqrt(1.0 + wave / (length // 32))).astype(np.float32)
    f32 = jnp.float32
    vmem = pl.BlockSpec(memory_space=pltpu.VMEM)
    smem = pl.BlockSpec(memory_space=pltpu.SMEM)
    result = pl.pallas_call(
        functools.partial(shared_kernel, shots, doms),
        out_shape=jax.ShapeDtypeStruct((rows * depth, width), f32),
        in_specs=[vmem] * 5 + [smem],
        out_specs=vmem,
        scratch_shapes=[
            pltpu.VMEM((shots, fold, rows, width), f32),
            pltpu.VMEM((shots, fold, rows, width), f32),
            pltpu.VMEM((shots, fold, rows, width), f32),
            pltpu.VMEM((fold, rows, width), f32),
            pltpu.VMEM((doms, lot, rows, width), f32),
            pltpu.VMEM((doms, lot, rows, width), f32),
            pltpu.VMEM((doms, lot, rows, width), f32),
            pltpu.VMEM((doms, lot, rows, width), f32),
            pltpu.SemaphoreType.DMA((3, doms)),
            pltpu.SemaphoreType.DMA((3, doms)),
            pltpu.SemaphoreType.DMA((shots,)),
            pltpu.SemaphoreType.DMA((shots,)),
        ],
        compiler_params=pltpu.CompilerParams(
            collective_id=1, has_side_effects=True, vmem_limit_bytes=32 * 1024 * 1024
        ),
    )(
        partial_value.reshape(rows * depth, width),
        noise_field.reshape(rows * depth, width),
        jnp.asarray(basis),
        jnp.asarray(np.ascontiguousarray(basis.T)),
        jnp.asarray(gain),
        step_size,
    )
    return result.reshape(rows, depth, width)[:, :, : width // shots]


def body(
    velocity,
    noise_field,
    step_size,
    field_prev,
    field_now,
    adjoint_next,
    adjoint_now,
    wavelet,
    source_cells,
    source_signs,
    record_cells,
    observed,
):
    partial_value = shot_gradient(
        velocity,
        field_prev,
        field_now,
        adjoint_next,
        adjoint_now,
        wavelet,
        source_cells,
        source_signs,
        record_cells,
        observed,
    )
    rate = step_size[0]
    shot_rows = velocity.shape[2] // lax.axis_size("shot")
    start = lax.axis_index("shot") * shot_rows
    if velocity.shape[1] % (lax.axis_size("shot") * lax.axis_size("dom")) == 0:
        moved = shared_update(partial_value, noise_field, step_size)
        return lax.dynamic_slice_in_dim(velocity, start, shot_rows, 2) + moved
    share = lax.psum_scatter(partial_value, "shot", scatter_dimension=2, tiled=True)
    noise_part = lax.dynamic_slice_in_dim(noise_field, start, shot_rows, 2)
    grad_cols, noise_cols = (
        lax.all_to_all(share, "dom", split_axis=2, concat_axis=0, tiled=True),
        lax.all_to_all(noise_part, "dom", split_axis=2, concat_axis=0, tiled=True),
    )
    update = precondition(grad_cols, noise_cols, rate)
    returned = lax.all_to_all(update, "dom", split_axis=0, concat_axis=2, tiled=True)
    result = lax.dynamic_slice_in_dim(velocity, start, shot_rows, 2) + returned
    return result


def solution(mesh):
    placed = (
        P("dom", None, None),
        P("dom", None, None),
        P(),
        P("shot", "dom", None, None),
        P("shot", "dom", None, None),
        P("shot", "dom", None, None),
        P("shot", "dom", None, None),
        P("shot", None),
        P("shot", None),
        P("shot", None),
        P("shot", None),
        P("shot", None, None),
    )
    return jax.shard_map(
        body, mesh=mesh, in_specs=placed, out_specs=P("dom", None, "shot"), check_vma=False
    )
```

```python
import functools
import math

import jax
import jax.numpy as jnp
import numpy as np
from jax import lax
from jax.experimental import pallas as pl
from jax.experimental.pallas import tpu as pltpu
from jax.sharding import PartitionSpec as P

STEPS = 4


COEFFS = (-205.0 / 72.0, 8.0 / 5.0, -1.0 / 5.0, 8.0 / 315.0, -1.0 / 560.0)
COURANT = 0.02


MARGIN = 4
MESH = pl.DeviceIdType.MESH


REACH = 2 * MARGIN
BORDER = 3 * MARGIN
WEIGHTS = (-43050.0, 8064.0, -1008.0, 128.0, -9.0)
SCALE = 5040.0


def split_two(value):
    high = value.astype(jnp.bfloat16)
    low = (value - high.astype(jnp.float32)).astype(jnp.bfloat16)
    return high, low


def banded(size, block, centre):
    down = lax.broadcasted_iota(jnp.int32, (size, size), 0)
    over = lax.broadcasted_iota(jnp.int32, (size, size), 1)
    apart = jnp.abs(down - over)
    band = jnp.where(apart == 0, centre, 0.0)
    for r in range(1, MARGIN + 1):
        band = jnp.where(apart == r, WEIGHTS[r], band)
    if block < size:
        band = jnp.where(down // block == over // block, band, 0.0)
    return band.astype(jnp.bfloat16)


def wave_kernel(
    doms,
    now_hbm,
    adj_hbm,
    prev_hbm,
    later_hbm,
    speed_hbm,
    pulse,
    src_cells,
    src_signs,
    record_cells,
    observed,
    out,
    f0,
    f1,
    f2,
    f3,
    f4,
    a4,
    a3,
    a2,
    a1,
    prev,
    later,
    speed,
    squares,
    laps,
    hf0,
    hf1,
    ha,
    hb,
    across_y,
    mixed,
    blend,
    across_z,
    spread_src,
    pick,
    put,
    hot,
    columns,
    measured,
    found,
    beside,
    values,
    total,
    load_sem,
    send_sem,
    recv_sem,
):
    fields = (f0, f1, f2, f3, f4)
    hf = (hf0, hf1)
    shots, rows, depth, width = prev.shape
    here = lax.axis_index("dom")
    left = jnp.maximum(here - 1, 0)
    right = jnp.minimum(here + 1, doms - 1)
    has_left = here > 0
    has_right = here < doms - 1
    group = MARGIN
    groups = rows // group
    half = 16
    halves = depth // half
    f32 = jnp.float32

    loads = [
        pltpu.make_async_copy(now_hbm, f0.at[:, pl.ds(MARGIN, rows)], load_sem.at[0]),
        pltpu.make_async_copy(speed_hbm, speed.at[pl.ds(REACH, rows)], load_sem.at[1]),
        pltpu.make_async_copy(prev_hbm, prev, load_sem.at[2]),
        pltpu.make_async_copy(adj_hbm, a4.at[:, pl.ds(BORDER, rows)], load_sem.at[3]),
        pltpu.make_async_copy(later_hbm, later, load_sem.at[4]),
    ]
    for load in loads:
        load.start()

    barrier = pltpu.get_barrier_semaphore()

    @pl.when(has_left)
    def _():
        pl.semaphore_signal(barrier, inc=1, device_id={"dom": left}, device_id_type=MESH)

    @pl.when(has_right)
    def _():
        pl.semaphore_signal(barrier, inc=1, device_id={"dom": right}, device_id_type=MESH)

    pl.semaphore_wait(barrier, has_left.astype(jnp.int32) + has_right.astype(jnp.int32))

    pairs = []

    def pair(low_source, high_target, high_source, low_target):
        index = len(pairs)
        to_left = pltpu.make_async_remote_copy(
            src_ref=low_source,
            dst_ref=high_target,
            send_sem=send_sem.at[index, 0],
            recv_sem=recv_sem.at[index, 1],
            device_id={"dom": left},
            device_id_type=MESH,
        )
        to_right = pltpu.make_async_remote_copy(
            src_ref=high_source,
            dst_ref=low_target,
            send_sem=send_sem.at[index, 1],
            recv_sem=recv_sem.at[index, 0],
            device_id={"dom": right},
            device_id_type=MESH,
        )
        pairs.append((to_left, to_right))
        return pairs[-1]

    def send(copies):
        @pl.when(has_left)
        def _():
            copies[0].start()

        @pl.when(has_right)
        def _():
            copies[1].start()

    def receive(copies):
        @pl.when(has_left)
        def _():
            copies[1].wait_recv()

        @pl.when(has_right)
        def _():
            copies[0].wait_recv()

    def sent(copies):
        @pl.when(has_left)
        def _():
            copies[0].wait_send()

        @pl.when(has_right)
        def _():
            copies[1].wait_send()

    halos = []
    for k in range(STEPS):
        halos.append([])
        for s in range(shots):
            field = fields[k]
            source = now_hbm if k == 0 else field
            base = 0 if k == 0 else MARGIN
            halos[k].append(
                pair(
                    source.at[s, pl.ds(base, MARGIN)],
                    field.at[s, pl.ds(MARGIN + rows, MARGIN)],
                    source.at[s, pl.ds(base + rows - MARGIN, MARGIN)],
                    field.at[s, pl.ds(0, MARGIN)],
                )
            )
    adj_halo = pair(
        adj_hbm.at[:, pl.ds(0, REACH)],
        a4.at[:, pl.ds(BORDER + rows, REACH)],
        adj_hbm.at[:, pl.ds(rows - REACH, REACH)],
        a4.at[:, pl.ds(BORDER - REACH, REACH)],
    )
    speed_halo = pair(
        speed_hbm.at[pl.ds(0, REACH)],
        speed.at[pl.ds(REACH + rows, REACH)],
        speed_hbm.at[pl.ds(rows - REACH, REACH)],
        speed.at[pl.ds(0, REACH)],
    )
    border_halo = pair(
        a3.at[:, pl.ds(BORDER, BORDER)],
        a3.at[:, pl.ds(BORDER + rows, BORDER)],
        a3.at[:, pl.ds(rows, BORDER)],
        a3.at[:, pl.ds(0, BORDER)],
    )
    samples = [
        pair(found.at[k], beside.at[k, 1], found.at[k], beside.at[k, 0]) for k in range(STEPS)
    ]

    for s in range(shots):
        send(halos[0][s])
    send(adj_halo)
    send(speed_halo)

    def clear(first_field, first_adj, first_border, first_speed, side):
        for k in range(STEPS):
            for s in range(shots):
                fields[k][s, pl.ds(first_field, MARGIN)] = jnp.zeros((MARGIN, depth, width), f32)
        for s in range(shots):
            a4[s, pl.ds(first_adj, REACH)] = jnp.zeros((REACH, depth, width), f32)
            a3[s, pl.ds(first_border, BORDER)] = jnp.zeros((BORDER, depth, width), f32)
        speed[pl.ds(first_speed, REACH)] = jnp.zeros((REACH, depth, width), f32)
        for k in range(STEPS):
            beside[k, side] = jnp.zeros(beside.shape[2:], f32)

    @pl.when(jnp.logical_not(has_left))
    def _():
        clear(0, BORDER - REACH, 0, 0, 0)

    @pl.when(jnp.logical_not(has_right))
    def _():
        clear(MARGIN + rows, BORDER + rows, BORDER + rows, REACH + rows, 1)

    across_y[...] = jnp.concatenate([banded(width, width, -43008.0)] * 2, axis=0)
    across_z[...] = jnp.concatenate([banded(group * depth, depth, -42.0)] * 2, axis=1)

    receivers = record_cells.shape[1]
    tiles = receivers // 8
    lane = lax.broadcasted_iota(jnp.int32, (8, width), 1)
    first = here * (rows * depth)
    row_of = lambda cell: lax.div(cell, jnp.int32(width))
    lane_of = lambda cell: lax.rem(cell, jnp.int32(width))
    tile = (width, receivers)
    place = lax.broadcasted_iota(jnp.int32, tile, 0)
    span = 8 * depth
    compact = [jnp.zeros((8, width), f32) for _ in range(STEPS)]
    for s in range(shots):
        cells = record_cells[s : s + 1, :]
        rec_rows = row_of(cells) - first
        table = jnp.where(
            place == STEPS,
            jnp.broadcast_to(rec_rows.astype(f32), tile),
            jnp.broadcast_to(lane_of(cells).astype(f32), tile),
        )
        for k in range(STEPS):
            table = jnp.where(place == k, jnp.broadcast_to(observed[s, k : k + 1, :], tile), table)
        columns[s] = jnp.transpose(table)
        rec_col = columns[s, :, STEPS : STEPS + 1].astype(jnp.int32)
        rec_lane = columns[s, :, STEPS + 1 : STEPS + 2].astype(jnp.int32)
        hot[s] = (lax.broadcasted_iota(jnp.int32, (receivers, width), 1) == rec_lane).astype(f32)
        for k in range(STEPS):
            for j in range(tiles):
                column = columns[s, pl.ds(j * 8, 8), k : k + 1]
                compact[k] = jnp.where(lane == s * tiles + j, column, compact[k])
        count = src_cells.shape[1]
        padded = count + (-count) % 128
        order = lax.broadcasted_iota(jnp.int32, (padded, width), 0)
        across = lax.broadcasted_iota(jnp.int32, (padded, width), 1)
        along = lax.broadcasted_iota(jnp.int32, (1, padded), 1)
        tall = jnp.zeros((padded, width), f32)
        src_rows = jnp.full((1, padded), -1, jnp.int32)
        for j in range(count):
            cell = src_cells[s, j]
            sign = (2 * src_signs[s, j] - 1).astype(f32)
            tall = jnp.where((order == j) & (across == lane_of(cell)), sign, tall)
            src_rows = jnp.where(along == j, row_of(cell) - first, src_rows)
        tall = tall.astype(jnp.bfloat16)

        for c in range(rows * depth // span):
            cell = lax.broadcasted_iota(jnp.int32, (receivers, span), 1) + c * span
            pick[s, :, c * span : (c + 1) * span] = (
                (cell == rec_col).astype(f32).astype(jnp.bfloat16)
            )

        @pl.loop(0, rows * depth // span)
        def _(c):
            cell = lax.broadcasted_iota(jnp.int32, (span, padded), 0) + c * span
            wide = (cell == src_rows).astype(f32).astype(jnp.bfloat16)
            spots = jnp.dot(wide, tall, preferred_element_type=f32)
            spread_src[s, pl.ds(c * 8, 8)] = spots.reshape(8, depth, width)

        @pl.loop(0, (rows + 2 * BORDER) // 8)
        def _(c):
            cell = lax.broadcasted_iota(jnp.int32, (span, receivers), 0)
            cell = cell + (c * span - BORDER * depth)
            put[s, pl.ds(pl.multiple_of(c * span, span), span)] = (
                (cell == rec_rows).astype(f32).astype(jnp.bfloat16)
            )

    for k in range(STEPS):
        measured[k] = compact[k]

    def keep_split(ref, s, row, part, value):
        high, low = split_two(value)
        ref[s, row, part, 0:width] = high
        ref[s, row, part, width : 2 * width] = low

    everyone = tuple(range(shots))

    def mix(split, row, mixed):
        lines = [
            split[s, pl.ds(row, group)].reshape(group * depth, 2 * width) for s in everyone
        ]
        highs = jnp.concatenate([line[:, :width] for line in lines], axis=1)
        lows = jnp.concatenate([line[:, width:] for line in lines], axis=1)
        down = jnp.dot(
            across_z[...], jnp.concatenate([highs, lows], axis=0), preferred_element_type=f32
        )
        over = jnp.dot(
            jnp.concatenate(lines, axis=0), across_y[...], preferred_element_type=f32
        )
        for s in everyone:
            both = over[s * group * depth : (s + 1) * group * depth]
            both = both + down[:, s * width : (s + 1) * width]
            mixed[s, pl.ds(row, group)] = both.reshape(group, depth, width)

    def beside_x(window, i):
        summed = WEIGHTS[1] * (window[i + 3] + window[i + 5])
        for r in range(2, MARGIN + 1):
            summed += WEIGHTS[r] * (window[i + MARGIN + r] + window[i + MARGIN - r])
        return summed

    def sweep(first, last, point, ahead):
        ahead(first)

        @pl.loop(first, last, unroll=2)
        def _(g):
            point(g)
            ahead(g + 1)

    def square(first, last):
        @pl.loop(first, last)
        def _(x):
            squares[x] = (COURANT / SCALE) * speed[x] * speed[x]

    parts = [pl.ds(h * half, half) for h in range(halves)]
    def prepare(field, margin, split, split_margin):
        @pl.loop(0, rows)
        def _(x):
            for s in range(shots):
                for part in parts:
                    keep_split(split, s, x + split_margin, part, field[s, x + margin, part])

    def forward_point(k, g, which):
        x = g * group
        field, target, split = fields[k], fields[k + 1], hf[(k + 1) % 2]
        for part in parts:
            for s in which:
                window = [field[s, x + i, part] for i in range(group + 2 * MARGIN)]
                for i in range(group):
                    lap = beside_x(window, i) + mixed[s, x + i, part]
                    laps[k, s, x + i, part] = lap
                    if k == 0:
                        before = prev[s, x + i, part]
                    else:
                        before = fields[k - 1][s, x + i + MARGIN, part]
                    fresh = 2.0 * window[i + MARGIN] - before
                    fresh = fresh + pulse[s, k] * spread_src[s, x + i, part]
                    fresh = fresh + squares[x + i + REACH, part] * lap
                    target[s, x + i + MARGIN, part] = fresh
                    keep_split(split, s, x + i, part, fresh)

    def forward_inside(k):
        ahead = lambda g: mix(hf[k % 2], g * group, mixed)
        ahead(0)
        sweep(1, groups - 1, lambda g: forward_point(k, g, everyone), ahead)

    def sample(k):
        split = hf[(k + 1) % 2]
        gathered = jnp.zeros((8, width), f32)
        for s in range(shots):
            both = jnp.dot(
                pick[s],
                split[s].reshape(rows * depth, 2 * width),
                preferred_element_type=f32,
            )
            chosen = (both[:, :width] + both[:, width:]) * hot[s]
            column = jnp.sum(chosen, axis=1, keepdims=True)
            for j in range(tiles):
                gathered = jnp.where(
                    lane == s * tiles + j, column[j * 8 : (j + 1) * 8], gathered
                )
        found[k] = gathered

    def misfits(k, everywhere):
        missed = found[k] - measured[k]
        if everywhere:
            missed = missed + (beside[k, 0] + beside[k, 1])
        for s in range(shots):
            for j in range(0, tiles, 2):
                block = []
                for t in (j, j + 1):
                    at = s * tiles + t
                    block.append(missed[:, at : at + 1] * hot[s, pl.ds(t * 8, 8)])
                high, low = split_two(jnp.concatenate(block, axis=0))
                values[k, s, pl.ds(j * 8, 16), 0:width] = high
                values[k, s, pl.ds(j * 8, 16), width : 2 * width] = low

    def dropped(k, s, x):
        at = pl.multiple_of((x + BORDER) * depth, group * depth)
        both = jnp.dot(
            put[s, pl.ds(at, group * depth)], values[k, s], preferred_element_type=f32
        )
        return (both[:, :width] + both[:, width:]).reshape(group, depth, width)

    def free_point(g):
        x = g * group
        for part in parts:
            for s in range(shots):
                window = [
                    a4[s, x + BORDER - MARGIN + i, part] for i in range(group + 2 * MARGIN)
                ]
                for i in range(group):
                    lap = beside_x(window, i) + blend[s, x + BORDER + i, part]
                    fresh = 2.0 * window[i + MARGIN] - later[s, x + i, part]
                    a3[s, x + i + BORDER, part] = fresh + squares[x + i + REACH, part] * lap

    def drop_point(g, inside):
        x = g * group
        gathered = None
        for s in range(shots):
            fresh = a3[s, pl.ds(x + BORDER, group)] + dropped(STEPS - 1, s, x)
            a3[s, pl.ds(x + BORDER, group)] = fresh
            high, low = split_two(fresh)
            hb[s, pl.ds(x + BORDER, group), :, 0:width] = high
            hb[s, pl.ds(x + BORDER, group), :, width : 2 * width] = low
            if inside:
                term = fresh * laps[STEPS - 1, s, pl.ds(x, group)]
                gathered = term if gathered is None else gathered + term
        if inside:
            total[pl.ds(x, group)] = gathered

    adj = {4: a4, 3: a3, 2: a2, 1: a1}
    splits = {4: ha, 3: hb, 2: ha, 1: hb}

    def backward_point(m, g, inside):
        x = g * group
        field, after = adj[m], adj[m + 1]
        fallen = [dropped(m - 1, s, x) for s in range(shots)]
        for h, part in enumerate(parts):
            rim = slice(h * half, (h + 1) * half)
            gathered = [None] * group
            for s in range(shots):
                window = [
                    field[s, x + BORDER - MARGIN + i, part] for i in range(group + 2 * MARGIN)
                ]
                for i in range(group):
                    lap = beside_x(window, i) + blend[s, x + BORDER + i, part]
                    fresh = 2.0 * window[i + MARGIN] - after[s, x + i + BORDER, part]
                    fresh = fresh + fallen[s][i, rim]
                    fresh = fresh + squares[x + i + REACH, part] * lap
                    if m > 1:
                        adj[m - 1][s, x + i + BORDER, part] = fresh
                        keep_split(splits[m - 1], s, x + i + BORDER, part, fresh)
                    if inside:
                        term = fresh * laps[m - 1, s, x + i, part]
                        gathered[i] = term if gathered[i] is None else gathered[i] + term
            if inside:
                for i in range(group):
                    summed = total[x + i, part] + gathered[i]
                    if m > 1:
                        total[x + i, part] = summed
                    else:
                        factor = (2.0 * COURANT / SCALE) * speed[x + i + REACH, part]
                        out[x + i, part] = factor * summed

    def backward(m, first, last, inside):
        ahead = lambda g: mix(splits[m], g * group + BORDER, blend)
        sweep(first, last, lambda g: backward_point(m, g, inside), ahead)

    for load in loads[:3]:
        load.wait()
    square(REACH, REACH + rows)
    prepare(f0, MARGIN, hf0, 0)
    forward_inside(0)
    for k in range(STEPS):
        rims = (0, groups - 1)
        for s in everyone:
            receive(halos[k][s])
            for g in rims:
                forward_point(k, g, (s,))
            if k + 1 < STEPS:
                send(halos[k + 1][s])
        if k + 1 < STEPS:
            forward_inside(k + 1)
        sample(k)
        send(samples[k])
        if k == 0:
            for load in loads[3:]:
                load.wait()
            prepare(a4, BORDER, ha, BORDER)
            receive(adj_halo)
            sweep(0, groups, free_point, lambda g: mix(ha, g * group + BORDER, blend))
            send(border_halo)
            receive(speed_halo)
            square(0, REACH)
            square(REACH + rows, 2 * REACH + rows)
        else:
            receive(samples[k - 1])
            misfits(k - 1, True)

    sent(border_halo)
    misfits(STEPS - 1, False)

    @pl.loop(0, groups, unroll=2)
    def _(g):
        drop_point(g, True)

    backward(3, 1, groups - 1, True)
    receive(samples[STEPS - 1])
    misfits(STEPS - 1, True)
    receive(border_halo)
    far = BORDER // group
    for g in range(far):
        drop_point(-1 - g, False)
        drop_point(groups + g, False)
    outer = [g for t in range(far - 1) for g in (-1 - t, groups + t)]
    reached = outer + [0, groups - 1]
    for g in reached[:2]:
        mix(splits[3], g * group + BORDER, blend)
    for n, g in enumerate(reached):
        backward_point(3, g, g not in outer)
        if n + 2 < len(reached):
            mix(splits[3], reached[n + 2] * group + BORDER, blend)
    for g in (-1, groups):
        mix(splits[2], g * group + BORDER, blend)
    for g in (-1, groups):
        backward_point(2, g, False)
    backward(2, 0, groups, True)
    backward(1, 0, groups, True)
    for copies in pairs:
        if copies is not border_halo:
            sent(copies)


def shot_gradient(
    velocity, prev, now, later, adjoint, wavelet, source_cells, signs, record_cells, observed
):
    shots, rows, depth, width = now.shape
    receivers = record_cells.shape[1]
    hbm = pl.BlockSpec(memory_space=pl.ANY)
    vmem = pl.BlockSpec(memory_space=pltpu.VMEM)
    smem = pl.BlockSpec(memory_space=pltpu.SMEM)
    f32, bf16 = jnp.float32, jnp.bfloat16
    group = MARGIN
    wide = rows + 2 * REACH
    widest = rows + 2 * BORDER
    exchanges = STEPS * shots + 3 + STEPS
    return pl.pallas_call(
        functools.partial(wave_kernel, lax.axis_size("dom")),
        out_shape=jax.ShapeDtypeStruct((rows, depth, width), f32),
        in_specs=[hbm] * 5 + [smem] * 3 + [vmem] * 2,
        out_specs=vmem,
        scratch_shapes=[pltpu.VMEM((shots, rows + 2 * MARGIN, depth, width), f32)] * (STEPS + 1)
        + [pltpu.VMEM((shots, widest, depth, width), f32)] * STEPS
        + [
            pltpu.VMEM((shots, rows, depth, width), f32),
            pltpu.VMEM((shots, rows, depth, width), f32),
            pltpu.VMEM((wide, depth, width), f32),
            pltpu.VMEM((wide, depth, width), f32),
            pltpu.VMEM((STEPS, shots, rows, depth, width), f32),
            pltpu.VMEM((shots, rows, depth, 2 * width), bf16),
            pltpu.VMEM((shots, rows, depth, 2 * width), bf16),
            pltpu.VMEM((shots, widest, depth, 2 * width), bf16),
            pltpu.VMEM((shots, widest, depth, 2 * width), bf16),
            pltpu.VMEM((2 * width, width), bf16),
            pltpu.VMEM((shots, rows, depth, width), f32),
            pltpu.VMEM((shots, widest, depth, width), f32),
            pltpu.VMEM((group * depth, 2 * group * depth), bf16),
            pltpu.VMEM((shots, rows, depth, width), f32),
            pltpu.VMEM((shots, receivers, rows * depth), bf16),
            pltpu.VMEM((shots, widest * depth, receivers), bf16),
            pltpu.VMEM((shots, receivers, width), f32),
            pltpu.VMEM((shots, receivers, width), f32),
            pltpu.VMEM((STEPS, 8, width), f32),
            pltpu.VMEM((STEPS, 8, width), f32),
            pltpu.VMEM((STEPS, 2, 8, width), f32),
            pltpu.VMEM((STEPS, shots, receivers, 2 * width), bf16),
            pltpu.VMEM((rows, depth, width), f32),
            pltpu.SemaphoreType.DMA((5,)),
            pltpu.SemaphoreType.DMA((exchanges, 2)),
            pltpu.SemaphoreType.DMA((exchanges, 2)),
        ],
        compiler_params=pltpu.CompilerParams(
            collective_id=0, has_side_effects=True, vmem_limit_bytes=56 * 1024 * 1024
        ),
    )(
        now,
        adjoint,
        prev,
        later,
        velocity,
        wavelet,
        source_cells,
        signs,
        record_cells,
        observed,
    )


def cosine_basis(length):
    wave_index = jnp.arange(length, dtype=jnp.int32)[:, None]
    position = jnp.arange(length, dtype=jnp.int32)[None, :]
    phase = wave_index * (2 * position + 1) % (4 * length)
    angle = math.pi / (2.0 * length) * phase.astype(jnp.float32)
    factor = jnp.where(wave_index == 0, math.sqrt(1.0 / length), math.sqrt(2.0 / length)).astype(
        jnp.float32
    )
    return factor * jnp.cos(angle)


def prior_gain(length, cutoff):
    scaled = jnp.arange(length, dtype=jnp.float32) / float(cutoff)
    return 1.0 / jnp.sqrt(1.0 + scaled)


def precondition(gradient, noise_cols, rate):
    length = gradient.shape[0]
    basis = cosine_basis(length)
    spectrum = prior_gain(length, length // 32)[:, None]
    highest = lax.Precision.HIGHEST
    grad_hat = jnp.dot(basis, gradient.reshape(length, -1), precision=highest)
    noise_hat = jnp.dot(basis, noise_cols.reshape(length, -1), precision=highest)
    weights = spectrum * (-0.5 * rate * spectrum * grad_hat + jnp.sqrt(rate) * noise_hat)
    update = lax.dot_general(basis, weights, (((0,), (0,)), ((), ())), precision=highest)
    return update.reshape(gradient.shape)


def shared_kernel(
    shots,
    doms,
    partial,
    noise,
    basis,
    basis_t,
    gain,
    step_size,
    out,
    folded,
    noise_fold,
    sums,
    own,
    noise_lines,
    grad_lines,
    update,
    returned,
    send_sem,
    recv_sem,
    shot_send,
    shot_recv,
):
    depth, rows, width = shots * folded.shape[1], folded.shape[2], folded.shape[3]
    fold = folded.shape[1]
    lot = fold // doms
    lane_share = width // shots
    me = lax.axis_index("shot")
    here = lax.axis_index("dom")
    dom_peer = [lax.rem(here + o, doms) for o in range(doms)]
    shot_peer = [lax.rem(me + o, shots) for o in range(shots)]

    barrier = pltpu.get_barrier_semaphore()
    for o in range(1, doms):
        pl.semaphore_signal(barrier, inc=1, device_id={"dom": dom_peer[o]}, device_id_type=MESH)
    for o in range(1, shots):
        pl.semaphore_signal(barrier, inc=1, device_id={"shot": shot_peer[o]}, device_id_type=MESH)

    group = lax.broadcasted_iota(jnp.int32, (rows, width), 1) // lane_share

    def fold_lanes(source, target):
        @pl.loop(0, fold)
        def _(level):
            slabs = [
                source[pl.ds(block * fold + level, rows, stride=depth), :]
                for block in range(shots)
            ]
            for share in range(shots):
                merged = None
                for block in range(shots):
                    shift = (block - share) * lane_share % width
                    turned = pltpu.roll(slabs[block], shift, 1) if shift else slabs[block]
                    merged = turned if merged is None else jnp.where(group == block, turned, merged)
                target[share, level] = merged

    def exchange(phase, source_of, target):
        moves = []
        for o in range(1, doms):
            moves.append(
                pltpu.make_async_remote_copy(
                    src_ref=source_of(dom_peer[o]),
                    dst_ref=target.at[here],
                    send_sem=send_sem.at[phase, o],
                    recv_sem=recv_sem.at[phase, o],
                    device_id={"dom": dom_peer[o]},
                    device_id_type=MESH,
                )
            )
        return moves

    fold_lanes(partial, folded)
    pl.semaphore_wait(barrier, doms + shots - 2)
    sharing = []
    for o in range(1, shots):
        move = pltpu.make_async_remote_copy(
            src_ref=folded.at[shot_peer[o]],
            dst_ref=sums.at[o],
            send_sem=shot_send.at[o],
            recv_sem=shot_recv.at[o],
            device_id={"shot": shot_peer[o]},
            device_id_type=MESH,
        )
        move.start()
        sharing.append(move)
    fold_lanes(noise, noise_fold)
    noise_moves = exchange(0, lambda d: noise_fold.at[me, pl.ds(d * lot, lot)], noise_lines)
    for move in noise_moves:
        move.start()
    noise_lines[here] = noise_fold[me, pl.ds(here * lot, lot)]
    for move in noise_moves:
        move.wait_recv()
    rate = step_size[0]
    highest = lax.Precision.HIGHEST
    lines = doms * rows
    noise_hats = [
        jnp.dot(
            basis[...],
            noise_lines[:, i].reshape(lines, width),
            precision=highest,
            preferred_element_type=jnp.float32,
        )
        for i in range(lot)
    ]
    root = jnp.sqrt(jnp.full((1, 1), rate, jnp.float32))
    for move in sharing:
        move.wait_recv()
    gathered = folded[me]
    for o in range(1, shots):
        gathered = gathered + sums[o]
    own[...] = gathered
    grad_moves = exchange(1, lambda d: own.at[pl.ds(d * lot, lot)], grad_lines)
    for move in grad_moves:
        move.start()
    grad_lines[here] = own[pl.ds(here * lot, lot)]
    for move in grad_moves:
        move.wait_recv()
    for i in range(lot):
        grad_hat = jnp.dot(
            basis[...],
            grad_lines[:, i].reshape(lines, width),
            precision=highest,
            preferred_element_type=jnp.float32,
        )
        weights = gain[...] * (-0.5 * rate * gain[...] * grad_hat + root * noise_hats[i])
        update[:, i] = jnp.dot(
            basis_t[...], weights, precision=highest, preferred_element_type=jnp.float32
        ).reshape(doms, rows, width)
    back_moves = exchange(2, lambda d: update.at[d], returned)
    for move in back_moves:
        move.start()
    returned[here] = update[here]
    for move in back_moves:
        move.wait_recv()
    for d in range(doms):
        for i in range(lot):
            line = returned[d, i]
            for block in range(shots):
                shift = -block * lane_share % width
                turned = pltpu.roll(line, shift, 1) if shift else line
                out[pl.ds(block * fold + d * lot + i, rows, stride=depth), :] = turned
    for move in sharing + noise_moves + grad_moves + back_moves:
        move.wait_send()


def shared_update(partial_value, noise_field, step_size):
    rows, depth, width = partial_value.shape
    shots, doms = lax.axis_size("shot"), lax.axis_size("dom")
    length = rows * doms
    fold = depth // shots
    lot = fold // doms
    wave = np.arange(length)[:, None]
    phase = wave * (2 * np.arange(length)[None, :] + 1) % (4 * length)
    factor = np.where(wave == 0, math.sqrt(1.0 / length), math.sqrt(2.0 / length))
    basis = (factor * np.cos(math.pi / (2.0 * length) * phase)).astype(np.float32)
    gain = (1.0 / np.sqrt(1.0 + wave / (length // 32))).astype(np.float32)
    f32 = jnp.float32
    vmem = pl.BlockSpec(memory_space=pltpu.VMEM)
    smem = pl.BlockSpec(memory_space=pltpu.SMEM)
    result = pl.pallas_call(
        functools.partial(shared_kernel, shots, doms),
        out_shape=jax.ShapeDtypeStruct((rows * depth, width), f32),
        in_specs=[vmem] * 5 + [smem],
        out_specs=vmem,
        scratch_shapes=[
            pltpu.VMEM((shots, fold, rows, width), f32),
            pltpu.VMEM((shots, fold, rows, width), f32),
            pltpu.VMEM((shots, fold, rows, width), f32),
            pltpu.VMEM((fold, rows, width), f32),
            pltpu.VMEM((doms, lot, rows, width), f32),
            pltpu.VMEM((doms, lot, rows, width), f32),
            pltpu.VMEM((doms, lot, rows, width), f32),
            pltpu.VMEM((doms, lot, rows, width), f32),
            pltpu.SemaphoreType.DMA((3, doms)),
            pltpu.SemaphoreType.DMA((3, doms)),
            pltpu.SemaphoreType.DMA((shots,)),
            pltpu.SemaphoreType.DMA((shots,)),
        ],
        compiler_params=pltpu.CompilerParams(
            collective_id=1, has_side_effects=True, vmem_limit_bytes=32 * 1024 * 1024
        ),
    )(
        partial_value.reshape(rows * depth, width),
        noise_field.reshape(rows * depth, width),
        jnp.asarray(basis),
        jnp.asarray(np.ascontiguousarray(basis.T)),
        jnp.asarray(gain),
        step_size,
    )
    return result.reshape(rows, depth, width)[:, :, : width // shots]


def body(
    velocity,
    noise_field,
    step_size,
    field_prev,
    field_now,
    adjoint_next,
    adjoint_now,
    wavelet,
    source_cells,
    source_signs,
    record_cells,
    observed,
):
    partial_value = shot_gradient(
        velocity,
        field_prev,
        field_now,
        adjoint_next,
        adjoint_now,
        wavelet,
        source_cells,
        source_signs,
        record_cells,
        observed,
    )
    rate = step_size[0]
    shot_rows = velocity.shape[2] // lax.axis_size("shot")
    start = lax.axis_index("shot") * shot_rows
    if velocity.shape[1] % (lax.axis_size("shot") * lax.axis_size("dom")) == 0:
        moved = shared_update(partial_value, noise_field, step_size)
        return lax.dynamic_slice_in_dim(velocity, start, shot_rows, 2) + moved
    share = lax.psum_scatter(partial_value, "shot", scatter_dimension=2, tiled=True)
    noise_part = lax.dynamic_slice_in_dim(noise_field, start, shot_rows, 2)
    grad_cols, noise_cols = (
        lax.all_to_all(share, "dom", split_axis=2, concat_axis=0, tiled=True),
        lax.all_to_all(noise_part, "dom", split_axis=2, concat_axis=0, tiled=True),
    )
    update = precondition(grad_cols, noise_cols, rate)
    returned = lax.all_to_all(update, "dom", split_axis=0, concat_axis=2, tiled=True)
    result = lax.dynamic_slice_in_dim(velocity, start, shot_rows, 2) + returned
    return result


def solution(mesh):
    placed = (
        P("dom", None, None),
        P("dom", None, None),
        P(),
        P("shot", "dom", None, None),
        P("shot", "dom", None, None),
        P("shot", "dom", None, None),
        P("shot", "dom", None, None),
        P("shot", None),
        P("shot", None),
        P("shot", None),
        P("shot", None),
        P("shot", None, None),
    )
    return jax.shard_map(
        body, mesh=mesh, in_specs=placed, out_specs=P("dom", None, "shot"), check_vma=False
    )
```

```python
import functools
import math

import jax
import jax.numpy as jnp
import numpy as np
from jax import lax
from jax.experimental import pallas as pl
from jax.experimental.pallas import tpu as pltpu
from jax.sharding import PartitionSpec as P

STEPS = 4


COEFFS = (-205.0 / 72.0, 8.0 / 5.0, -1.0 / 5.0, 8.0 / 315.0, -1.0 / 560.0)
COURANT = 0.02


MARGIN = 4
MESH = pl.DeviceIdType.MESH


REACH = 2 * MARGIN
BORDER = 3 * MARGIN
WEIGHTS = (-43050.0, 8064.0, -1008.0, 128.0, -9.0)
SCALE = 5040.0


def split_two(value):
    high = value.astype(jnp.bfloat16)
    low = (value - high.astype(jnp.float32)).astype(jnp.bfloat16)
    return high, low


def banded(size, block, centre):
    down = lax.broadcasted_iota(jnp.int32, (size, size), 0)
    over = lax.broadcasted_iota(jnp.int32, (size, size), 1)
    apart = jnp.abs(down - over)
    band = jnp.where(apart == 0, centre, 0.0)
    for r in range(1, MARGIN + 1):
        band = jnp.where(apart == r, WEIGHTS[r], band)
    if block < size:
        band = jnp.where(down // block == over // block, band, 0.0)
    return band.astype(jnp.bfloat16)


WAVE_REFS = 36


class Prior:
    def __init__(
        self,
        doms,
        shares,
        noise_hbm,
        grad_map_hbm,
        noise_map_hbm,
        step_size,
        out,
        noise,
        grad_map,
        noise_map,
        folded,
        sums,
        own,
        noise_fold,
        noise_lines,
        grad_lines,
        base,
        update,
        returned,
        load_sem,
        send_sem,
        recv_sem,
        shot_send,
        shot_recv,
    ):
        self.doms, self.shares = doms, shares
        self.noise, self.out, self.step_size = noise, out, step_size
        self.grad_map, self.noise_map = grad_map, noise_map
        self.folded, self.sums, self.own = folded, sums, own
        self.noise_fold, self.noise_lines, self.grad_lines = noise_fold, noise_lines, grad_lines
        self.base, self.update, self.returned = base, update, returned
        self.me = lax.axis_index("shot")
        self.here = lax.axis_index("dom")
        self.depth = doms * shares
        self.fold, self.rows, self.width = folded.shape[1:]
        self.piece = self.width // shares
        self.group = lax.broadcasted_iota(jnp.int32, (self.rows, self.width), 1) // self.piece
        self.half = doms // 2
        self.near = (self.here // self.half) * self.half
        self.far = self.half - self.near
        self.loads = [
            pltpu.make_async_copy(noise_hbm, noise, load_sem.at[0]),
            pltpu.make_async_copy(noise_map_hbm, noise_map, load_sem.at[1]),
            pltpu.make_async_copy(grad_map_hbm, grad_map, load_sem.at[2]),
        ]
        turn = [lax.rem(self.here + o, self.half) for o in range(self.half)]
        self.away = [self.far + t for t in turn]
        self.close = [self.near + t for t in turn]
        self.sems = (send_sem, recv_sem)
        self.shot_sems = (shot_send, shot_recv)
        self.moves = []

    def load(self):
        for load in self.loads:
            load.start()

    def slabs(self, source, level):
        return [
            source[pl.ds(block * self.fold + level, self.rows, stride=self.depth), :]
            for block in range(self.shares)
        ]

    def join(self, slabs, share):
        merged = None
        for block in range(self.shares):
            shift = (block - share) * self.piece
            if isinstance(share, int):
                shift = shift % self.width
                turned = pltpu.roll(slabs[block], shift, 1) if shift else slabs[block]
            else:
                shift = lax.rem(shift + self.width, self.width)
                turned = pltpu.roll(slabs[block], shift, 1)
            merged = turned if merged is None else jnp.where(self.group == block, turned, merged)
        return merged

    def exchange(self, phase, source_of, target, far):
        peers = self.away if far else self.close
        for o in range(0 if far else 1, self.half):
            index = o + (self.half if far else 0)
            move = pltpu.make_async_remote_copy(
                src_ref=source_of(peers[o]),
                dst_ref=target.at[self.here],
                send_sem=self.sems[0].at[phase, index],
                recv_sem=self.sems[1].at[phase, index],
                device_id={"dom": peers[o]},
                device_id_type=MESH,
            )
            move.start()
            self.moves.append((phase, move))

    def arrive(self, phase):
        for which, move in self.moves:
            if which == phase:
                move.wait_recv()

    def send_noise(self):
        for load in self.loads:
            load.wait()

        @pl.loop(0, self.fold)
        def _(level):
            self.noise_fold[level] = self.join(self.slabs(self.noise, level), self.me)

        for far in (True, False):
            self.exchange(0, lambda d: self.noise_fold.at[d], self.noise_lines, far)
        self.noise_lines[self.here] = self.noise_fold[self.here]

    def mapped(self, matrix, lines):
        high, low = split_two(lines[...].reshape(self.doms * self.rows, self.width))
        return jnp.dot(
            matrix[...],
            jnp.concatenate([high, low, high], axis=0),
            preferred_element_type=jnp.float32,
        )

    def noise_update(self):
        self.arrive(0)
        root = jnp.sqrt(jnp.full((1, 1), self.step_size[0], jnp.float32))
        self.base[...] = root * self.mapped(self.noise_map, self.noise_lines)

    def apply(self, partial):
        sharing = []
        for far in (True, False):
            start = self.far if far else self.near

            @pl.loop(0, self.half)
            def _(i):
                slabs = self.slabs(partial, start + i)
                for share in range(self.shares):
                    self.folded[share, start + i] = self.join(slabs, share)

            sharing.append([])
            for o in range(1, self.shares):
                peer = lax.rem(self.me + o, self.shares)
                index = o + (self.shares if far else 0)
                move = pltpu.make_async_remote_copy(
                    src_ref=self.folded.at[peer, pl.ds(start, self.half)],
                    dst_ref=self.sums.at[o, pl.ds(start, self.half)],
                    send_sem=self.shot_sems[0].at[index],
                    recv_sem=self.shot_sems[1].at[index],
                    device_id={"shot": peer},
                    device_id_type=MESH,
                )
                move.start()
                sharing[-1].append(move)
        for far in (True, False):
            start = self.far if far else self.near
            for move in sharing[0 if far else 1]:
                move.wait_recv()
            span = pl.ds(start, self.half)
            gathered = self.folded[self.me, span]
            for o in range(1, self.shares):
                gathered = gathered + self.sums[o, span]
            self.own[span] = gathered
            self.exchange(1, lambda d: self.own.at[d], self.grad_lines, far)
        self.grad_lines[self.here] = self.own[self.here]
        self.arrive(1)
        pull = self.mapped(self.grad_map, self.grad_lines)
        fresh = self.base[...] - (0.5 * self.step_size[0]) * pull
        self.update[...] = fresh.reshape(self.doms, self.rows, self.width)
        for far in (True, False):
            self.exchange(2, lambda d: self.update.at[d], self.returned, far)
        self.returned[self.here] = self.update[self.here]
        self.arrive(2)
        for d in range(self.doms):
            line = self.returned[d]
            for block in range(self.shares):
                shift = -block * self.piece % self.width
                turned = pltpu.roll(line, shift, 1) if shift else line
                self.out[pl.ds(block * self.fold + d, self.rows, stride=self.depth), :] = turned
        for moves in sharing:
            for move in moves:
                move.wait_send()
        for _, move in self.moves:
            move.wait_send()


def wave_kernel(doms, shares, *refs):
    inputs = 14 if shares else 10
    arrays, out, scratch = refs[:inputs], refs[inputs], refs[inputs + 1 :]
    wave = arrays[:10] + (scratch[0] if shares else out,) + scratch[1:WAVE_REFS]
    rest = arrays[10:] + (out,) + scratch[WAVE_REFS:] if shares else ()
    gradient_steps(doms, shares, rest, *wave)


def gradient_steps(
    doms,
    shares,
    rest,
    now_hbm,
    adj_hbm,
    prev_hbm,
    later_hbm,
    speed_hbm,
    pulse,
    src_cells,
    src_signs,
    record_cells,
    observed,
    out,
    f0,
    f1,
    f2,
    f3,
    f4,
    a4,
    a3,
    a2,
    a1,
    prev,
    later,
    speed,
    squares,
    laps,
    hf0,
    hf1,
    ha,
    hb,
    across_y,
    mixed,
    blend,
    across_z,
    spread_src,
    pick,
    put,
    hot,
    columns,
    measured,
    found,
    beside,
    values,
    total,
    load_sem,
    send_sem,
    recv_sem,
):
    fields = (f0, f1, f2, f3, f4)
    hf = (hf0, hf1)
    shots, rows, depth, width = prev.shape
    here = lax.axis_index("dom")
    left = jnp.maximum(here - 1, 0)
    right = jnp.minimum(here + 1, doms - 1)
    has_left = here > 0
    has_right = here < doms - 1
    group = MARGIN
    groups = rows // group
    half = 16
    halves = depth // half
    f32 = jnp.float32

    loads = [
        pltpu.make_async_copy(now_hbm, f0.at[:, pl.ds(MARGIN, rows)], load_sem.at[0]),
        pltpu.make_async_copy(speed_hbm, speed.at[pl.ds(REACH, rows)], load_sem.at[1]),
        pltpu.make_async_copy(prev_hbm, prev, load_sem.at[2]),
        pltpu.make_async_copy(adj_hbm, a4.at[:, pl.ds(BORDER, rows)], load_sem.at[3]),
        pltpu.make_async_copy(later_hbm, later, load_sem.at[4]),
    ]
    for load in loads:
        load.start()

    barrier = pltpu.get_barrier_semaphore()
    if shares:
        prior = Prior(doms, shares, *rest)
        prior.load()
        for o in range(1, doms):
            peer = {"dom": lax.rem(here + o, doms)}
            pl.semaphore_signal(barrier, inc=1, device_id=peer, device_id_type=MESH)
        for o in range(1, shares):
            peer = {"shot": lax.rem(lax.axis_index("shot") + o, shares)}
            pl.semaphore_signal(barrier, inc=1, device_id=peer, device_id_type=MESH)
        pl.semaphore_wait(barrier, doms + shares - 2)
    else:

        @pl.when(has_left)
        def _():
            pl.semaphore_signal(barrier, inc=1, device_id={"dom": left}, device_id_type=MESH)

        @pl.when(has_right)
        def _():
            pl.semaphore_signal(barrier, inc=1, device_id={"dom": right}, device_id_type=MESH)

        pl.semaphore_wait(barrier, has_left.astype(jnp.int32) + has_right.astype(jnp.int32))

    pairs = []

    def pair(low_source, high_target, high_source, low_target):
        index = len(pairs)
        to_left = pltpu.make_async_remote_copy(
            src_ref=low_source,
            dst_ref=high_target,
            send_sem=send_sem.at[index, 0],
            recv_sem=recv_sem.at[index, 1],
            device_id={"dom": left},
            device_id_type=MESH,
        )
        to_right = pltpu.make_async_remote_copy(
            src_ref=high_source,
            dst_ref=low_target,
            send_sem=send_sem.at[index, 1],
            recv_sem=recv_sem.at[index, 0],
            device_id={"dom": right},
            device_id_type=MESH,
        )
        pairs.append((to_left, to_right))
        return pairs[-1]

    def send(copies):
        @pl.when(has_left)
        def _():
            copies[0].start()

        @pl.when(has_right)
        def _():
            copies[1].start()

    def receive(copies):
        @pl.when(has_left)
        def _():
            copies[1].wait_recv()

        @pl.when(has_right)
        def _():
            copies[0].wait_recv()

    def sent(copies):
        @pl.when(has_left)
        def _():
            copies[0].wait_send()

        @pl.when(has_right)
        def _():
            copies[1].wait_send()

    halos = []
    for k in range(STEPS):
        halos.append([])
        for s in range(shots):
            field = fields[k]
            source = now_hbm if k == 0 else field
            base = 0 if k == 0 else MARGIN
            halos[k].append(
                pair(
                    source.at[s, pl.ds(base, MARGIN)],
                    field.at[s, pl.ds(MARGIN + rows, MARGIN)],
                    source.at[s, pl.ds(base + rows - MARGIN, MARGIN)],
                    field.at[s, pl.ds(0, MARGIN)],
                )
            )
    adj_halo = pair(
        adj_hbm.at[:, pl.ds(0, REACH)],
        a4.at[:, pl.ds(BORDER + rows, REACH)],
        adj_hbm.at[:, pl.ds(rows - REACH, REACH)],
        a4.at[:, pl.ds(BORDER - REACH, REACH)],
    )
    speed_halo = pair(
        speed_hbm.at[pl.ds(0, REACH)],
        speed.at[pl.ds(REACH + rows, REACH)],
        speed_hbm.at[pl.ds(rows - REACH, REACH)],
        speed.at[pl.ds(0, REACH)],
    )
    border_halo = pair(
        a3.at[:, pl.ds(BORDER, BORDER)],
        a3.at[:, pl.ds(BORDER + rows, BORDER)],
        a3.at[:, pl.ds(rows, BORDER)],
        a3.at[:, pl.ds(0, BORDER)],
    )
    samples = [
        pair(found.at[k], beside.at[k, 1], found.at[k], beside.at[k, 0]) for k in range(STEPS)
    ]

    for s in range(shots):
        send(halos[0][s])
    send(adj_halo)
    send(speed_halo)

    def clear(first_field, first_adj, first_border, first_speed, side):
        for k in range(STEPS):
            for s in range(shots):
                fields[k][s, pl.ds(first_field, MARGIN)] = jnp.zeros((MARGIN, depth, width), f32)
        for s in range(shots):
            a4[s, pl.ds(first_adj, REACH)] = jnp.zeros((REACH, depth, width), f32)
            a3[s, pl.ds(first_border, BORDER)] = jnp.zeros((BORDER, depth, width), f32)
        speed[pl.ds(first_speed, REACH)] = jnp.zeros((REACH, depth, width), f32)
        for k in range(STEPS):
            beside[k, side] = jnp.zeros(beside.shape[2:], f32)

    @pl.when(jnp.logical_not(has_left))
    def _():
        clear(0, BORDER - REACH, 0, 0, 0)

    @pl.when(jnp.logical_not(has_right))
    def _():
        clear(MARGIN + rows, BORDER + rows, BORDER + rows, REACH + rows, 1)

    across_y[...] = jnp.concatenate([banded(width, width, -43008.0)] * 2, axis=0)
    across_z[...] = jnp.concatenate([banded(group * depth, depth, -42.0)] * 2, axis=1)

    receivers = record_cells.shape[1]
    tiles = receivers // 8
    lane = lax.broadcasted_iota(jnp.int32, (8, width), 1)
    first = here * (rows * depth)
    row_of = lambda cell: lax.div(cell, jnp.int32(width))
    lane_of = lambda cell: lax.rem(cell, jnp.int32(width))
    tile = (width, receivers)
    place = lax.broadcasted_iota(jnp.int32, tile, 0)
    span = 8 * depth
    compact = [jnp.zeros((8, width), f32) for _ in range(STEPS)]
    for s in range(shots):
        cells = record_cells[s : s + 1, :]
        rec_rows = row_of(cells) - first
        table = jnp.where(
            place == STEPS,
            jnp.broadcast_to(rec_rows.astype(f32), tile),
            jnp.broadcast_to(lane_of(cells).astype(f32), tile),
        )
        for k in range(STEPS):
            table = jnp.where(place == k, jnp.broadcast_to(observed[s, k : k + 1, :], tile), table)
        columns[s] = jnp.transpose(table)
        rec_col = columns[s, :, STEPS : STEPS + 1].astype(jnp.int32)
        rec_lane = columns[s, :, STEPS + 1 : STEPS + 2].astype(jnp.int32)
        hot[s] = (lax.broadcasted_iota(jnp.int32, (receivers, width), 1) == rec_lane).astype(f32)
        for k in range(STEPS):
            for j in range(tiles):
                column = columns[s, pl.ds(j * 8, 8), k : k + 1]
                compact[k] = jnp.where(lane == s * tiles + j, column, compact[k])
        count = src_cells.shape[1]
        padded = count + (-count) % 128
        order = lax.broadcasted_iota(jnp.int32, (padded, width), 0)
        across = lax.broadcasted_iota(jnp.int32, (padded, width), 1)
        along = lax.broadcasted_iota(jnp.int32, (1, padded), 1)
        tall = jnp.zeros((padded, width), f32)
        src_rows = jnp.full((1, padded), -1, jnp.int32)
        for j in range(count):
            cell = src_cells[s, j]
            sign = (2 * src_signs[s, j] - 1).astype(f32)
            tall = jnp.where((order == j) & (across == lane_of(cell)), sign, tall)
            src_rows = jnp.where(along == j, row_of(cell) - first, src_rows)
        tall = tall.astype(jnp.bfloat16)

        for c in range(rows * depth // span):
            cell = lax.broadcasted_iota(jnp.int32, (receivers, span), 1) + c * span
            pick[s, :, c * span : (c + 1) * span] = (
                (cell == rec_col).astype(f32).astype(jnp.bfloat16)
            )

        @pl.loop(0, rows * depth // span)
        def _(c):
            cell = lax.broadcasted_iota(jnp.int32, (span, padded), 0) + c * span
            wide = (cell == src_rows).astype(f32).astype(jnp.bfloat16)
            spots = jnp.dot(wide, tall, preferred_element_type=f32)
            spread_src[s, pl.ds(c * 8, 8)] = spots.reshape(8, depth, width)

        @pl.loop(0, (rows + 2 * BORDER) // 8)
        def _(c):
            cell = lax.broadcasted_iota(jnp.int32, (span, receivers), 0)
            cell = cell + (c * span - BORDER * depth)
            put[s, pl.ds(pl.multiple_of(c * span, span), span)] = (
                (cell == rec_rows).astype(f32).astype(jnp.bfloat16)
            )

    for k in range(STEPS):
        measured[k] = compact[k]

    def keep_split(ref, s, row, part, value):
        high, low = split_two(value)
        ref[s, row, part, 0:width] = high
        ref[s, row, part, width : 2 * width] = low

    everyone = tuple(range(shots))

    def mix(split, row, mixed):
        lines = [
            split[s, pl.ds(row, group)].reshape(group * depth, 2 * width) for s in everyone
        ]
        highs = jnp.concatenate([line[:, :width] for line in lines], axis=1)
        lows = jnp.concatenate([line[:, width:] for line in lines], axis=1)
        down = jnp.dot(
            across_z[...], jnp.concatenate([highs, lows], axis=0), preferred_element_type=f32
        )
        over = jnp.dot(
            jnp.concatenate(lines, axis=0), across_y[...], preferred_element_type=f32
        )
        for s in everyone:
            both = over[s * group * depth : (s + 1) * group * depth]
            both = both + down[:, s * width : (s + 1) * width]
            mixed[s, pl.ds(row, group)] = both.reshape(group, depth, width)

    def beside_x(window, i):
        summed = WEIGHTS[1] * (window[i + 3] + window[i + 5])
        for r in range(2, MARGIN + 1):
            summed += WEIGHTS[r] * (window[i + MARGIN + r] + window[i + MARGIN - r])
        return summed

    def sweep(first, last, point, ahead):
        ahead(first)

        @pl.loop(first, last, unroll=2)
        def _(g):
            point(g)
            ahead(g + 1)

    def square(first, last):
        @pl.loop(first, last)
        def _(x):
            squares[x] = (COURANT / SCALE) * speed[x] * speed[x]

    parts = [pl.ds(h * half, half) for h in range(halves)]
    def prepare(field, margin, split, split_margin):
        @pl.loop(0, rows)
        def _(x):
            for s in range(shots):
                for part in parts:
                    keep_split(split, s, x + split_margin, part, field[s, x + margin, part])

    def forward_point(k, g, which):
        x = g * group
        field, target, split = fields[k], fields[k + 1], hf[(k + 1) % 2]
        for part in parts:
            for s in which:
                window = [field[s, x + i, part] for i in range(group + 2 * MARGIN)]
                for i in range(group):
                    lap = beside_x(window, i) + mixed[s, x + i, part]
                    laps[k, s, x + i, part] = lap
                    if k == 0:
                        before = prev[s, x + i, part]
                    else:
                        before = fields[k - 1][s, x + i + MARGIN, part]
                    fresh = 2.0 * window[i + MARGIN] - before
                    fresh = fresh + pulse[s, k] * spread_src[s, x + i, part]
                    fresh = fresh + squares[x + i + REACH, part] * lap
                    target[s, x + i + MARGIN, part] = fresh
                    keep_split(split, s, x + i, part, fresh)

    def forward_inside(k):
        ahead = lambda g: mix(hf[k % 2], g * group, mixed)
        ahead(0)
        sweep(1, groups - 1, lambda g: forward_point(k, g, everyone), ahead)

    def sample(k):
        split = hf[(k + 1) % 2]
        gathered = jnp.zeros((8, width), f32)
        for s in range(shots):
            both = jnp.dot(
                pick[s],
                split[s].reshape(rows * depth, 2 * width),
                preferred_element_type=f32,
            )
            chosen = (both[:, :width] + both[:, width:]) * hot[s]
            column = jnp.sum(chosen, axis=1, keepdims=True)
            for j in range(tiles):
                gathered = jnp.where(
                    lane == s * tiles + j, column[j * 8 : (j + 1) * 8], gathered
                )
        found[k] = gathered

    def misfits(k, everywhere):
        missed = found[k] - measured[k]
        if everywhere:
            missed = missed + (beside[k, 0] + beside[k, 1])
        for s in range(shots):
            for j in range(0, tiles, 2):
                block = []
                for t in (j, j + 1):
                    at = s * tiles + t
                    block.append(missed[:, at : at + 1] * hot[s, pl.ds(t * 8, 8)])
                high, low = split_two(jnp.concatenate(block, axis=0))
                values[k, s, pl.ds(j * 8, 16), 0:width] = high
                values[k, s, pl.ds(j * 8, 16), width : 2 * width] = low

    def dropped(k, s, x):
        at = pl.multiple_of((x + BORDER) * depth, group * depth)
        both = jnp.dot(
            put[s, pl.ds(at, group * depth)], values[k, s], preferred_element_type=f32
        )
        return (both[:, :width] + both[:, width:]).reshape(group, depth, width)

    def free_point(g):
        x = g * group
        for part in parts:
            for s in range(shots):
                window = [
                    a4[s, x + BORDER - MARGIN + i, part] for i in range(group + 2 * MARGIN)
                ]
                for i in range(group):
                    lap = beside_x(window, i) + blend[s, x + BORDER + i, part]
                    fresh = 2.0 * window[i + MARGIN] - later[s, x + i, part]
                    a3[s, x + i + BORDER, part] = fresh + squares[x + i + REACH, part] * lap

    def drop_point(g, inside):
        x = g * group
        gathered = None
        for s in range(shots):
            fresh = a3[s, pl.ds(x + BORDER, group)] + dropped(STEPS - 1, s, x)
            a3[s, pl.ds(x + BORDER, group)] = fresh
            high, low = split_two(fresh)
            hb[s, pl.ds(x + BORDER, group), :, 0:width] = high
            hb[s, pl.ds(x + BORDER, group), :, width : 2 * width] = low
            if inside:
                term = fresh * laps[STEPS - 1, s, pl.ds(x, group)]
                gathered = term if gathered is None else gathered + term
        if inside:
            total[pl.ds(x, group)] = gathered

    adj = {4: a4, 3: a3, 2: a2, 1: a1}
    splits = {4: ha, 3: hb, 2: ha, 1: hb}

    def backward_point(m, g, inside):
        x = g * group
        field, after = adj[m], adj[m + 1]
        fallen = [dropped(m - 1, s, x) for s in range(shots)]
        for h, part in enumerate(parts):
            rim = slice(h * half, (h + 1) * half)
            gathered = [None] * group
            for s in range(shots):
                window = [
                    field[s, x + BORDER - MARGIN + i, part] for i in range(group + 2 * MARGIN)
                ]
                for i in range(group):
                    lap = beside_x(window, i) + blend[s, x + BORDER + i, part]
                    fresh = 2.0 * window[i + MARGIN] - after[s, x + i + BORDER, part]
                    fresh = fresh + fallen[s][i, rim]
                    fresh = fresh + squares[x + i + REACH, part] * lap
                    if m > 1:
                        adj[m - 1][s, x + i + BORDER, part] = fresh
                        keep_split(splits[m - 1], s, x + i + BORDER, part, fresh)
                    if inside:
                        term = fresh * laps[m - 1, s, x + i, part]
                        gathered[i] = term if gathered[i] is None else gathered[i] + term
            if inside:
                for i in range(group):
                    summed = total[x + i, part] + gathered[i]
                    if m > 1:
                        total[x + i, part] = summed
                    else:
                        factor = (2.0 * COURANT / SCALE) * speed[x + i + REACH, part]
                        if shares:
                            line = pl.multiple_of((x + i) * depth + h * half, half)
                            out[pl.ds(line, half), :] = factor * summed
                        else:
                            out[x + i, part] = factor * summed

    def backward(m, first, last, inside):
        ahead = lambda g: mix(splits[m], g * group + BORDER, blend)
        sweep(first, last, lambda g: backward_point(m, g, inside), ahead)

    for load in loads[:3]:
        load.wait()
    square(REACH, REACH + rows)
    prepare(f0, MARGIN, hf0, 0)
    forward_inside(0)
    for k in range(STEPS):
        rims = (0, groups - 1)
        for s in everyone:
            receive(halos[k][s])
            for g in rims:
                forward_point(k, g, (s,))
            if k + 1 < STEPS:
                send(halos[k + 1][s])
        if k + 1 < STEPS:
            forward_inside(k + 1)
        sample(k)
        send(samples[k])
        if k == 0:
            for load in loads[3:]:
                load.wait()
            prepare(a4, BORDER, ha, BORDER)
            receive(adj_halo)
            sweep(0, groups, free_point, lambda g: mix(ha, g * group + BORDER, blend))
            send(border_halo)
            receive(speed_halo)
            square(0, REACH)
            square(REACH + rows, 2 * REACH + rows)
        else:
            receive(samples[k - 1])
            misfits(k - 1, True)
        if shares and k == 1:
            prior.send_noise()
        if shares and k == 2:
            prior.noise_update()

    sent(border_halo)
    misfits(STEPS - 1, False)

    @pl.loop(0, groups, unroll=2)
    def _(g):
        drop_point(g, True)

    backward(3, 1, groups - 1, True)
    receive(samples[STEPS - 1])
    misfits(STEPS - 1, True)
    receive(border_halo)
    far = BORDER // group
    for g in range(far):
        drop_point(-1 - g, False)
        drop_point(groups + g, False)
    outer = [g for t in range(far - 1) for g in (-1 - t, groups + t)]
    reached = outer + [0, groups - 1]
    for g in reached[:2]:
        mix(splits[3], g * group + BORDER, blend)
    for n, g in enumerate(reached):
        backward_point(3, g, g not in outer)
        if n + 2 < len(reached):
            mix(splits[3], reached[n + 2] * group + BORDER, blend)
    for g in (-1, groups):
        mix(splits[2], g * group + BORDER, blend)
    for g in (-1, groups):
        backward_point(2, g, False)
    backward(2, 0, groups, True)
    backward(1, 0, groups, True)
    if shares:
        prior.apply(out)
    for copies in pairs:
        if copies is not border_halo:
            sent(copies)


def shot_gradient(
    velocity,
    prev,
    now,
    later,
    adjoint,
    wavelet,
    source_cells,
    signs,
    record_cells,
    observed,
    noise_field=None,
    step_size=None,
):
    shots, rows, depth, width = now.shape
    receivers = record_cells.shape[1]
    hbm = pl.BlockSpec(memory_space=pl.ANY)
    vmem = pl.BlockSpec(memory_space=pltpu.VMEM)
    smem = pl.BlockSpec(memory_space=pltpu.SMEM)
    f32, bf16 = jnp.float32, jnp.bfloat16
    group = MARGIN
    wide = rows + 2 * REACH
    widest = rows + 2 * BORDER
    exchanges = STEPS * shots + 3 + STEPS
    doms = lax.axis_size("dom")
    shares = 0 if noise_field is None else lax.axis_size("shot")
    more, more_specs, first, last = (), [], [], []
    if shares:
        lines = (doms, rows, width)
        maps = (doms * rows, 3 * doms * rows)
        more = (noise_field.reshape(rows * depth, width), *prior_maps(doms * rows), step_size)
        more_specs = [hbm] * 3 + [smem]
        first = [pltpu.VMEM((rows * depth, width), f32)]
        last = [
            pltpu.VMEM((rows * depth, width), f32),
            pltpu.VMEM(maps, bf16),
            pltpu.VMEM(maps, bf16),
            pltpu.VMEM((shares, *lines), f32),
            pltpu.VMEM((shares, *lines), f32),
            pltpu.VMEM(lines, f32),
            pltpu.VMEM(lines, f32),
            pltpu.VMEM(lines, f32),
            pltpu.VMEM(lines, f32),
            pltpu.VMEM((doms * rows, width), f32),
            pltpu.VMEM(lines, f32),
            pltpu.VMEM(lines, f32),
            pltpu.SemaphoreType.DMA((3,)),
            pltpu.SemaphoreType.DMA((3, doms)),
            pltpu.SemaphoreType.DMA((3, doms)),
            pltpu.SemaphoreType.DMA((2 * shares,)),
            pltpu.SemaphoreType.DMA((2 * shares,)),
        ]
    else:
        first = [pltpu.VMEM((8, width), f32)]
    shape = (rows * depth, width) if shares else (rows, depth, width)
    return pl.pallas_call(
        functools.partial(wave_kernel, doms, shares),
        out_shape=jax.ShapeDtypeStruct(shape, f32),
        in_specs=[hbm] * 5 + [smem] * 3 + [vmem] * 2 + more_specs,
        out_specs=vmem,
        scratch_shapes=first
        + [pltpu.VMEM((shots, rows + 2 * MARGIN, depth, width), f32)] * (STEPS + 1)
        + [pltpu.VMEM((shots, widest, depth, width), f32)] * STEPS
        + [
            pltpu.VMEM((shots, rows, depth, width), f32),
            pltpu.VMEM((shots, rows, depth, width), f32),
            pltpu.VMEM((wide, depth, width), f32),
            pltpu.VMEM((wide, depth, width), f32),
            pltpu.VMEM((STEPS, shots, rows, depth, width), f32),
            pltpu.VMEM((shots, rows, depth, 2 * width), bf16),
            pltpu.VMEM((shots, rows, depth, 2 * width), bf16),
            pltpu.VMEM((shots, widest, depth, 2 * width), bf16),
            pltpu.VMEM((shots, widest, depth, 2 * width), bf16),
            pltpu.VMEM((2 * width, width), bf16),
            pltpu.VMEM((shots, rows, depth, width), f32),
            pltpu.VMEM((shots, widest, depth, width), f32),
            pltpu.VMEM((group * depth, 2 * group * depth), bf16),
            pltpu.VMEM((shots, rows, depth, width), f32),
            pltpu.VMEM((shots, receivers, rows * depth), bf16),
            pltpu.VMEM((shots, widest * depth, receivers), bf16),
            pltpu.VMEM((shots, receivers, width), f32),
            pltpu.VMEM((shots, receivers, width), f32),
            pltpu.VMEM((STEPS, 8, width), f32),
            pltpu.VMEM((STEPS, 8, width), f32),
            pltpu.VMEM((STEPS, 2, 8, width), f32),
            pltpu.VMEM((STEPS, shots, receivers, 2 * width), bf16),
            pltpu.VMEM((rows, depth, width), f32),
            pltpu.SemaphoreType.DMA((5,)),
            pltpu.SemaphoreType.DMA((exchanges, 2)),
            pltpu.SemaphoreType.DMA((exchanges, 2)),
        ]
        + last,
        compiler_params=pltpu.CompilerParams(
            collective_id=0, has_side_effects=True, vmem_limit_bytes=56 * 1024 * 1024
        ),
    )(
        now,
        adjoint,
        prev,
        later,
        velocity,
        wavelet,
        source_cells,
        signs,
        record_cells,
        observed,
        *more,
    )


def prior_maps(length):
    wave = np.arange(length)[:, None]
    phase = wave * (2 * np.arange(length)[None, :] + 1) % (4 * length)
    factor = np.where(wave == 0, math.sqrt(1.0 / length), math.sqrt(2.0 / length))
    basis = factor * np.cos(math.pi / (2.0 * length) * phase)
    gain = 1.0 / np.sqrt(1.0 + wave / (length // 32))
    maps = []
    for weights in (gain * gain, gain):
        whole = basis.T @ (weights * basis)
        high = whole.astype(jnp.bfloat16)
        low = (whole - high.astype(np.float64)).astype(jnp.bfloat16)
        maps.append(jnp.asarray(np.concatenate([high, high, low], axis=1)))
    return maps


def cosine_basis(length):
    wave_index = jnp.arange(length, dtype=jnp.int32)[:, None]
    position = jnp.arange(length, dtype=jnp.int32)[None, :]
    phase = wave_index * (2 * position + 1) % (4 * length)
    angle = math.pi / (2.0 * length) * phase.astype(jnp.float32)
    factor = jnp.where(wave_index == 0, math.sqrt(1.0 / length), math.sqrt(2.0 / length)).astype(
        jnp.float32
    )
    return factor * jnp.cos(angle)


def prior_gain(length, cutoff):
    scaled = jnp.arange(length, dtype=jnp.float32) / float(cutoff)
    return 1.0 / jnp.sqrt(1.0 + scaled)


def precondition(gradient, noise_cols, rate):
    length = gradient.shape[0]
    basis = cosine_basis(length)
    spectrum = prior_gain(length, length // 32)[:, None]
    highest = lax.Precision.HIGHEST
    grad_hat = jnp.dot(basis, gradient.reshape(length, -1), precision=highest)
    noise_hat = jnp.dot(basis, noise_cols.reshape(length, -1), precision=highest)
    weights = spectrum * (-0.5 * rate * spectrum * grad_hat + jnp.sqrt(rate) * noise_hat)
    update = lax.dot_general(basis, weights, (((0,), (0,)), ((), ())), precision=highest)
    return update.reshape(gradient.shape)


def body(
    velocity,
    noise_field,
    step_size,
    field_prev,
    field_now,
    adjoint_next,
    adjoint_now,
    wavelet,
    source_cells,
    source_signs,
    record_cells,
    observed,
):
    fields = (
        velocity,
        field_prev,
        field_now,
        adjoint_next,
        adjoint_now,
        wavelet,
        source_cells,
        source_signs,
        record_cells,
        observed,
    )
    rate = step_size[0]
    rows, depth, width = velocity.shape
    shares = lax.axis_size("shot")
    shot_rows = width // shares
    start = lax.axis_index("shot") * shot_rows
    if depth == shares * lax.axis_size("dom"):
        moved = shot_gradient(*fields, noise_field, step_size).reshape(velocity.shape)
        return lax.dynamic_slice_in_dim(velocity, start, shot_rows, 2) + moved[:, :, :shot_rows]
    partial_value = shot_gradient(*fields)
    share = lax.psum_scatter(partial_value, "shot", scatter_dimension=2, tiled=True)
    noise_part = lax.dynamic_slice_in_dim(noise_field, start, shot_rows, 2)
    grad_cols, noise_cols = (
        lax.all_to_all(share, "dom", split_axis=2, concat_axis=0, tiled=True),
        lax.all_to_all(noise_part, "dom", split_axis=2, concat_axis=0, tiled=True),
    )
    update = precondition(grad_cols, noise_cols, rate)
    returned = lax.all_to_all(update, "dom", split_axis=0, concat_axis=2, tiled=True)
    result = lax.dynamic_slice_in_dim(velocity, start, shot_rows, 2) + returned
    return result


def solution(mesh):
    placed = (
        P("dom", None, None),
        P("dom", None, None),
        P(),
        P("shot", "dom", None, None),
        P("shot", "dom", None, None),
        P("shot", "dom", None, None),
        P("shot", "dom", None, None),
        P("shot", None),
        P("shot", None),
        P("shot", None),
        P("shot", None),
        P("shot", None, None),
    )
    return jax.shard_map(
        body, mesh=mesh, in_specs=placed, out_specs=P("dom", None, "shot"), check_vma=False
    )
```

```python
import functools
import math

import jax
import jax.numpy as jnp
import numpy as np
from jax import lax
from jax.experimental import pallas as pl
from jax.experimental.pallas import tpu as pltpu
from jax.sharding import PartitionSpec as P

STEPS = 4


COEFFS = (-205.0 / 72.0, 8.0 / 5.0, -1.0 / 5.0, 8.0 / 315.0, -1.0 / 560.0)
COURANT = 0.02


MARGIN = 4
MESH = pl.DeviceIdType.MESH


REACH = 2 * MARGIN
BORDER = 3 * MARGIN
WEIGHTS = (-43050.0, 8064.0, -1008.0, 128.0, -9.0)
SCALE = 5040.0


def split_two(value):
    high = value.astype(jnp.bfloat16)
    low = (value - high.astype(jnp.float32)).astype(jnp.bfloat16)
    return high, low


def banded(size, block, centre):
    down = lax.broadcasted_iota(jnp.int32, (size, size), 0)
    over = lax.broadcasted_iota(jnp.int32, (size, size), 1)
    apart = jnp.abs(down - over)
    band = jnp.where(apart == 0, centre, 0.0)
    for r in range(1, MARGIN + 1):
        band = jnp.where(apart == r, WEIGHTS[r], band)
    if block < size:
        band = jnp.where(down // block == over // block, band, 0.0)
    return band.astype(jnp.bfloat16)


WAVE_REFS = 36


class Prior:
    def __init__(
        self,
        doms,
        shares,
        noise_hbm,
        grad_map_hbm,
        noise_map_hbm,
        step_size,
        out,
        noise,
        grad_map,
        noise_map,
        folded,
        sums,
        own,
        noise_fold,
        noise_lines,
        grad_lines,
        base,
        update,
        returned,
        load_sem,
        send_sem,
        recv_sem,
        shot_send,
        shot_recv,
    ):
        self.doms, self.shares = doms, shares
        self.noise, self.out, self.step_size = noise, out, step_size
        self.grad_map, self.noise_map = grad_map, noise_map
        self.folded, self.sums, self.own = folded, sums, own
        self.noise_fold, self.noise_lines, self.grad_lines = noise_fold, noise_lines, grad_lines
        self.base, self.update, self.returned = base, update, returned
        self.me = lax.axis_index("shot")
        self.here = lax.axis_index("dom")
        self.depth = doms * shares
        self.fold, self.rows, self.width = folded.shape[1:]
        self.piece = self.width // shares
        self.group = lax.broadcasted_iota(jnp.int32, (self.rows, self.width), 1) // self.piece
        self.half = doms // 2
        self.near = (self.here // self.half) * self.half
        self.far = self.half - self.near
        self.loads = [
            pltpu.make_async_copy(noise_hbm, noise, load_sem.at[0]),
            pltpu.make_async_copy(noise_map_hbm, noise_map, load_sem.at[1]),
            pltpu.make_async_copy(grad_map_hbm, grad_map, load_sem.at[2]),
        ]
        turn = [lax.rem(self.here + o, self.half) for o in range(self.half)]
        self.away = [self.far + t for t in turn]
        self.close = [self.near + t for t in turn]
        self.sems = (send_sem, recv_sem)
        self.shot_sems = (shot_send, shot_recv)
        self.moves = []
        self.sharing = []

    def load(self):
        for load in self.loads:
            load.start()

    def slabs(self, source, level):
        return [
            source[pl.ds(block * self.fold + level, self.rows, stride=self.depth), :]
            for block in range(self.shares)
        ]

    def join(self, slabs, share):
        merged = None
        for block in range(self.shares):
            shift = (block - share) * self.piece
            if isinstance(share, int):
                shift = shift % self.width
                turned = pltpu.roll(slabs[block], shift, 1) if shift else slabs[block]
            else:
                shift = lax.rem(shift + self.width, self.width)
                turned = pltpu.roll(slabs[block], shift, 1)
            merged = turned if merged is None else jnp.where(self.group == block, turned, merged)
        return merged

    def exchange(self, phase, source_of, target, far):
        peers = self.away if far else self.close
        for o in range(0 if far else 1, self.half):
            index = o + (self.half if far else 0)
            move = pltpu.make_async_remote_copy(
                src_ref=source_of(peers[o]),
                dst_ref=target.at[self.here],
                send_sem=self.sems[0].at[phase, index],
                recv_sem=self.sems[1].at[phase, index],
                device_id={"dom": peers[o]},
                device_id_type=MESH,
            )
            move.start()
            self.moves.append((phase, move))

    def arrive(self, phase):
        for which, move in self.moves:
            if which == phase:
                move.wait_recv()

    def fold_noise(self):
        for load in self.loads:
            load.wait()

        @pl.loop(0, self.fold)
        def _(level):
            self.noise_fold[level] = self.join(self.slabs(self.noise, level), self.me)

    def send_noise(self):
        for far in (True, False):
            self.exchange(0, lambda d: self.noise_fold.at[d], self.noise_lines, far)
        self.noise_lines[self.here] = self.noise_fold[self.here]

    def mapped(self, matrix, lines):
        high, low = split_two(lines[...].reshape(self.doms * self.rows, self.width))
        return jnp.dot(
            matrix[...],
            jnp.concatenate([high, low, high], axis=0),
            preferred_element_type=jnp.float32,
        )

    def noise_update(self):
        self.arrive(0)
        root = jnp.sqrt(jnp.full((1, 1), self.step_size[0], jnp.float32))
        self.base[...] = root * self.mapped(self.noise_map, self.noise_lines)

    def slabs_part(self, source, level, first, count):
        return [
            source[
                pl.ds(first * self.depth + block * self.fold + level, count, stride=self.depth), :
            ]
            for block in range(self.shares)
        ]

    def share_out(self, partial, part, first, count, start, levels):
        group = self.group[:count]

        @pl.loop(0, levels, unroll=2)
        def _(i):
            slabs = self.slabs_part(partial, start + i, first, count)
            for share in range(self.shares):
                merged = None
                for block in range(self.shares):
                    shift = (block - share) * self.piece % self.width
                    turned = pltpu.roll(slabs[block], shift, 1) if shift else slabs[block]
                    if merged is None:
                        merged = turned
                    else:
                        merged = jnp.where(group == block, turned, merged)
                self.folded[share, start + i, pl.ds(first, count)] = merged

        moves = []
        for o in range(1, self.shares):
            peer = lax.rem(self.me + o, self.shares)
            index = o + part * self.shares
            span, lines = pl.ds(start, levels), pl.ds(first, count)
            move = pltpu.make_async_remote_copy(
                src_ref=self.folded.at[peer, span, lines],
                dst_ref=self.sums.at[o, span, lines],
                send_sem=self.shot_sems[0].at[index],
                recv_sem=self.shot_sems[1].at[index],
                device_id={"shot": peer},
                device_id_type=MESH,
            )
            move.start()
            moves.append(move)
        self.sharing.append(moves)

    def share_first(self, partial):
        self.share_out(partial, 0, 0, self.rows // 2, 0, self.doms)

    def apply(self, partial):
        rest = self.rows - self.rows // 2
        self.share_out(partial, 1, self.rows // 2, rest, self.far, self.half)
        self.share_out(partial, 2, self.rows // 2, rest, self.near, self.half)
        self.noise_update()
        sharing = self.sharing
        for move in sharing[0]:
            move.wait_recv()
        for far in (True, False):
            start = self.far if far else self.near
            for move in sharing[1 if far else 2]:
                move.wait_recv()
            span = pl.ds(start, self.half)
            gathered = self.folded[self.me, span]
            for o in range(1, self.shares):
                gathered = gathered + self.sums[o, span]
            self.own[span] = gathered
            self.exchange(1, lambda d: self.own.at[d], self.grad_lines, far)
        self.grad_lines[self.here] = self.own[self.here]
        self.arrive(1)
        pull = self.mapped(self.grad_map, self.grad_lines)
        fresh = self.base[...] - (0.5 * self.step_size[0]) * pull
        self.update[...] = fresh.reshape(self.doms, self.rows, self.width)
        for far in (True, False):
            self.exchange(2, lambda d: self.update.at[d], self.returned, far)
        self.returned[self.here] = self.update[self.here]
        self.arrive(2)
        for d in range(self.doms):
            line = self.returned[d]
            for block in range(self.shares):
                shift = -block * self.piece % self.width
                turned = pltpu.roll(line, shift, 1) if shift else line
                self.out[pl.ds(block * self.fold + d, self.rows, stride=self.depth), :] = turned
        for moves in sharing:
            for move in moves:
                move.wait_send()
        for _, move in self.moves:
            move.wait_send()


def wave_kernel(doms, shares, *refs):
    inputs = 14 if shares else 10
    arrays, out, scratch = refs[:inputs], refs[inputs], refs[inputs + 1 :]
    wave = arrays[:10] + (scratch[0] if shares else out,) + scratch[1:WAVE_REFS]
    rest = arrays[10:] + (out,) + scratch[WAVE_REFS:] if shares else ()
    gradient_steps(doms, shares, rest, *wave)


def gradient_steps(
    doms,
    shares,
    rest,
    now_hbm,
    adj_hbm,
    prev_hbm,
    later_hbm,
    speed_hbm,
    pulse,
    src_cells,
    src_signs,
    record_cells,
    observed,
    out,
    f0,
    f1,
    f2,
    f3,
    f4,
    a4,
    a3,
    a2,
    a1,
    prev,
    later,
    speed,
    squares,
    laps,
    hf0,
    hf1,
    ha,
    hb,
    across_y,
    mixed,
    blend,
    across_z,
    spread_src,
    pick,
    put,
    hot,
    columns,
    measured,
    found,
    beside,
    values,
    total,
    load_sem,
    send_sem,
    recv_sem,
):
    fields = (f0, f1, f2, f3, f4)
    hf = (hf0, hf1)
    shots, rows, depth, width = prev.shape
    here = lax.axis_index("dom")
    left = jnp.maximum(here - 1, 0)
    right = jnp.minimum(here + 1, doms - 1)
    has_left = here > 0
    has_right = here < doms - 1
    group = MARGIN
    groups = rows // group
    half = 16
    halves = depth // half
    f32 = jnp.float32

    loads = [
        pltpu.make_async_copy(now_hbm, f0.at[:, pl.ds(MARGIN, rows)], load_sem.at[0]),
        pltpu.make_async_copy(speed_hbm, speed.at[pl.ds(REACH, rows)], load_sem.at[1]),
        pltpu.make_async_copy(prev_hbm, prev, load_sem.at[2]),
        pltpu.make_async_copy(adj_hbm, a4.at[:, pl.ds(BORDER, rows)], load_sem.at[3]),
        pltpu.make_async_copy(later_hbm, later, load_sem.at[4]),
    ]
    for load in loads:
        load.start()

    barrier = pltpu.get_barrier_semaphore()
    if shares:
        prior = Prior(doms, shares, *rest)
        prior.load()
        for o in range(1, doms):
            peer = {"dom": lax.rem(here + o, doms)}
            pl.semaphore_signal(barrier, inc=1, device_id=peer, device_id_type=MESH)
        for o in range(1, shares):
            peer = {"shot": lax.rem(lax.axis_index("shot") + o, shares)}
            pl.semaphore_signal(barrier, inc=1, device_id=peer, device_id_type=MESH)
        pl.semaphore_wait(barrier, doms + shares - 2)
    else:

        @pl.when(has_left)
        def _():
            pl.semaphore_signal(barrier, inc=1, device_id={"dom": left}, device_id_type=MESH)

        @pl.when(has_right)
        def _():
            pl.semaphore_signal(barrier, inc=1, device_id={"dom": right}, device_id_type=MESH)

        pl.semaphore_wait(barrier, has_left.astype(jnp.int32) + has_right.astype(jnp.int32))

    pairs = []

    def pair(low_source, high_target, high_source, low_target):
        index = len(pairs)
        to_left = pltpu.make_async_remote_copy(
            src_ref=low_source,
            dst_ref=high_target,
            send_sem=send_sem.at[index, 0],
            recv_sem=recv_sem.at[index, 1],
            device_id={"dom": left},
            device_id_type=MESH,
        )
        to_right = pltpu.make_async_remote_copy(
            src_ref=high_source,
            dst_ref=low_target,
            send_sem=send_sem.at[index, 1],
            recv_sem=recv_sem.at[index, 0],
            device_id={"dom": right},
            device_id_type=MESH,
        )
        pairs.append((to_left, to_right))
        return pairs[-1]

    def send(copies):
        @pl.when(has_left)
        def _():
            copies[0].start()

        @pl.when(has_right)
        def _():
            copies[1].start()

    def receive(copies):
        @pl.when(has_left)
        def _():
            copies[1].wait_recv()

        @pl.when(has_right)
        def _():
            copies[0].wait_recv()

    def sent(copies):
        @pl.when(has_left)
        def _():
            copies[0].wait_send()

        @pl.when(has_right)
        def _():
            copies[1].wait_send()

    halos = []
    for k in range(STEPS):
        halos.append([])
        for s in range(shots):
            field = fields[k]
            source = now_hbm if k == 0 else field
            base = 0 if k == 0 else MARGIN
            halos[k].append(
                pair(
                    source.at[s, pl.ds(base, MARGIN)],
                    field.at[s, pl.ds(MARGIN + rows, MARGIN)],
                    source.at[s, pl.ds(base + rows - MARGIN, MARGIN)],
                    field.at[s, pl.ds(0, MARGIN)],
                )
            )
    adj_halo = pair(
        adj_hbm.at[:, pl.ds(0, REACH)],
        a4.at[:, pl.ds(BORDER + rows, REACH)],
        adj_hbm.at[:, pl.ds(rows - REACH, REACH)],
        a4.at[:, pl.ds(BORDER - REACH, REACH)],
    )
    speed_halo = pair(
        speed_hbm.at[pl.ds(0, REACH)],
        speed.at[pl.ds(REACH + rows, REACH)],
        speed_hbm.at[pl.ds(rows - REACH, REACH)],
        speed.at[pl.ds(0, REACH)],
    )
    border_halos = [
        pair(
            a3.at[s, pl.ds(BORDER, BORDER)],
            a3.at[s, pl.ds(BORDER + rows, BORDER)],
            a3.at[s, pl.ds(rows, BORDER)],
            a3.at[s, pl.ds(0, BORDER)],
        )
        for s in range(shots)
    ]
    samples = [
        pair(found.at[k], beside.at[k, 1], found.at[k], beside.at[k, 0]) for k in range(STEPS)
    ]

    for s in range(shots):
        send(halos[0][s])
    send(adj_halo)
    send(speed_halo)

    def clear(first_field, first_adj, first_border, first_speed, side):
        for k in range(STEPS):
            for s in range(shots):
                fields[k][s, pl.ds(first_field, MARGIN)] = jnp.zeros((MARGIN, depth, width), f32)
        for s in range(shots):
            a4[s, pl.ds(first_adj, REACH)] = jnp.zeros((REACH, depth, width), f32)
            a3[s, pl.ds(first_border, BORDER)] = jnp.zeros((BORDER, depth, width), f32)
        speed[pl.ds(first_speed, REACH)] = jnp.zeros((REACH, depth, width), f32)
        for k in range(STEPS):
            beside[k, side] = jnp.zeros(beside.shape[2:], f32)

    @pl.when(jnp.logical_not(has_left))
    def _():
        clear(0, BORDER - REACH, 0, 0, 0)

    @pl.when(jnp.logical_not(has_right))
    def _():
        clear(MARGIN + rows, BORDER + rows, BORDER + rows, REACH + rows, 1)

    across_y[...] = jnp.concatenate([banded(width, width, -43008.0)] * 2, axis=0)
    across_z[...] = jnp.concatenate([banded(group * depth, depth, -42.0)] * 2, axis=1)

    receivers = record_cells.shape[1]
    tiles = receivers // 8
    lane = lax.broadcasted_iota(jnp.int32, (8, width), 1)
    first = here * (rows * depth)
    row_of = lambda cell: lax.div(cell, jnp.int32(width))
    lane_of = lambda cell: lax.rem(cell, jnp.int32(width))
    tile = (width, receivers)
    place = lax.broadcasted_iota(jnp.int32, tile, 0)
    span = 8 * depth
    compact = [jnp.zeros((8, width), f32) for _ in range(STEPS)]
    for s in range(shots):
        cells = record_cells[s : s + 1, :]
        rec_rows = row_of(cells) - first
        table = jnp.where(
            place == STEPS,
            jnp.broadcast_to(rec_rows.astype(f32), tile),
            jnp.broadcast_to(lane_of(cells).astype(f32), tile),
        )
        for k in range(STEPS):
            table = jnp.where(place == k, jnp.broadcast_to(observed[s, k : k + 1, :], tile), table)
        columns[s] = jnp.transpose(table)
        rec_col = columns[s, :, STEPS : STEPS + 1].astype(jnp.int32)
        rec_lane = columns[s, :, STEPS + 1 : STEPS + 2].astype(jnp.int32)
        hot[s] = (lax.broadcasted_iota(jnp.int32, (receivers, width), 1) == rec_lane).astype(f32)
        for k in range(STEPS):
            for j in range(tiles):
                column = columns[s, pl.ds(j * 8, 8), k : k + 1]
                compact[k] = jnp.where(lane == s * tiles + j, column, compact[k])
        count = src_cells.shape[1]
        padded = count + (-count) % 128
        order = lax.broadcasted_iota(jnp.int32, (padded, width), 0)
        across = lax.broadcasted_iota(jnp.int32, (padded, width), 1)
        along = lax.broadcasted_iota(jnp.int32, (1, padded), 1)
        tall = jnp.zeros((padded, width), f32)
        src_rows = jnp.full((1, padded), -1, jnp.int32)
        for j in range(count):
            cell = src_cells[s, j]
            sign = (2 * src_signs[s, j] - 1).astype(f32)
            tall = jnp.where((order == j) & (across == lane_of(cell)), sign, tall)
            src_rows = jnp.where(along == j, row_of(cell) - first, src_rows)
        tall = tall.astype(jnp.bfloat16)

        for c in range(rows * depth // span):
            cell = lax.broadcasted_iota(jnp.int32, (receivers, span), 1) + c * span
            pick[s, :, c * span : (c + 1) * span] = (
                (cell == rec_col).astype(f32).astype(jnp.bfloat16)
            )

        @pl.loop(0, rows * depth // span)
        def _(c):
            cell = lax.broadcasted_iota(jnp.int32, (span, padded), 0) + c * span
            wide = (cell == src_rows).astype(f32).astype(jnp.bfloat16)
            spots = jnp.dot(wide, tall, preferred_element_type=f32)
            spread_src[s, pl.ds(c * 8, 8)] = spots.reshape(8, depth, width)

        @pl.loop(0, (rows + 2 * BORDER) // 8)
        def _(c):
            cell = lax.broadcasted_iota(jnp.int32, (span, receivers), 0)
            cell = cell + (c * span - BORDER * depth)
            put[s, pl.ds(pl.multiple_of(c * span, span), span)] = (
                (cell == rec_rows).astype(f32).astype(jnp.bfloat16)
            )

    for k in range(STEPS):
        measured[k] = compact[k]

    def keep_split(ref, s, row, part, value):
        high, low = split_two(value)
        ref[s, row, part, 0:width] = high
        ref[s, row, part, width : 2 * width] = low

    everyone = tuple(range(shots))

    def mix(split, row, mixed):
        lines = [
            split[s, pl.ds(row, group)].reshape(group * depth, 2 * width) for s in everyone
        ]
        highs = jnp.concatenate([line[:, :width] for line in lines], axis=1)
        lows = jnp.concatenate([line[:, width:] for line in lines], axis=1)
        down = jnp.dot(
            across_z[...], jnp.concatenate([highs, lows], axis=0), preferred_element_type=f32
        )
        over = jnp.dot(
            jnp.concatenate(lines, axis=0), across_y[...], preferred_element_type=f32
        )
        for s in everyone:
            both = over[s * group * depth : (s + 1) * group * depth]
            both = both + down[:, s * width : (s + 1) * width]
            mixed[s, pl.ds(row, group)] = both.reshape(group, depth, width)

    def beside_x(window, i):
        summed = WEIGHTS[1] * (window[i + 3] + window[i + 5])
        for r in range(2, MARGIN + 1):
            summed += WEIGHTS[r] * (window[i + MARGIN + r] + window[i + MARGIN - r])
        return summed

    def sweep(first, last, point, ahead):
        ahead(first)

        @pl.loop(first, last, unroll=2)
        def _(g):
            point(g)
            ahead(g + 1)

    def square(first, last):
        @pl.loop(first, last)
        def _(x):
            squares[x] = (COURANT / SCALE) * speed[x] * speed[x]

    parts = [pl.ds(h * half, half) for h in range(halves)]
    def prepare(field, margin, split, split_margin):
        @pl.loop(0, rows)
        def _(x):
            for s in range(shots):
                for part in parts:
                    keep_split(split, s, x + split_margin, part, field[s, x + margin, part])

    def forward_point(k, g, which):
        x = g * group
        field, target, split = fields[k], fields[k + 1], hf[(k + 1) % 2]
        for part in parts:
            for s in which:
                window = [field[s, x + i, part] for i in range(group + 2 * MARGIN)]
                for i in range(group):
                    lap = beside_x(window, i) + mixed[s, x + i, part]
                    laps[k, s, x + i, part] = lap
                    if k == 0:
                        before = prev[s, x + i, part]
                    else:
                        before = fields[k - 1][s, x + i + MARGIN, part]
                    fresh = 2.0 * window[i + MARGIN] - before
                    fresh = fresh + pulse[s, k] * spread_src[s, x + i, part]
                    fresh = fresh + squares[x + i + REACH, part] * lap
                    target[s, x + i + MARGIN, part] = fresh
                    keep_split(split, s, x + i, part, fresh)

    def forward_inside(k):
        ahead = lambda g: mix(hf[k % 2], g * group, mixed)
        ahead(0)
        sweep(1, groups - 1, lambda g: forward_point(k, g, everyone), ahead)

    def sample(k):
        split = hf[(k + 1) % 2]
        gathered = jnp.zeros((8, width), f32)
        for s in range(shots):
            both = jnp.dot(
                pick[s],
                split[s].reshape(rows * depth, 2 * width),
                preferred_element_type=f32,
            )
            chosen = (both[:, :width] + both[:, width:]) * hot[s]
            column = jnp.sum(chosen, axis=1, keepdims=True)
            for j in range(tiles):
                gathered = jnp.where(
                    lane == s * tiles + j, column[j * 8 : (j + 1) * 8], gathered
                )
        found[k] = gathered

    def misfits(k, everywhere):
        missed = found[k] - measured[k]
        if everywhere:
            missed = missed + (beside[k, 0] + beside[k, 1])
        for s in range(shots):
            for j in range(0, tiles, 2):
                block = []
                for t in (j, j + 1):
                    at = s * tiles + t
                    block.append(missed[:, at : at + 1] * hot[s, pl.ds(t * 8, 8)])
                high, low = split_two(jnp.concatenate(block, axis=0))
                values[k, s, pl.ds(j * 8, 16), 0:width] = high
                values[k, s, pl.ds(j * 8, 16), width : 2 * width] = low

    def dropped(k, s, x):
        at = pl.multiple_of((x + BORDER) * depth, group * depth)
        both = jnp.dot(
            put[s, pl.ds(at, group * depth)], values[k, s], preferred_element_type=f32
        )
        return (both[:, :width] + both[:, width:]).reshape(group, depth, width)

    def free_point(g):
        x = g * group
        for part in parts:
            for s in range(shots):
                window = [
                    a4[s, x + BORDER - MARGIN + i, part] for i in range(group + 2 * MARGIN)
                ]
                for i in range(group):
                    lap = beside_x(window, i) + blend[s, x + BORDER + i, part]
                    fresh = 2.0 * window[i + MARGIN] - later[s, x + i, part]
                    a3[s, x + i + BORDER, part] = fresh + squares[x + i + REACH, part] * lap

    def drop_point(g, inside):
        x = g * group
        gathered = None
        for s in range(shots):
            fresh = a3[s, pl.ds(x + BORDER, group)] + dropped(STEPS - 1, s, x)
            a3[s, pl.ds(x + BORDER, group)] = fresh
            high, low = split_two(fresh)
            hb[s, pl.ds(x + BORDER, group), :, 0:width] = high
            hb[s, pl.ds(x + BORDER, group), :, width : 2 * width] = low
            if inside:
                term = fresh * laps[STEPS - 1, s, pl.ds(x, group)]
                gathered = term if gathered is None else gathered + term
        if inside:
            total[pl.ds(x, group)] = gathered

    adj = {4: a4, 3: a3, 2: a2, 1: a1}
    splits = {4: ha, 3: hb, 2: ha, 1: hb}

    def backward_point(m, g, inside):
        x = g * group
        field, after = adj[m], adj[m + 1]
        fallen = [dropped(m - 1, s, x) for s in range(shots)]
        for h, part in enumerate(parts):
            rim = slice(h * half, (h + 1) * half)
            gathered = [None] * group
            for s in range(shots):
                window = [
                    field[s, x + BORDER - MARGIN + i, part] for i in range(group + 2 * MARGIN)
                ]
                for i in range(group):
                    lap = beside_x(window, i) + blend[s, x + BORDER + i, part]
                    fresh = 2.0 * window[i + MARGIN] - after[s, x + i + BORDER, part]
                    fresh = fresh + fallen[s][i, rim]
                    fresh = fresh + squares[x + i + REACH, part] * lap
                    if m > 1:
                        adj[m - 1][s, x + i + BORDER, part] = fresh
                        keep_split(splits[m - 1], s, x + i + BORDER, part, fresh)
                    if inside:
                        term = fresh * laps[m - 1, s, x + i, part]
                        gathered[i] = term if gathered[i] is None else gathered[i] + term
            if inside:
                for i in range(group):
                    summed = total[x + i, part] + gathered[i]
                    if m > 1:
                        total[x + i, part] = summed
                    else:
                        factor = (2.0 * COURANT / SCALE) * speed[x + i + REACH, part]
                        if shares:
                            line = pl.multiple_of((x + i) * depth + h * half, half)
                            out[pl.ds(line, half), :] = factor * summed
                        else:
                            out[x + i, part] = factor * summed

    def backward(m, first, last, inside):
        ahead = lambda g: mix(splits[m], g * group + BORDER, blend)
        sweep(first, last, lambda g: backward_point(m, g, inside), ahead)

    for load in loads[:3]:
        load.wait()
    square(REACH, REACH + rows)
    prepare(f0, MARGIN, hf0, 0)
    forward_inside(0)
    for k in range(STEPS):
        rims = (0, groups - 1)
        for s in everyone:
            receive(halos[k][s])
            for g in rims:
                forward_point(k, g, (s,))
            if k + 1 < STEPS:
                send(halos[k + 1][s])
        for s in everyone:
            if k == (1 if 2 * s < shots else 2):
                send(border_halos[s])
        if k == 1:
            sample(0)
            send(samples[0])
        if k + 1 < STEPS:
            forward_inside(k + 1)
        if k > 0:
            sample(k)
            send(samples[k])
        if k == 0:
            for load in loads[3:]:
                load.wait()
            prepare(a4, BORDER, ha, BORDER)
            receive(adj_halo)
            sweep(0, groups, free_point, lambda g: mix(ha, g * group + BORDER, blend))
            receive(speed_halo)
            square(0, REACH)
            square(REACH + rows, 2 * REACH + rows)
        else:
            receive(samples[k - 1])
            misfits(k - 1, True)
        if shares and k == 2:
            prior.fold_noise()
    if shares:
        prior.send_noise()

    for copies in border_halos:
        sent(copies)
    misfits(STEPS - 1, False)

    @pl.loop(0, groups, unroll=2)
    def _(g):
        drop_point(g, True)

    backward(3, 1, groups - 1, True)
    receive(samples[STEPS - 1])
    misfits(STEPS - 1, True)
    for copies in border_halos:
        receive(copies)
    far = BORDER // group
    for g in range(far):
        drop_point(-1 - g, False)
        drop_point(groups + g, False)
    outer = [g for t in range(far - 1) for g in (-1 - t, groups + t)]
    reached = outer + [0, groups - 1]
    for g in reached[:2]:
        mix(splits[3], g * group + BORDER, blend)
    for n, g in enumerate(reached):
        backward_point(3, g, g not in outer)
        if n + 2 < len(reached):
            mix(splits[3], reached[n + 2] * group + BORDER, blend)
    for g in (-1, groups):
        mix(splits[2], g * group + BORDER, blend)
    for g in (-1, groups):
        backward_point(2, g, False)
    backward(2, 0, groups, True)
    backward(1, 0, groups // 2, True)
    if shares:
        prior.share_first(out)
    backward(1, groups // 2, groups, True)
    if shares:
        prior.apply(out)
    for copies in pairs:
        if not any(copies is other for other in border_halos):
            sent(copies)


def shot_gradient(
    velocity,
    prev,
    now,
    later,
    adjoint,
    wavelet,
    source_cells,
    signs,
    record_cells,
    observed,
    noise_field=None,
    step_size=None,
):
    shots, rows, depth, width = now.shape
    receivers = record_cells.shape[1]
    hbm = pl.BlockSpec(memory_space=pl.ANY)
    vmem = pl.BlockSpec(memory_space=pltpu.VMEM)
    smem = pl.BlockSpec(memory_space=pltpu.SMEM)
    f32, bf16 = jnp.float32, jnp.bfloat16
    group = MARGIN
    wide = rows + 2 * REACH
    widest = rows + 2 * BORDER
    exchanges = STEPS * shots + 2 + shots + STEPS
    doms = lax.axis_size("dom")
    shares = 0 if noise_field is None else lax.axis_size("shot")
    more, more_specs, first, last = (), [], [], []
    if shares:
        lines = (doms, rows, width)
        maps = (doms * rows, 3 * doms * rows)
        more = (noise_field.reshape(rows * depth, width), *prior_maps(doms * rows), step_size)
        more_specs = [hbm] * 3 + [smem]
        first = [pltpu.VMEM((rows * depth, width), f32)]
        last = [
            pltpu.VMEM((rows * depth, width), f32),
            pltpu.VMEM(maps, bf16),
            pltpu.VMEM(maps, bf16),
            pltpu.VMEM((shares, *lines), f32),
            pltpu.VMEM((shares, *lines), f32),
            pltpu.VMEM(lines, f32),
            pltpu.VMEM(lines, f32),
            pltpu.VMEM(lines, f32),
            pltpu.VMEM(lines, f32),
            pltpu.VMEM((doms * rows, width), f32),
            pltpu.VMEM(lines, f32),
            pltpu.VMEM(lines, f32),
            pltpu.SemaphoreType.DMA((3,)),
            pltpu.SemaphoreType.DMA((3, doms)),
            pltpu.SemaphoreType.DMA((3, doms)),
            pltpu.SemaphoreType.DMA((3 * shares,)),
            pltpu.SemaphoreType.DMA((3 * shares,)),
        ]
    else:
        first = [pltpu.VMEM((8, width), f32)]
    shape = (rows * depth, width) if shares else (rows, depth, width)
    return pl.pallas_call(
        functools.partial(wave_kernel, doms, shares),
        out_shape=jax.ShapeDtypeStruct(shape, f32),
        in_specs=[hbm] * 5 + [smem] * 3 + [vmem] * 2 + more_specs,
        out_specs=vmem,
        scratch_shapes=first
        + [pltpu.VMEM((shots, rows + 2 * MARGIN, depth, width), f32)] * (STEPS + 1)
        + [pltpu.VMEM((shots, widest, depth, width), f32)] * STEPS
        + [
            pltpu.VMEM((shots, rows, depth, width), f32),
            pltpu.VMEM((shots, rows, depth, width), f32),
            pltpu.VMEM((wide, depth, width), f32),
            pltpu.VMEM((wide, depth, width), f32),
            pltpu.VMEM((STEPS, shots, rows, depth, width), f32),
            pltpu.VMEM((shots, rows, depth, 2 * width), bf16),
            pltpu.VMEM((shots, rows, depth, 2 * width), bf16),
            pltpu.VMEM((shots, widest, depth, 2 * width), bf16),
            pltpu.VMEM((shots, widest, depth, 2 * width), bf16),
            pltpu.VMEM((2 * width, width), bf16),
            pltpu.VMEM((shots, rows, depth, width), f32),
            pltpu.VMEM((shots, widest, depth, width), f32),
            pltpu.VMEM((group * depth, 2 * group * depth), bf16),
            pltpu.VMEM((shots, rows, depth, width), f32),
            pltpu.VMEM((shots, receivers, rows * depth), bf16),
            pltpu.VMEM((shots, widest * depth, receivers), bf16),
            pltpu.VMEM((shots, receivers, width), f32),
            pltpu.VMEM((shots, receivers, width), f32),
            pltpu.VMEM((STEPS, 8, width), f32),
            pltpu.VMEM((STEPS, 8, width), f32),
            pltpu.VMEM((STEPS, 2, 8, width), f32),
            pltpu.VMEM((STEPS, shots, receivers, 2 * width), bf16),
            pltpu.VMEM((rows, depth, width), f32),
            pltpu.SemaphoreType.DMA((5,)),
            pltpu.SemaphoreType.DMA((exchanges, 2)),
            pltpu.SemaphoreType.DMA((exchanges, 2)),
        ]
        + last,
        compiler_params=pltpu.CompilerParams(
            collective_id=0, has_side_effects=True, vmem_limit_bytes=56 * 1024 * 1024
        ),
    )(
        now,
        adjoint,
        prev,
        later,
        velocity,
        wavelet,
        source_cells,
        signs,
        record_cells,
        observed,
        *more,
    )


def prior_maps(length):
    wave = np.arange(length)[:, None]
    phase = wave * (2 * np.arange(length)[None, :] + 1) % (4 * length)
    factor = np.where(wave == 0, math.sqrt(1.0 / length), math.sqrt(2.0 / length))
    basis = factor * np.cos(math.pi / (2.0 * length) * phase)
    gain = 1.0 / np.sqrt(1.0 + wave / (length // 32))
    maps = []
    for weights in (gain * gain, gain):
        whole = basis.T @ (weights * basis)
        high = whole.astype(jnp.bfloat16)
        low = (whole - high.astype(np.float64)).astype(jnp.bfloat16)
        maps.append(jnp.asarray(np.concatenate([high, high, low], axis=1)))
    return maps


def cosine_basis(length):
    wave_index = jnp.arange(length, dtype=jnp.int32)[:, None]
    position = jnp.arange(length, dtype=jnp.int32)[None, :]
    phase = wave_index * (2 * position + 1) % (4 * length)
    angle = math.pi / (2.0 * length) * phase.astype(jnp.float32)
    factor = jnp.where(wave_index == 0, math.sqrt(1.0 / length), math.sqrt(2.0 / length)).astype(
        jnp.float32
    )
    return factor * jnp.cos(angle)


def prior_gain(length, cutoff):
    scaled = jnp.arange(length, dtype=jnp.float32) / float(cutoff)
    return 1.0 / jnp.sqrt(1.0 + scaled)


def precondition(gradient, noise_cols, rate):
    length = gradient.shape[0]
    basis = cosine_basis(length)
    spectrum = prior_gain(length, length // 32)[:, None]
    highest = lax.Precision.HIGHEST
    grad_hat = jnp.dot(basis, gradient.reshape(length, -1), precision=highest)
    noise_hat = jnp.dot(basis, noise_cols.reshape(length, -1), precision=highest)
    weights = spectrum * (-0.5 * rate * spectrum * grad_hat + jnp.sqrt(rate) * noise_hat)
    update = lax.dot_general(basis, weights, (((0,), (0,)), ((), ())), precision=highest)
    return update.reshape(gradient.shape)


def body(
    velocity,
    noise_field,
    step_size,
    field_prev,
    field_now,
    adjoint_next,
    adjoint_now,
    wavelet,
    source_cells,
    source_signs,
    record_cells,
    observed,
):
    fields = (
        velocity,
        field_prev,
        field_now,
        adjoint_next,
        adjoint_now,
        wavelet,
        source_cells,
        source_signs,
        record_cells,
        observed,
    )
    rate = step_size[0]
    rows, depth, width = velocity.shape
    shares = lax.axis_size("shot")
    shot_rows = width // shares
    start = lax.axis_index("shot") * shot_rows
    if depth == shares * lax.axis_size("dom"):
        moved = shot_gradient(*fields, noise_field, step_size).reshape(velocity.shape)
        return lax.dynamic_slice_in_dim(velocity, start, shot_rows, 2) + moved[:, :, :shot_rows]
    partial_value = shot_gradient(*fields)
    share = lax.psum_scatter(partial_value, "shot", scatter_dimension=2, tiled=True)
    noise_part = lax.dynamic_slice_in_dim(noise_field, start, shot_rows, 2)
    grad_cols, noise_cols = (
        lax.all_to_all(share, "dom", split_axis=2, concat_axis=0, tiled=True),
        lax.all_to_all(noise_part, "dom", split_axis=2, concat_axis=0, tiled=True),
    )
    update = precondition(grad_cols, noise_cols, rate)
    returned = lax.all_to_all(update, "dom", split_axis=0, concat_axis=2, tiled=True)
    result = lax.dynamic_slice_in_dim(velocity, start, shot_rows, 2) + returned
    return result


def solution(mesh):
    placed = (
        P("dom", None, None),
        P("dom", None, None),
        P(),
        P("shot", "dom", None, None),
        P("shot", "dom", None, None),
        P("shot", "dom", None, None),
        P("shot", "dom", None, None),
        P("shot", None),
        P("shot", None),
        P("shot", None),
        P("shot", None),
        P("shot", None, None),
    )
    return jax.shard_map(
        body, mesh=mesh, in_specs=placed, out_specs=P("dom", None, "shot"), check_vma=False
    )
```

```python
import functools
import math

import jax
import jax.numpy as jnp
import numpy as np
from jax import lax
from jax.experimental import pallas as pl
from jax.experimental.pallas import tpu as pltpu
from jax.sharding import PartitionSpec as P

STEPS = 4


COEFFS = (-205.0 / 72.0, 8.0 / 5.0, -1.0 / 5.0, 8.0 / 315.0, -1.0 / 560.0)
COURANT = 0.02


MARGIN = 4
MESH = pl.DeviceIdType.MESH


REACH = 2 * MARGIN
BORDER = 3 * MARGIN
WEIGHTS = (-43050.0, 8064.0, -1008.0, 128.0, -9.0)
SCALE = 5040.0


def split_two(value):
    high = value.astype(jnp.bfloat16)
    low = (value - high.astype(jnp.float32)).astype(jnp.bfloat16)
    return high, low


def banded(size, block, centre):
    down = lax.broadcasted_iota(jnp.int32, (size, size), 0)
    over = lax.broadcasted_iota(jnp.int32, (size, size), 1)
    apart = jnp.abs(down - over)
    band = jnp.where(apart == 0, centre, 0.0)
    for r in range(1, MARGIN + 1):
        band = jnp.where(apart == r, WEIGHTS[r], band)
    if block < size:
        band = jnp.where(down // block == over // block, band, 0.0)
    return band.astype(jnp.bfloat16)


WAVE_REFS = 36


class Prior:
    def __init__(
        self,
        doms,
        shares,
        noise_hbm,
        grad_map_hbm,
        noise_map_hbm,
        step_size,
        out,
        noise,
        grad_map,
        noise_map,
        folded,
        sums,
        own,
        noise_fold,
        noise_lines,
        grad_lines,
        base,
        update,
        returned,
        load_sem,
        send_sem,
        recv_sem,
        shot_send,
        shot_recv,
    ):
        self.doms, self.shares = doms, shares
        self.noise, self.out, self.step_size = noise, out, step_size
        self.grad_map, self.noise_map = grad_map, noise_map
        self.folded, self.sums, self.own = folded, sums, own
        self.noise_fold, self.noise_lines, self.grad_lines = noise_fold, noise_lines, grad_lines
        self.base, self.update, self.returned = base, update, returned
        self.me = lax.axis_index("shot")
        self.here = lax.axis_index("dom")
        self.depth = doms * shares
        self.fold, self.rows, self.width = folded.shape[1:]
        self.piece = self.width // shares
        self.group = lax.broadcasted_iota(jnp.int32, (self.rows, self.width), 1) // self.piece
        self.half = doms // 2
        self.near = (self.here // self.half) * self.half
        self.far = self.half - self.near
        self.loads = [
            pltpu.make_async_copy(noise_hbm, noise, load_sem.at[0]),
            pltpu.make_async_copy(noise_map_hbm, noise_map, load_sem.at[1]),
            pltpu.make_async_copy(grad_map_hbm, grad_map, load_sem.at[2]),
        ]
        turn = [lax.rem(self.here + o, self.half) for o in range(self.half)]
        self.away = [self.far + t for t in turn]
        self.close = [self.near + t for t in turn]
        self.sems = (send_sem, recv_sem)
        self.shot_sems = (shot_send, shot_recv)
        self.moves = []
        self.sharing = []

    def load(self):
        for load in self.loads:
            load.start()

    def slabs(self, source, level):
        return [
            source[pl.ds(block * self.fold + level, self.rows, stride=self.depth), :]
            for block in range(self.shares)
        ]

    def join(self, slabs, share):
        merged = None
        for block in range(self.shares):
            shift = (block - share) * self.piece
            if isinstance(share, int):
                shift = shift % self.width
                turned = pltpu.roll(slabs[block], shift, 1) if shift else slabs[block]
            else:
                shift = lax.rem(shift + self.width, self.width)
                turned = pltpu.roll(slabs[block], shift, 1)
            merged = turned if merged is None else jnp.where(self.group == block, turned, merged)
        return merged

    def exchange(self, phase, source_of, target, far):
        peers = self.away if far else self.close
        for o in range(0 if far else 1, self.half):
            index = o + (self.half if far else 0)
            move = pltpu.make_async_remote_copy(
                src_ref=source_of(peers[o]),
                dst_ref=target.at[self.here],
                send_sem=self.sems[0].at[phase, index],
                recv_sem=self.sems[1].at[phase, index],
                device_id={"dom": peers[o]},
                device_id_type=MESH,
            )
            move.start()
            self.moves.append((phase, move))

    def arrive(self, phase):
        for which, move in self.moves:
            if which == phase:
                move.wait_recv()

    def fold_noise(self):
        for load in self.loads:
            load.wait()

        @pl.loop(0, self.fold)
        def _(level):
            self.noise_fold[level] = self.join(self.slabs(self.noise, level), self.me)

    def send_noise(self):
        for far in (True, False):
            self.exchange(0, lambda d: self.noise_fold.at[d], self.noise_lines, far)
        self.noise_lines[self.here] = self.noise_fold[self.here]

    def mapped(self, matrix, lines):
        high, low = split_two(lines[...].reshape(self.doms * self.rows, self.width))
        return jnp.dot(
            matrix[...],
            jnp.concatenate([high, low, high], axis=0),
            preferred_element_type=jnp.float32,
        )

    def noise_update(self):
        self.arrive(0)
        root = jnp.sqrt(jnp.full((1, 1), self.step_size[0], jnp.float32))
        self.base[...] = root * self.mapped(self.noise_map, self.noise_lines)

    def slabs_part(self, source, level, first, count):
        return [
            source[
                pl.ds(first * self.depth + block * self.fold + level, count, stride=self.depth), :
            ]
            for block in range(self.shares)
        ]

    def share_out(self, partial, part, first, count, start, levels):
        group = self.group[:count]

        @pl.loop(0, levels, unroll=2)
        def _(i):
            slabs = self.slabs_part(partial, start + i, first, count)
            for share in range(self.shares):
                merged = None
                for block in range(self.shares):
                    shift = (block - share) * self.piece % self.width
                    turned = pltpu.roll(slabs[block], shift, 1) if shift else slabs[block]
                    if merged is None:
                        merged = turned
                    else:
                        merged = jnp.where(group == block, turned, merged)
                self.folded[share, start + i, pl.ds(first, count)] = merged

        moves = []
        for o in range(1, self.shares):
            peer = lax.rem(self.me + o, self.shares)
            index = o + part * self.shares
            span, lines = pl.ds(start, levels), pl.ds(first, count)
            move = pltpu.make_async_remote_copy(
                src_ref=self.folded.at[peer, span, lines],
                dst_ref=self.sums.at[o, span, lines],
                send_sem=self.shot_sems[0].at[index],
                recv_sem=self.shot_sems[1].at[index],
                device_id={"shot": peer},
                device_id_type=MESH,
            )
            move.start()
            moves.append(move)
        self.sharing.append(moves)

    def share_first(self, partial):
        self.share_out(partial, 0, 0, self.rows // 2, 0, self.doms)

    def apply(self, partial):
        rest = self.rows - self.rows // 2
        self.share_out(partial, 1, self.rows // 2, rest, self.far, self.half)
        self.share_out(partial, 2, self.rows // 2, rest, self.near, self.half)
        self.noise_update()
        sharing = self.sharing
        for move in sharing[0]:
            move.wait_recv()
        for far in (True, False):
            start = self.far if far else self.near
            for move in sharing[1 if far else 2]:
                move.wait_recv()
            span = pl.ds(start, self.half)
            gathered = self.folded[self.me, span]
            for o in range(1, self.shares):
                gathered = gathered + self.sums[o, span]
            self.own[span] = gathered
            self.exchange(1, lambda d: self.own.at[d], self.grad_lines, far)
        self.grad_lines[self.here] = self.own[self.here]
        self.arrive(1)
        pull = self.mapped(self.grad_map, self.grad_lines)
        fresh = self.base[...] - (0.5 * self.step_size[0]) * pull
        self.update[...] = fresh.reshape(self.doms, self.rows, self.width)
        for far in (True, False):
            self.exchange(2, lambda d: self.update.at[d], self.returned, far)
        self.returned[self.here] = self.update[self.here]
        self.arrive(2)
        for d in range(self.doms):
            line = self.returned[d]
            for block in range(self.shares):
                shift = -block * self.piece % self.width
                turned = pltpu.roll(line, shift, 1) if shift else line
                self.out[pl.ds(block * self.fold + d, self.rows, stride=self.depth), :] = turned
        for moves in sharing:
            for move in moves:
                move.wait_send()
        for _, move in self.moves:
            move.wait_send()


def wave_kernel(doms, shares, *refs):
    inputs = 14 if shares else 10
    arrays, out, scratch = refs[:inputs], refs[inputs], refs[inputs + 1 :]
    wave = arrays[:10] + (scratch[0] if shares else out,) + scratch[1:WAVE_REFS]
    small, scratch = scratch[WAVE_REFS : WAVE_REFS + 6], scratch[WAVE_REFS + 6 :]
    staged = [
        pltpu.make_async_copy(source, target, small[5].at[i])
        for i, (source, target) in enumerate(zip(arrays[5:10], small))
    ]
    for copy in staged:
        copy.start()
    wave = wave[:5] + small[:5] + wave[10:]
    rest = arrays[10:] + (out,) + scratch if shares else ()
    gradient_steps(doms, shares, rest, staged, *wave)


def gradient_steps(
    doms,
    shares,
    rest,
    staged,
    now_hbm,
    adj_hbm,
    prev_hbm,
    later_hbm,
    speed_hbm,
    pulse,
    src_cells,
    src_signs,
    record_cells,
    observed,
    out,
    f0,
    f1,
    f2,
    f3,
    f4,
    a4,
    a3,
    a2,
    a1,
    prev,
    later,
    speed,
    squares,
    laps,
    hf0,
    hf1,
    ha,
    hb,
    across_y,
    mixed,
    blend,
    across_z,
    spread_src,
    pick,
    put,
    hot,
    columns,
    measured,
    found,
    beside,
    values,
    total,
    load_sem,
    send_sem,
    recv_sem,
):
    fields = (f0, f1, f2, f3, f4)
    hf = (hf0, hf1)
    shots, rows, depth, width = prev.shape
    here = lax.axis_index("dom")
    left = jnp.maximum(here - 1, 0)
    right = jnp.minimum(here + 1, doms - 1)
    has_left = here > 0
    has_right = here < doms - 1
    group = MARGIN
    groups = rows // group
    half = 16
    halves = depth // half
    f32 = jnp.float32

    loads = [
        pltpu.make_async_copy(now_hbm, f0.at[:, pl.ds(MARGIN, rows)], load_sem.at[0]),
        pltpu.make_async_copy(speed_hbm, speed.at[pl.ds(REACH, rows)], load_sem.at[1]),
        pltpu.make_async_copy(prev_hbm, prev, load_sem.at[2]),
        pltpu.make_async_copy(adj_hbm, a4.at[:, pl.ds(BORDER, rows)], load_sem.at[3]),
        pltpu.make_async_copy(later_hbm, later, load_sem.at[4]),
    ]
    for load in loads:
        load.start()

    barrier = pltpu.get_barrier_semaphore()
    if shares:
        prior = Prior(doms, shares, *rest)
        prior.load()
        for o in range(1, doms):
            peer = {"dom": lax.rem(here + o, doms)}
            pl.semaphore_signal(barrier, inc=1, device_id=peer, device_id_type=MESH)
        for o in range(1, shares):
            peer = {"shot": lax.rem(lax.axis_index("shot") + o, shares)}
            pl.semaphore_signal(barrier, inc=1, device_id=peer, device_id_type=MESH)
        pl.semaphore_wait(barrier, doms + shares - 2)
    else:

        @pl.when(has_left)
        def _():
            pl.semaphore_signal(barrier, inc=1, device_id={"dom": left}, device_id_type=MESH)

        @pl.when(has_right)
        def _():
            pl.semaphore_signal(barrier, inc=1, device_id={"dom": right}, device_id_type=MESH)

        pl.semaphore_wait(barrier, has_left.astype(jnp.int32) + has_right.astype(jnp.int32))

    pairs = []

    def pair(low_source, high_target, high_source, low_target):
        index = len(pairs)
        to_left = pltpu.make_async_remote_copy(
            src_ref=low_source,
            dst_ref=high_target,
            send_sem=send_sem.at[index, 0],
            recv_sem=recv_sem.at[index, 1],
            device_id={"dom": left},
            device_id_type=MESH,
        )
        to_right = pltpu.make_async_remote_copy(
            src_ref=high_source,
            dst_ref=low_target,
            send_sem=send_sem.at[index, 1],
            recv_sem=recv_sem.at[index, 0],
            device_id={"dom": right},
            device_id_type=MESH,
        )
        pairs.append((to_left, to_right))
        return pairs[-1]

    def send(copies):
        @pl.when(has_left)
        def _():
            copies[0].start()

        @pl.when(has_right)
        def _():
            copies[1].start()

    def receive(copies):
        @pl.when(has_left)
        def _():
            copies[1].wait_recv()

        @pl.when(has_right)
        def _():
            copies[0].wait_recv()

    def sent(copies):
        @pl.when(has_left)
        def _():
            copies[0].wait_send()

        @pl.when(has_right)
        def _():
            copies[1].wait_send()

    halos = []
    for k in range(STEPS):
        halos.append([])
        for s in range(shots):
            field = fields[k]
            source = now_hbm if k == 0 else field
            base = 0 if k == 0 else MARGIN
            halos[k].append(
                pair(
                    source.at[s, pl.ds(base, MARGIN)],
                    field.at[s, pl.ds(MARGIN + rows, MARGIN)],
                    source.at[s, pl.ds(base + rows - MARGIN, MARGIN)],
                    field.at[s, pl.ds(0, MARGIN)],
                )
            )
    adj_halo = pair(
        adj_hbm.at[:, pl.ds(0, REACH)],
        a4.at[:, pl.ds(BORDER + rows, REACH)],
        adj_hbm.at[:, pl.ds(rows - REACH, REACH)],
        a4.at[:, pl.ds(BORDER - REACH, REACH)],
    )
    speed_halo = pair(
        speed_hbm.at[pl.ds(0, REACH)],
        speed.at[pl.ds(REACH + rows, REACH)],
        speed_hbm.at[pl.ds(rows - REACH, REACH)],
        speed.at[pl.ds(0, REACH)],
    )
    border_halos = [
        pair(
            a3.at[s, pl.ds(BORDER, BORDER)],
            a3.at[s, pl.ds(BORDER + rows, BORDER)],
            a3.at[s, pl.ds(rows, BORDER)],
            a3.at[s, pl.ds(0, BORDER)],
        )
        for s in range(shots)
    ]
    samples = [
        pair(found.at[k], beside.at[k, 1], found.at[k], beside.at[k, 0]) for k in range(STEPS)
    ]

    for s in range(shots):
        send(halos[0][s])

    def clear(first_field, first_adj, first_border, first_speed, side):
        for k in range(STEPS):
            for s in range(shots):
                fields[k][s, pl.ds(first_field, MARGIN)] = jnp.zeros((MARGIN, depth, width), f32)
        for s in range(shots):
            a4[s, pl.ds(first_adj, REACH)] = jnp.zeros((REACH, depth, width), f32)
            a3[s, pl.ds(first_border, BORDER)] = jnp.zeros((BORDER, depth, width), f32)
        speed[pl.ds(first_speed, REACH)] = jnp.zeros((REACH, depth, width), f32)
        for k in range(STEPS):
            beside[k, side] = jnp.zeros(beside.shape[2:], f32)

    @pl.when(jnp.logical_not(has_left))
    def _():
        clear(0, BORDER - REACH, 0, 0, 0)

    @pl.when(jnp.logical_not(has_right))
    def _():
        clear(MARGIN + rows, BORDER + rows, BORDER + rows, REACH + rows, 1)

    across_y[...] = jnp.concatenate([banded(width, width, -43008.0)] * 2, axis=0)
    across_z[...] = jnp.concatenate([banded(group * depth, depth, -42.0)] * 2, axis=1)

    for copy in staged:
        copy.wait()
    receivers = record_cells.shape[1]
    tiles = receivers // 8
    lane = lax.broadcasted_iota(jnp.int32, (8, width), 1)
    first = here * (rows * depth)
    row_of = lambda cell: lax.div(cell, jnp.int32(width))
    lane_of = lambda cell: lax.rem(cell, jnp.int32(width))
    tile = (width, receivers)
    place = lax.broadcasted_iota(jnp.int32, tile, 0)
    span = 8 * depth
    compact = [jnp.zeros((8, width), f32) for _ in range(STEPS)]
    for s in range(shots):
        cells = record_cells[s : s + 1, :]
        rec_rows = row_of(cells) - first
        table = jnp.where(
            place == STEPS,
            jnp.broadcast_to(rec_rows.astype(f32), tile),
            jnp.broadcast_to(lane_of(cells).astype(f32), tile),
        )
        for k in range(STEPS):
            table = jnp.where(place == k, jnp.broadcast_to(observed[s, k : k + 1, :], tile), table)
        columns[s] = jnp.transpose(table)
        rec_col = columns[s, :, STEPS : STEPS + 1].astype(jnp.int32)
        rec_lane = columns[s, :, STEPS + 1 : STEPS + 2].astype(jnp.int32)
        hot[s] = (lax.broadcasted_iota(jnp.int32, (receivers, width), 1) == rec_lane).astype(f32)
        for k in range(STEPS):
            for j in range(tiles):
                column = columns[s, pl.ds(j * 8, 8), k : k + 1]
                compact[k] = jnp.where(lane == s * tiles + j, column, compact[k])
        count = src_cells.shape[1]
        padded = count + (-count) % 128
        order = lax.broadcasted_iota(jnp.int32, (padded, width), 0)
        across = lax.broadcasted_iota(jnp.int32, (padded, width), 1)
        along = lax.broadcasted_iota(jnp.int32, (1, padded), 1)
        tall = jnp.zeros((padded, width), f32)
        src_rows = jnp.full((1, padded), -1, jnp.int32)
        for j in range(count):
            cell = src_cells[s, j]
            sign = (2 * src_signs[s, j] - 1).astype(f32)
            tall = jnp.where((order == j) & (across == lane_of(cell)), sign, tall)
            src_rows = jnp.where(along == j, row_of(cell) - first, src_rows)
        tall = tall.astype(jnp.bfloat16)

        for c in range(rows * depth // span):
            cell = lax.broadcasted_iota(jnp.int32, (receivers, span), 1) + c * span
            pick[s, :, c * span : (c + 1) * span] = (
                (cell == rec_col).astype(f32).astype(jnp.bfloat16)
            )

        @pl.loop(0, rows * depth // span)
        def _(c):
            cell = lax.broadcasted_iota(jnp.int32, (span, padded), 0) + c * span
            wide = (cell == src_rows).astype(f32).astype(jnp.bfloat16)
            spots = jnp.dot(wide, tall, preferred_element_type=f32)
            spread_src[s, pl.ds(c * 8, 8)] = spots.reshape(8, depth, width)

        @pl.loop(0, (rows + 2 * BORDER) // 8)
        def _(c):
            cell = lax.broadcasted_iota(jnp.int32, (span, receivers), 0)
            cell = cell + (c * span - BORDER * depth)
            put[s, pl.ds(pl.multiple_of(c * span, span), span)] = (
                (cell == rec_rows).astype(f32).astype(jnp.bfloat16)
            )

        if s == 0:
            send(adj_halo)

    for k in range(STEPS):
        measured[k] = compact[k]

    def keep_split(ref, s, row, part, value):
        high, low = split_two(value)
        ref[s, row, part, 0:width] = high
        ref[s, row, part, width : 2 * width] = low

    everyone = tuple(range(shots))

    def mix(split, row, mixed):
        lines = [
            split[s, pl.ds(row, group)].reshape(group * depth, 2 * width) for s in everyone
        ]
        highs = jnp.concatenate([line[:, :width] for line in lines], axis=1)
        lows = jnp.concatenate([line[:, width:] for line in lines], axis=1)
        down = jnp.dot(
            across_z[...], jnp.concatenate([highs, lows], axis=0), preferred_element_type=f32
        )
        over = jnp.dot(
            jnp.concatenate(lines, axis=0), across_y[...], preferred_element_type=f32
        )
        for s in everyone:
            both = over[s * group * depth : (s + 1) * group * depth]
            both = both + down[:, s * width : (s + 1) * width]
            mixed[s, pl.ds(row, group)] = both.reshape(group, depth, width)

    def beside_x(window, i):
        summed = WEIGHTS[1] * (window[i + 3] + window[i + 5])
        for r in range(2, MARGIN + 1):
            summed += WEIGHTS[r] * (window[i + MARGIN + r] + window[i + MARGIN - r])
        return summed

    def sweep(first, last, point, ahead):
        ahead(first)

        @pl.loop(first, last, unroll=2)
        def _(g):
            point(g)
            ahead(g + 1)

    def square(first, last):
        @pl.loop(first, last)
        def _(x):
            squares[x] = (COURANT / SCALE) * speed[x] * speed[x]

    parts = [pl.ds(h * half, half) for h in range(halves)]
    def prepare(field, margin, split, split_margin):
        @pl.loop(0, rows)
        def _(x):
            for s in range(shots):
                for part in parts:
                    keep_split(split, s, x + split_margin, part, field[s, x + margin, part])

    def forward_point(k, g, which):
        x = g * group
        field, target, split = fields[k], fields[k + 1], hf[(k + 1) % 2]
        for part in parts:
            for s in which:
                window = [field[s, x + i, part] for i in range(group + 2 * MARGIN)]
                for i in range(group):
                    lap = beside_x(window, i) + mixed[s, x + i, part]
                    laps[k, s, x + i, part] = lap
                    if k == 0:
                        before = prev[s, x + i, part]
                    else:
                        before = fields[k - 1][s, x + i + MARGIN, part]
                    fresh = 2.0 * window[i + MARGIN] - before
                    fresh = fresh + pulse[s, k] * spread_src[s, x + i, part]
                    fresh = fresh + squares[x + i + REACH, part] * lap
                    target[s, x + i + MARGIN, part] = fresh
                    keep_split(split, s, x + i, part, fresh)

    def forward_inside(k):
        ahead = lambda g: mix(hf[k % 2], g * group, mixed)
        ahead(0)
        sweep(1, groups - 1, lambda g: forward_point(k, g, everyone), ahead)

    def sample(k):
        split = hf[(k + 1) % 2]
        gathered = jnp.zeros((8, width), f32)
        for s in range(shots):
            both = jnp.dot(
                pick[s],
                split[s].reshape(rows * depth, 2 * width),
                preferred_element_type=f32,
            )
            chosen = (both[:, :width] + both[:, width:]) * hot[s]
            column = jnp.sum(chosen, axis=1, keepdims=True)
            for j in range(tiles):
                gathered = jnp.where(
                    lane == s * tiles + j, column[j * 8 : (j + 1) * 8], gathered
                )
        found[k] = gathered

    def misfits(k, everywhere):
        missed = found[k] - measured[k]
        if everywhere:
            missed = missed + (beside[k, 0] + beside[k, 1])
        for s in range(shots):
            for j in range(0, tiles, 2):
                block = []
                for t in (j, j + 1):
                    at = s * tiles + t
                    block.append(missed[:, at : at + 1] * hot[s, pl.ds(t * 8, 8)])
                high, low = split_two(jnp.concatenate(block, axis=0))
                values[k, s, pl.ds(j * 8, 16), 0:width] = high
                values[k, s, pl.ds(j * 8, 16), width : 2 * width] = low

    def dropped(k, s, x):
        at = pl.multiple_of((x + BORDER) * depth, group * depth)
        both = jnp.dot(
            put[s, pl.ds(at, group * depth)], values[k, s], preferred_element_type=f32
        )
        return (both[:, :width] + both[:, width:]).reshape(group, depth, width)

    def free_point(g):
        x = g * group
        for part in parts:
            for s in range(shots):
                window = [
                    a4[s, x + BORDER - MARGIN + i, part] for i in range(group + 2 * MARGIN)
                ]
                for i in range(group):
                    lap = beside_x(window, i) + blend[s, x + BORDER + i, part]
                    fresh = 2.0 * window[i + MARGIN] - later[s, x + i, part]
                    a3[s, x + i + BORDER, part] = fresh + squares[x + i + REACH, part] * lap

    def drop_point(g, inside):
        x = g * group
        gathered = None
        for s in range(shots):
            fresh = a3[s, pl.ds(x + BORDER, group)] + dropped(STEPS - 1, s, x)
            a3[s, pl.ds(x + BORDER, group)] = fresh
            high, low = split_two(fresh)
            hb[s, pl.ds(x + BORDER, group), :, 0:width] = high
            hb[s, pl.ds(x + BORDER, group), :, width : 2 * width] = low
            if inside:
                term = fresh * laps[STEPS - 1, s, pl.ds(x, group)]
                gathered = term if gathered is None else gathered + term
        if inside:
            total[pl.ds(x, group)] = gathered

    adj = {4: a4, 3: a3, 2: a2, 1: a1}
    splits = {4: ha, 3: hb, 2: ha, 1: hb}

    def backward_point(m, g, inside):
        x = g * group
        field, after = adj[m], adj[m + 1]
        fallen = [dropped(m - 1, s, x) for s in range(shots)]
        for h, part in enumerate(parts):
            rim = slice(h * half, (h + 1) * half)
            gathered = [None] * group
            for s in range(shots):
                window = [
                    field[s, x + BORDER - MARGIN + i, part] for i in range(group + 2 * MARGIN)
                ]
                for i in range(group):
                    lap = beside_x(window, i) + blend[s, x + BORDER + i, part]
                    fresh = 2.0 * window[i + MARGIN] - after[s, x + i + BORDER, part]
                    fresh = fresh + fallen[s][i, rim]
                    fresh = fresh + squares[x + i + REACH, part] * lap
                    if m > 1:
                        adj[m - 1][s, x + i + BORDER, part] = fresh
                        keep_split(splits[m - 1], s, x + i + BORDER, part, fresh)
                    if inside:
                        term = fresh * laps[m - 1, s, x + i, part]
                        gathered[i] = term if gathered[i] is None else gathered[i] + term
            if inside:
                for i in range(group):
                    summed = total[x + i, part] + gathered[i]
                    if m > 1:
                        total[x + i, part] = summed
                    else:
                        factor = (2.0 * COURANT / SCALE) * speed[x + i + REACH, part]
                        if shares:
                            line = pl.multiple_of((x + i) * depth + h * half, half)
                            out[pl.ds(line, half), :] = factor * summed
                        else:
                            out[x + i, part] = factor * summed

    def backward(m, first, last, inside):
        ahead = lambda g: mix(splits[m], g * group + BORDER, blend)
        sweep(first, last, lambda g: backward_point(m, g, inside), ahead)

    for load in loads[:3]:
        load.wait()
    square(REACH, REACH + rows)
    prepare(f0, MARGIN, hf0, 0)
    forward_inside(0)
    for k in range(STEPS):
        rims = (0, groups - 1)
        for s in everyone:
            receive(halos[k][s])
            for g in rims:
                forward_point(k, g, (s,))
            if k + 1 < STEPS:
                send(halos[k + 1][s])
        if k == 1:
            sample(0)
            send(samples[0])
        if k + 1 < STEPS:
            forward_inside(k + 1)
        if k == 0:
            send(speed_halo)
        for s in everyone:
            if k == (1 if 2 * s < shots else 2):
                send(border_halos[s])
        if k > 0:
            sample(k)
            send(samples[k])
        if k == 0:
            for load in loads[3:]:
                load.wait()
            prepare(a4, BORDER, ha, BORDER)
            receive(adj_halo)
            sweep(0, groups, free_point, lambda g: mix(ha, g * group + BORDER, blend))
        else:
            receive(samples[k - 1])
            misfits(k - 1, True)
        if k == 2:
            receive(speed_halo)
            square(0, REACH)
            square(REACH + rows, 2 * REACH + rows)
        if shares and k == 2:
            prior.fold_noise()
    if shares:
        prior.send_noise()

    for copies in border_halos:
        sent(copies)
    misfits(STEPS - 1, False)

    @pl.loop(0, groups, unroll=2)
    def _(g):
        drop_point(g, True)

    backward(3, 1, groups - 1, True)
    receive(samples[STEPS - 1])
    misfits(STEPS - 1, True)
    for copies in border_halos:
        receive(copies)
    far = BORDER // group
    for g in range(far):
        drop_point(-1 - g, False)
        drop_point(groups + g, False)
    outer = [g for t in range(far - 1) for g in (-1 - t, groups + t)]
    reached = outer + [0, groups - 1]
    for g in reached[:2]:
        mix(splits[3], g * group + BORDER, blend)
    for n, g in enumerate(reached):
        backward_point(3, g, g not in outer)
        if n + 2 < len(reached):
            mix(splits[3], reached[n + 2] * group + BORDER, blend)
    for g in (-1, groups):
        mix(splits[2], g * group + BORDER, blend)
    for g in (-1, groups):
        backward_point(2, g, False)
    backward(2, 0, groups, True)
    backward(1, 0, groups // 2, True)
    if shares:
        prior.share_first(out)
    backward(1, groups // 2, groups, True)
    if shares:
        prior.apply(out)
    for copies in pairs:
        if not any(copies is other for other in border_halos):
            sent(copies)


def shot_gradient(
    velocity,
    prev,
    now,
    later,
    adjoint,
    wavelet,
    source_cells,
    signs,
    record_cells,
    observed,
    noise_field=None,
    step_size=None,
):
    shots, rows, depth, width = now.shape
    receivers = record_cells.shape[1]
    hbm = pl.BlockSpec(memory_space=pl.ANY)
    vmem = pl.BlockSpec(memory_space=pltpu.VMEM)
    smem = pl.BlockSpec(memory_space=pltpu.SMEM)
    f32, bf16 = jnp.float32, jnp.bfloat16
    group = MARGIN
    wide = rows + 2 * REACH
    widest = rows + 2 * BORDER
    exchanges = STEPS * shots + 2 + shots + STEPS
    doms = lax.axis_size("dom")
    shares = 0 if noise_field is None else lax.axis_size("shot")
    more, more_specs, first, last = (), [], [], []
    if shares:
        lines = (doms, rows, width)
        maps = (doms * rows, 3 * doms * rows)
        more = (noise_field.reshape(rows * depth, width), *prior_maps(doms * rows), step_size)
        more_specs = [hbm] * 3 + [smem]
        first = [pltpu.VMEM((rows * depth, width), f32)]
        last = [
            pltpu.VMEM((rows * depth, width), f32),
            pltpu.VMEM(maps, bf16),
            pltpu.VMEM(maps, bf16),
            pltpu.VMEM((shares, *lines), f32),
            pltpu.VMEM((shares, *lines), f32),
            pltpu.VMEM(lines, f32),
            pltpu.VMEM(lines, f32),
            pltpu.VMEM(lines, f32),
            pltpu.VMEM(lines, f32),
            pltpu.VMEM((doms * rows, width), f32),
            pltpu.VMEM(lines, f32),
            pltpu.VMEM(lines, f32),
            pltpu.SemaphoreType.DMA((3,)),
            pltpu.SemaphoreType.DMA((3, doms)),
            pltpu.SemaphoreType.DMA((3, doms)),
            pltpu.SemaphoreType.DMA((3 * shares,)),
            pltpu.SemaphoreType.DMA((3 * shares,)),
        ]
    else:
        first = [pltpu.VMEM((8, width), f32)]
    shape = (rows * depth, width) if shares else (rows, depth, width)
    return pl.pallas_call(
        functools.partial(wave_kernel, doms, shares),
        out_shape=jax.ShapeDtypeStruct(shape, f32),
        in_specs=[hbm] * 10 + more_specs,
        out_specs=vmem,
        scratch_shapes=first
        + [pltpu.VMEM((shots, rows + 2 * MARGIN, depth, width), f32)] * (STEPS + 1)
        + [pltpu.VMEM((shots, widest, depth, width), f32)] * STEPS
        + [
            pltpu.VMEM((shots, rows, depth, width), f32),
            pltpu.VMEM((shots, rows, depth, width), f32),
            pltpu.VMEM((wide, depth, width), f32),
            pltpu.VMEM((wide, depth, width), f32),
            pltpu.VMEM((STEPS, shots, rows, depth, width), f32),
            pltpu.VMEM((shots, rows, depth, 2 * width), bf16),
            pltpu.VMEM((shots, rows, depth, 2 * width), bf16),
            pltpu.VMEM((shots, widest, depth, 2 * width), bf16),
            pltpu.VMEM((shots, widest, depth, 2 * width), bf16),
            pltpu.VMEM((2 * width, width), bf16),
            pltpu.VMEM((shots, rows, depth, width), f32),
            pltpu.VMEM((shots, widest, depth, width), f32),
            pltpu.VMEM((group * depth, 2 * group * depth), bf16),
            pltpu.VMEM((shots, rows, depth, width), f32),
            pltpu.VMEM((shots, receivers, rows * depth), bf16),
            pltpu.VMEM((shots, widest * depth, receivers), bf16),
            pltpu.VMEM((shots, receivers, width), f32),
            pltpu.VMEM((shots, receivers, width), f32),
            pltpu.VMEM((STEPS, 8, width), f32),
            pltpu.VMEM((STEPS, 8, width), f32),
            pltpu.VMEM((STEPS, 2, 8, width), f32),
            pltpu.VMEM((STEPS, shots, receivers, 2 * width), bf16),
            pltpu.VMEM((rows, depth, width), f32),
            pltpu.SemaphoreType.DMA((5,)),
            pltpu.SemaphoreType.DMA((exchanges, 2)),
            pltpu.SemaphoreType.DMA((exchanges, 2)),
            pltpu.SMEM(wavelet.shape, f32),
            pltpu.SMEM(source_cells.shape, jnp.int32),
            pltpu.SMEM(signs.shape, jnp.int32),
            pltpu.VMEM(record_cells.shape, jnp.int32),
            pltpu.VMEM(observed.shape, f32),
            pltpu.SemaphoreType.DMA((5,)),
        ]
        + last,
        compiler_params=pltpu.CompilerParams(
            collective_id=0, has_side_effects=True, vmem_limit_bytes=56 * 1024 * 1024
        ),
    )(
        now,
        adjoint,
        prev,
        later,
        velocity,
        wavelet,
        source_cells,
        signs,
        record_cells,
        observed,
        *more,
    )


def prior_maps(length):
    wave = np.arange(length)[:, None]
    phase = wave * (2 * np.arange(length)[None, :] + 1) % (4 * length)
    factor = np.where(wave == 0, math.sqrt(1.0 / length), math.sqrt(2.0 / length))
    basis = factor * np.cos(math.pi / (2.0 * length) * phase)
    gain = 1.0 / np.sqrt(1.0 + wave / (length // 32))
    maps = []
    for weights in (gain * gain, gain):
        whole = basis.T @ (weights * basis)
        high = whole.astype(jnp.bfloat16)
        low = (whole - high.astype(np.float64)).astype(jnp.bfloat16)
        maps.append(jnp.asarray(np.concatenate([high, high, low], axis=1)))
    return maps


def cosine_basis(length):
    wave_index = jnp.arange(length, dtype=jnp.int32)[:, None]
    position = jnp.arange(length, dtype=jnp.int32)[None, :]
    phase = wave_index * (2 * position + 1) % (4 * length)
    angle = math.pi / (2.0 * length) * phase.astype(jnp.float32)
    factor = jnp.where(wave_index == 0, math.sqrt(1.0 / length), math.sqrt(2.0 / length)).astype(
        jnp.float32
    )
    return factor * jnp.cos(angle)


def prior_gain(length, cutoff):
    scaled = jnp.arange(length, dtype=jnp.float32) / float(cutoff)
    return 1.0 / jnp.sqrt(1.0 + scaled)


def precondition(gradient, noise_cols, rate):
    length = gradient.shape[0]
    basis = cosine_basis(length)
    spectrum = prior_gain(length, length // 32)[:, None]
    highest = lax.Precision.HIGHEST
    grad_hat = jnp.dot(basis, gradient.reshape(length, -1), precision=highest)
    noise_hat = jnp.dot(basis, noise_cols.reshape(length, -1), precision=highest)
    weights = spectrum * (-0.5 * rate * spectrum * grad_hat + jnp.sqrt(rate) * noise_hat)
    update = lax.dot_general(basis, weights, (((0,), (0,)), ((), ())), precision=highest)
    return update.reshape(gradient.shape)


def body(
    velocity,
    noise_field,
    step_size,
    field_prev,
    field_now,
    adjoint_next,
    adjoint_now,
    wavelet,
    source_cells,
    source_signs,
    record_cells,
    observed,
):
    fields = (
        velocity,
        field_prev,
        field_now,
        adjoint_next,
        adjoint_now,
        wavelet,
        source_cells,
        source_signs,
        record_cells,
        observed,
    )
    rate = step_size[0]
    rows, depth, width = velocity.shape
    shares = lax.axis_size("shot")
    shot_rows = width // shares
    start = lax.axis_index("shot") * shot_rows
    if depth == shares * lax.axis_size("dom"):
        moved = shot_gradient(*fields, noise_field, step_size).reshape(velocity.shape)
        return lax.dynamic_slice_in_dim(velocity, start, shot_rows, 2) + moved[:, :, :shot_rows]
    partial_value = shot_gradient(*fields)
    share = lax.psum_scatter(partial_value, "shot", scatter_dimension=2, tiled=True)
    noise_part = lax.dynamic_slice_in_dim(noise_field, start, shot_rows, 2)
    grad_cols, noise_cols = (
        lax.all_to_all(share, "dom", split_axis=2, concat_axis=0, tiled=True),
        lax.all_to_all(noise_part, "dom", split_axis=2, concat_axis=0, tiled=True),
    )
    update = precondition(grad_cols, noise_cols, rate)
    returned = lax.all_to_all(update, "dom", split_axis=0, concat_axis=2, tiled=True)
    result = lax.dynamic_slice_in_dim(velocity, start, shot_rows, 2) + returned
    return result


def solution(mesh):
    placed = (
        P("dom", None, None),
        P("dom", None, None),
        P(),
        P("shot", "dom", None, None),
        P("shot", "dom", None, None),
        P("shot", "dom", None, None),
        P("shot", "dom", None, None),
        P("shot", None),
        P("shot", None),
        P("shot", None),
        P("shot", None),
        P("shot", None, None),
    )
    return jax.shard_map(
        body, mesh=mesh, in_specs=placed, out_specs=P("dom", None, "shot"), check_vma=False
    )
```

```python
import functools
import math

import jax
import jax.numpy as jnp
import numpy as np
from jax import lax
from jax.experimental import pallas as pl
from jax.experimental.pallas import tpu as pltpu
from jax.sharding import PartitionSpec as P

STEPS = 4


COEFFS = (-205.0 / 72.0, 8.0 / 5.0, -1.0 / 5.0, 8.0 / 315.0, -1.0 / 560.0)
COURANT = 0.02


MARGIN = 4
MESH = pl.DeviceIdType.MESH


REACH = 2 * MARGIN
BORDER = 3 * MARGIN
WEIGHTS = (-43050.0, 8064.0, -1008.0, 128.0, -9.0)
SCALE = 5040.0


def split_two(value):
    high = value.astype(jnp.bfloat16)
    low = (value - high.astype(jnp.float32)).astype(jnp.bfloat16)
    return high, low


def banded(size, block, centre):
    down = lax.broadcasted_iota(jnp.int32, (size, size), 0)
    over = lax.broadcasted_iota(jnp.int32, (size, size), 1)
    apart = jnp.abs(down - over)
    band = jnp.where(apart == 0, centre, 0.0)
    for r in range(1, MARGIN + 1):
        band = jnp.where(apart == r, WEIGHTS[r], band)
    if block < size:
        band = jnp.where(down // block == over // block, band, 0.0)
    return band.astype(jnp.bfloat16)


WAVE_REFS = 36


class Prior:
    def __init__(
        self,
        doms,
        shares,
        noise_hbm,
        grad_map_hbm,
        noise_map_hbm,
        step_size,
        out,
        noise,
        grad_map,
        noise_map,
        folded,
        sums,
        own,
        noise_fold,
        noise_lines,
        grad_lines,
        base,
        update,
        returned,
        load_sem,
        send_sem,
        recv_sem,
        shot_send,
        shot_recv,
    ):
        self.doms, self.shares = doms, shares
        self.noise, self.out, self.step_size = noise, out, step_size
        self.grad_map, self.noise_map = grad_map, noise_map
        self.folded, self.sums, self.own = folded, sums, own
        self.noise_fold, self.noise_lines, self.grad_lines = noise_fold, noise_lines, grad_lines
        self.base, self.update, self.returned = base, update, returned
        self.me = lax.axis_index("shot")
        self.here = lax.axis_index("dom")
        self.depth = doms * shares
        self.fold, self.rows, self.width = folded.shape[1:]
        self.piece = self.width // shares
        self.group = lax.broadcasted_iota(jnp.int32, (self.rows, self.width), 1) // self.piece
        self.half = doms // 2
        self.near = (self.here // self.half) * self.half
        self.far = self.half - self.near
        self.loads = [
            pltpu.make_async_copy(noise_hbm, noise, load_sem.at[0]),
            pltpu.make_async_copy(noise_map_hbm, noise_map, load_sem.at[1]),
            pltpu.make_async_copy(grad_map_hbm, grad_map, load_sem.at[2]),
        ]
        turn = [lax.rem(self.here + o, self.half) for o in range(self.half)]
        self.away = [self.far + t for t in turn]
        self.close = [self.near + t for t in turn]
        self.sems = (send_sem, recv_sem)
        self.shot_sems = (shot_send, shot_recv)
        self.moves = []
        self.sharing = []

    def load(self):
        for load in self.loads:
            load.start()

    def slabs(self, source, level):
        return [
            source[pl.ds(block * self.fold + level, self.rows, stride=self.depth), :]
            for block in range(self.shares)
        ]

    def join(self, slabs, share):
        merged = None
        for block in range(self.shares):
            shift = (block - share) * self.piece
            if isinstance(share, int):
                shift = shift % self.width
                turned = pltpu.roll(slabs[block], shift, 1) if shift else slabs[block]
            else:
                shift = lax.rem(shift + self.width, self.width)
                turned = pltpu.roll(slabs[block], shift, 1)
            merged = turned if merged is None else jnp.where(self.group == block, turned, merged)
        return merged

    def exchange(self, phase, source_of, target, far):
        peers = self.away if far else self.close
        for o in range(0 if far else 1, self.half):
            index = o + (self.half if far else 0)
            move = pltpu.make_async_remote_copy(
                src_ref=source_of(peers[o]),
                dst_ref=target.at[self.here],
                send_sem=self.sems[0].at[phase, index],
                recv_sem=self.sems[1].at[phase, index],
                device_id={"dom": peers[o]},
                device_id_type=MESH,
            )
            move.start()
            self.moves.append((phase, move))

    def arrive(self, phase):
        for which, move in self.moves:
            if which == phase:
                move.wait_recv()

    def fold_noise(self):
        for load in self.loads:
            load.wait()

        @pl.loop(0, self.fold)
        def _(level):
            self.noise_fold[level] = self.join(self.slabs(self.noise, level), self.me)

    def send_noise(self):
        for far in (True, False):
            self.exchange(0, lambda d: self.noise_fold.at[d], self.noise_lines, far)
        self.noise_lines[self.here] = self.noise_fold[self.here]

    def mapped(self, matrix, lines):
        high, low = split_two(lines[...].reshape(self.doms * self.rows, self.width))
        return jnp.dot(
            matrix[...],
            jnp.concatenate([high, low, high], axis=0),
            preferred_element_type=jnp.float32,
        )

    def noise_update(self):
        self.arrive(0)
        root = jnp.sqrt(jnp.full((1, 1), self.step_size[0], jnp.float32))
        self.base[...] = root * self.mapped(self.noise_map, self.noise_lines)

    def slabs_part(self, source, level, first, count):
        return [
            source[
                pl.ds(first * self.depth + block * self.fold + level, count, stride=self.depth), :
            ]
            for block in range(self.shares)
        ]

    def share_out(self, partial, part, first, count, start, levels):
        group = self.group[:count]

        @pl.loop(0, levels, unroll=2)
        def _(i):
            slabs = self.slabs_part(partial, start + i, first, count)
            for share in range(self.shares):
                merged = None
                for block in range(self.shares):
                    shift = (block - share) * self.piece % self.width
                    turned = pltpu.roll(slabs[block], shift, 1) if shift else slabs[block]
                    if merged is None:
                        merged = turned
                    else:
                        merged = jnp.where(group == block, turned, merged)
                self.folded[share, start + i, pl.ds(first, count)] = merged

        moves = []
        for o in range(1, self.shares):
            peer = lax.rem(self.me + o, self.shares)
            index = o + part * self.shares
            span, lines = pl.ds(start, levels), pl.ds(first, count)
            move = pltpu.make_async_remote_copy(
                src_ref=self.folded.at[peer, span, lines],
                dst_ref=self.sums.at[o, span, lines],
                send_sem=self.shot_sems[0].at[index],
                recv_sem=self.shot_sems[1].at[index],
                device_id={"shot": peer},
                device_id_type=MESH,
            )
            move.start()
            moves.append(move)
        self.sharing.append(moves)

    def share_first(self, partial):
        self.share_out(partial, 0, 0, self.rows // 2, 0, self.doms)

    def apply(self, partial):
        rest = self.rows - self.rows // 2
        self.share_out(partial, 1, self.rows // 2, rest, self.far, self.half)
        self.share_out(partial, 2, self.rows // 2, rest, self.near, self.half)
        self.noise_update()
        sharing = self.sharing
        for move in sharing[0]:
            move.wait_recv()
        for far in (True, False):
            start = self.far if far else self.near
            for move in sharing[1 if far else 2]:
                move.wait_recv()
            span = pl.ds(start, self.half)
            gathered = self.folded[self.me, span]
            for o in range(1, self.shares):
                gathered = gathered + self.sums[o, span]
            self.own[span] = gathered
            self.exchange(1, lambda d: self.own.at[d], self.grad_lines, far)
        self.grad_lines[self.here] = self.own[self.here]
        self.arrive(1)
        pull = self.mapped(self.grad_map, self.grad_lines)
        fresh = self.base[...] - (0.5 * self.step_size[0]) * pull
        self.update[...] = fresh.reshape(self.doms, self.rows, self.width)
        for far in (True, False):
            self.exchange(2, lambda d: self.update.at[d], self.returned, far)
        self.returned[self.here] = self.update[self.here]
        self.arrive(2)
        for d in range(self.doms):
            line = self.returned[d]
            for block in range(self.shares):
                shift = -block * self.piece % self.width
                turned = pltpu.roll(line, shift, 1) if shift else line
                self.out[pl.ds(block * self.fold + d, self.rows, stride=self.depth), :] = turned
        for moves in sharing:
            for move in moves:
                move.wait_send()
        for _, move in self.moves:
            move.wait_send()


def wave_kernel(doms, shares, *refs):
    inputs = 14 if shares else 10
    arrays, out, scratch = refs[:inputs], refs[inputs], refs[inputs + 1 :]
    wave = arrays[:10] + (scratch[0] if shares else out,) + scratch[1:WAVE_REFS]
    small, scratch = scratch[WAVE_REFS : WAVE_REFS + 6], scratch[WAVE_REFS + 6 :]
    staged = [
        pltpu.make_async_copy(source, target, small[5].at[i])
        for i, (source, target) in enumerate(zip(arrays[5:10], small))
    ]
    for copy in staged:
        copy.start()
    wave = wave[:5] + small[:5] + wave[10:]
    rest = arrays[10:] + (out,) + scratch if shares else ()
    gradient_steps(doms, shares, rest, staged, *wave)


def gradient_steps(
    doms,
    shares,
    rest,
    staged,
    now_hbm,
    adj_hbm,
    prev_hbm,
    later_hbm,
    speed_hbm,
    pulse,
    src_cells,
    src_signs,
    record_cells,
    observed,
    out,
    f0,
    f1,
    f2,
    f3,
    f4,
    a4,
    a3,
    a2,
    a1,
    prev,
    later,
    speed,
    squares,
    laps,
    hf0,
    hf1,
    ha,
    hb,
    across_y,
    mixed,
    blend,
    across_z,
    spread_src,
    pick,
    put,
    hot,
    columns,
    measured,
    found,
    beside,
    values,
    total,
    load_sem,
    send_sem,
    recv_sem,
):
    fields = (f0, f1, f2, f3, f4)
    hf = (hf0, hf1)
    shots, rows, depth, width = prev.shape
    here = lax.axis_index("dom")
    left = jnp.maximum(here - 1, 0)
    right = jnp.minimum(here + 1, doms - 1)
    has_left = here > 0
    has_right = here < doms - 1
    group = MARGIN
    groups = rows // group
    half = 16
    halves = depth // half
    f32 = jnp.float32

    loads = [
        pltpu.make_async_copy(now_hbm, f0.at[:, pl.ds(MARGIN, rows)], load_sem.at[0]),
        pltpu.make_async_copy(speed_hbm, speed.at[pl.ds(REACH, rows)], load_sem.at[1]),
        pltpu.make_async_copy(prev_hbm, prev, load_sem.at[2]),
        pltpu.make_async_copy(adj_hbm, a4.at[:, pl.ds(BORDER, rows)], load_sem.at[3]),
        pltpu.make_async_copy(later_hbm, later, load_sem.at[4]),
    ]
    for load in loads:
        load.start()

    barrier = pltpu.get_barrier_semaphore()
    if shares:
        prior = Prior(doms, shares, *rest)
        prior.load()
        for o in range(1, doms):
            peer = {"dom": lax.rem(here + o, doms)}
            pl.semaphore_signal(barrier, inc=1, device_id=peer, device_id_type=MESH)
        for o in range(1, shares):
            peer = {"shot": lax.rem(lax.axis_index("shot") + o, shares)}
            pl.semaphore_signal(barrier, inc=1, device_id=peer, device_id_type=MESH)
        pl.semaphore_wait(barrier, doms + shares - 2)
    else:

        @pl.when(has_left)
        def _():
            pl.semaphore_signal(barrier, inc=1, device_id={"dom": left}, device_id_type=MESH)

        @pl.when(has_right)
        def _():
            pl.semaphore_signal(barrier, inc=1, device_id={"dom": right}, device_id_type=MESH)

        pl.semaphore_wait(barrier, has_left.astype(jnp.int32) + has_right.astype(jnp.int32))

    pairs = []

    def pair(low_source, high_target, high_source, low_target):
        index = len(pairs)
        to_left = pltpu.make_async_remote_copy(
            src_ref=low_source,
            dst_ref=high_target,
            send_sem=send_sem.at[index, 0],
            recv_sem=recv_sem.at[index, 1],
            device_id={"dom": left},
            device_id_type=MESH,
        )
        to_right = pltpu.make_async_remote_copy(
            src_ref=high_source,
            dst_ref=low_target,
            send_sem=send_sem.at[index, 1],
            recv_sem=recv_sem.at[index, 0],
            device_id={"dom": right},
            device_id_type=MESH,
        )
        pairs.append((to_left, to_right))
        return pairs[-1]

    def send(copies):
        @pl.when(has_left)
        def _():
            copies[0].start()

        @pl.when(has_right)
        def _():
            copies[1].start()

    def receive(copies):
        @pl.when(has_left)
        def _():
            copies[1].wait_recv()

        @pl.when(has_right)
        def _():
            copies[0].wait_recv()

    def sent(copies):
        @pl.when(has_left)
        def _():
            copies[0].wait_send()

        @pl.when(has_right)
        def _():
            copies[1].wait_send()

    halos = []
    for k in range(STEPS):
        halos.append([])
        for s in range(shots):
            field = fields[k]
            source = now_hbm if k == 0 else field
            base = 0 if k == 0 else MARGIN
            halos[k].append(
                pair(
                    source.at[s, pl.ds(base, MARGIN)],
                    field.at[s, pl.ds(MARGIN + rows, MARGIN)],
                    source.at[s, pl.ds(base + rows - MARGIN, MARGIN)],
                    field.at[s, pl.ds(0, MARGIN)],
                )
            )
    adj_halo = pair(
        adj_hbm.at[:, pl.ds(0, REACH)],
        a4.at[:, pl.ds(BORDER + rows, REACH)],
        adj_hbm.at[:, pl.ds(rows - REACH, REACH)],
        a4.at[:, pl.ds(BORDER - REACH, REACH)],
    )
    speed_halo = pair(
        speed_hbm.at[pl.ds(0, REACH)],
        speed.at[pl.ds(REACH + rows, REACH)],
        speed_hbm.at[pl.ds(rows - REACH, REACH)],
        speed.at[pl.ds(0, REACH)],
    )
    border_halos = [
        pair(
            a3.at[s, pl.ds(BORDER, BORDER)],
            a3.at[s, pl.ds(BORDER + rows, BORDER)],
            a3.at[s, pl.ds(rows, BORDER)],
            a3.at[s, pl.ds(0, BORDER)],
        )
        for s in range(shots)
    ]
    samples = [
        pair(found.at[k], beside.at[k, 1], found.at[k], beside.at[k, 0]) for k in range(STEPS)
    ]

    for s in range(shots):
        send(halos[0][s])

    def clear(first_field, first_adj, first_border, first_speed, side):
        for k in range(STEPS):
            for s in range(shots):
                fields[k][s, pl.ds(first_field, MARGIN)] = jnp.zeros((MARGIN, depth, width), f32)
        for s in range(shots):
            a4[s, pl.ds(first_adj, REACH)] = jnp.zeros((REACH, depth, width), f32)
            a3[s, pl.ds(first_border, BORDER)] = jnp.zeros((BORDER, depth, width), f32)
        speed[pl.ds(first_speed, REACH)] = jnp.zeros((REACH, depth, width), f32)
        for k in range(STEPS):
            beside[k, side] = jnp.zeros(beside.shape[2:], f32)

    @pl.when(jnp.logical_not(has_left))
    def _():
        clear(0, BORDER - REACH, 0, 0, 0)

    @pl.when(jnp.logical_not(has_right))
    def _():
        clear(MARGIN + rows, BORDER + rows, BORDER + rows, REACH + rows, 1)

    across_y[...] = jnp.concatenate([banded(width, width, -43008.0)] * 2, axis=0)
    across_z[...] = jnp.concatenate([banded(group * depth, depth, -42.0)] * 2, axis=1)

    for copy in staged:
        copy.wait()
    receivers = record_cells.shape[1]
    tiles = receivers // 8
    lane = lax.broadcasted_iota(jnp.int32, (8, width), 1)
    first = here * (rows * depth)
    row_of = lambda cell: lax.div(cell, jnp.int32(width))
    lane_of = lambda cell: lax.rem(cell, jnp.int32(width))
    tile = (width, receivers)
    place = lax.broadcasted_iota(jnp.int32, tile, 0)
    span = 8 * depth
    compact = [jnp.zeros((8, width), f32) for _ in range(STEPS)]
    for s in range(shots):
        cells = record_cells[s : s + 1, :]
        rec_rows = row_of(cells) - first
        table = jnp.where(
            place == STEPS,
            jnp.broadcast_to(rec_rows.astype(f32), tile),
            jnp.broadcast_to(lane_of(cells).astype(f32), tile),
        )
        for k in range(STEPS):
            table = jnp.where(place == k, jnp.broadcast_to(observed[s, k : k + 1, :], tile), table)
        columns[s] = jnp.transpose(table)
        rec_col = columns[s, :, STEPS : STEPS + 1].astype(jnp.int32)
        rec_lane = columns[s, :, STEPS + 1 : STEPS + 2].astype(jnp.int32)
        hot[s] = (lax.broadcasted_iota(jnp.int32, (receivers, width), 1) == rec_lane).astype(f32)
        for k in range(STEPS):
            for j in range(tiles):
                column = columns[s, pl.ds(j * 8, 8), k : k + 1]
                compact[k] = jnp.where(lane == s * tiles + j, column, compact[k])
        count = src_cells.shape[1]
        padded = count + (-count) % 128
        order = lax.broadcasted_iota(jnp.int32, (padded, width), 0)
        across = lax.broadcasted_iota(jnp.int32, (padded, width), 1)
        along = lax.broadcasted_iota(jnp.int32, (1, padded), 1)
        tall = jnp.zeros((padded, width), f32)
        src_rows = jnp.full((1, padded), -1, jnp.int32)
        for j in range(count):
            cell = src_cells[s, j]
            sign = (2 * src_signs[s, j] - 1).astype(f32)
            tall = jnp.where((order == j) & (across == lane_of(cell)), sign, tall)
            src_rows = jnp.where(along == j, row_of(cell) - first, src_rows)
        tall = tall.astype(jnp.bfloat16)

        for c in range(rows * depth // span):
            cell = lax.broadcasted_iota(jnp.int32, (receivers, span), 1) + c * span
            pick[s, :, c * span : (c + 1) * span] = (
                (cell == rec_col).astype(f32).astype(jnp.bfloat16)
            )

        @pl.loop(0, rows * depth // span)
        def _(c):
            cell = lax.broadcasted_iota(jnp.int32, (span, padded), 0) + c * span
            wide = (cell == src_rows).astype(f32).astype(jnp.bfloat16)
            spots = jnp.dot(wide, tall, preferred_element_type=f32)
            spread_src[s, pl.ds(c * 8, 8)] = spots.reshape(8, depth, width)

        @pl.loop(0, (rows + 2 * BORDER) // 8)
        def _(c):
            within = lax.broadcasted_iota(jnp.int32, (span, receivers), 0)
            within = within.astype(f32).astype(jnp.bfloat16)
            wanted = rec_rows - (c * span - BORDER * depth)
            wanted = jnp.where((wanted >= 0) & (wanted < span), wanted, -1)
            wanted = jnp.broadcast_to(wanted.astype(f32).astype(jnp.bfloat16), within.shape)
            put[s, pl.ds(pl.multiple_of(c * span, span), span)] = jnp.where(
                within == wanted, jnp.bfloat16(1), jnp.bfloat16(0)
            )

        if s == 0:
            send(adj_halo)

    for k in range(STEPS):
        measured[k] = compact[k]

    def keep_split(ref, s, row, part, value):
        high, low = split_two(value)
        ref[s, row, part, 0:width] = high
        ref[s, row, part, width : 2 * width] = low

    everyone = tuple(range(shots))

    def mix(split, row, mixed):
        lines = [
            split[s, pl.ds(row, group)].reshape(group * depth, 2 * width) for s in everyone
        ]
        highs = jnp.concatenate([line[:, :width] for line in lines], axis=1)
        lows = jnp.concatenate([line[:, width:] for line in lines], axis=1)
        down = jnp.dot(
            across_z[...], jnp.concatenate([highs, lows], axis=0), preferred_element_type=f32
        )
        over = jnp.dot(
            jnp.concatenate(lines, axis=0), across_y[...], preferred_element_type=f32
        )
        for s in everyone:
            both = over[s * group * depth : (s + 1) * group * depth]
            both = both + down[:, s * width : (s + 1) * width]
            mixed[s, pl.ds(row, group)] = both.reshape(group, depth, width)

    def beside_x(window, i):
        summed = WEIGHTS[1] * (window[i + 3] + window[i + 5])
        for r in range(2, MARGIN + 1):
            summed += WEIGHTS[r] * (window[i + MARGIN + r] + window[i + MARGIN - r])
        return summed

    def sweep(first, last, point, ahead):
        ahead(first)

        @pl.loop(first, last, unroll=2)
        def _(g):
            point(g)
            ahead(g + 1)

    def square(first, last):
        @pl.loop(first, last)
        def _(x):
            squares[x] = (COURANT / SCALE) * speed[x] * speed[x]

    parts = [pl.ds(h * half, half) for h in range(halves)]
    def prepare(field, margin, split, split_margin):
        @pl.loop(0, rows)
        def _(x):
            for s in range(shots):
                for part in parts:
                    keep_split(split, s, x + split_margin, part, field[s, x + margin, part])

    def forward_point(k, g, which):
        x = g * group
        field, target, split = fields[k], fields[k + 1], hf[(k + 1) % 2]
        for part in parts:
            for s in which:
                window = [field[s, x + i, part] for i in range(group + 2 * MARGIN)]
                for i in range(group):
                    lap = beside_x(window, i) + mixed[s, x + i, part]
                    laps[k, s, x + i, part] = lap
                    if k == 0:
                        before = prev[s, x + i, part]
                    else:
                        before = fields[k - 1][s, x + i + MARGIN, part]
                    fresh = 2.0 * window[i + MARGIN] - before
                    fresh = fresh + pulse[s, k] * spread_src[s, x + i, part]
                    fresh = fresh + squares[x + i + REACH, part] * lap
                    target[s, x + i + MARGIN, part] = fresh
                    keep_split(split, s, x + i, part, fresh)

    def forward_inside(k):
        ahead = lambda g: mix(hf[k % 2], g * group, mixed)
        ahead(0)
        sweep(1, groups - 1, lambda g: forward_point(k, g, everyone), ahead)

    def sample(k):
        split = hf[(k + 1) % 2]
        gathered = jnp.zeros((8, width), f32)
        for s in range(shots):
            both = jnp.dot(
                pick[s],
                split[s].reshape(rows * depth, 2 * width),
                preferred_element_type=f32,
            )
            chosen = (both[:, :width] + both[:, width:]) * hot[s]
            column = jnp.sum(chosen, axis=1, keepdims=True)
            for j in range(tiles):
                gathered = jnp.where(
                    lane == s * tiles + j, column[j * 8 : (j + 1) * 8], gathered
                )
        found[k] = gathered

    def misfits(k, everywhere):
        missed = found[k] - measured[k]
        if everywhere:
            missed = missed + (beside[k, 0] + beside[k, 1])
        for s in range(shots):
            for j in range(0, tiles, 2):
                block = []
                for t in (j, j + 1):
                    at = s * tiles + t
                    block.append(missed[:, at : at + 1] * hot[s, pl.ds(t * 8, 8)])
                high, low = split_two(jnp.concatenate(block, axis=0))
                values[k, s, pl.ds(j * 8, 16), 0:width] = high
                values[k, s, pl.ds(j * 8, 16), width : 2 * width] = low

    def dropped(k, s, x):
        at = pl.multiple_of((x + BORDER) * depth, group * depth)
        both = jnp.dot(
            put[s, pl.ds(at, group * depth)], values[k, s], preferred_element_type=f32
        )
        return (both[:, :width] + both[:, width:]).reshape(group, depth, width)

    def free_point(g):
        x = g * group
        for part in parts:
            for s in range(shots):
                window = [
                    a4[s, x + BORDER - MARGIN + i, part] for i in range(group + 2 * MARGIN)
                ]
                for i in range(group):
                    lap = beside_x(window, i) + blend[s, x + BORDER + i, part]
                    fresh = 2.0 * window[i + MARGIN] - later[s, x + i, part]
                    a3[s, x + i + BORDER, part] = fresh + squares[x + i + REACH, part] * lap

    def drop_point(g, inside):
        x = g * group
        gathered = None
        for s in range(shots):
            fresh = a3[s, pl.ds(x + BORDER, group)] + dropped(STEPS - 1, s, x)
            a3[s, pl.ds(x + BORDER, group)] = fresh
            high, low = split_two(fresh)
            hb[s, pl.ds(x + BORDER, group), :, 0:width] = high
            hb[s, pl.ds(x + BORDER, group), :, width : 2 * width] = low
            if inside:
                term = fresh * laps[STEPS - 1, s, pl.ds(x, group)]
                gathered = term if gathered is None else gathered + term
        if inside:
            total[pl.ds(x, group)] = gathered

    adj = {4: a4, 3: a3, 2: a2, 1: a1}
    splits = {4: ha, 3: hb, 2: ha, 1: hb}

    def backward_point(m, g, inside):
        x = g * group
        field, after = adj[m], adj[m + 1]
        fallen = [dropped(m - 1, s, x) for s in range(shots)]
        for h, part in enumerate(parts):
            rim = slice(h * half, (h + 1) * half)
            gathered = [None] * group
            for s in range(shots):
                window = [
                    field[s, x + BORDER - MARGIN + i, part] for i in range(group + 2 * MARGIN)
                ]
                for i in range(group):
                    lap = beside_x(window, i) + blend[s, x + BORDER + i, part]
                    fresh = 2.0 * window[i + MARGIN] - after[s, x + i + BORDER, part]
                    fresh = fresh + fallen[s][i, rim]
                    fresh = fresh + squares[x + i + REACH, part] * lap
                    if m > 1:
                        adj[m - 1][s, x + i + BORDER, part] = fresh
                        keep_split(splits[m - 1], s, x + i + BORDER, part, fresh)
                    if inside:
                        term = fresh * laps[m - 1, s, x + i, part]
                        gathered[i] = term if gathered[i] is None else gathered[i] + term
            if inside:
                for i in range(group):
                    summed = total[x + i, part] + gathered[i]
                    if m > 1:
                        total[x + i, part] = summed
                    else:
                        factor = (2.0 * COURANT / SCALE) * speed[x + i + REACH, part]
                        if shares:
                            line = pl.multiple_of((x + i) * depth + h * half, half)
                            out[pl.ds(line, half), :] = factor * summed
                        else:
                            out[x + i, part] = factor * summed

    def backward(m, first, last, inside):
        ahead = lambda g: mix(splits[m], g * group + BORDER, blend)
        sweep(first, last, lambda g: backward_point(m, g, inside), ahead)

    for load in loads[:3]:
        load.wait()
    square(REACH, REACH + rows)
    prepare(f0, MARGIN, hf0, 0)
    forward_inside(0)
    for k in range(STEPS):
        rims = (0, groups - 1)
        for s in everyone:
            receive(halos[k][s])
            for g in rims:
                forward_point(k, g, (s,))
            if k + 1 < STEPS:
                send(halos[k + 1][s])
        if k == 1:
            sample(0)
            send(samples[0])
        if k + 1 < STEPS:
            forward_inside(k + 1)
        if k == 0:
            send(speed_halo)
        for s in everyone:
            if k == (1 if 2 * s < shots else 2):
                send(border_halos[s])
        if k > 0:
            sample(k)
            send(samples[k])
        if k == 0:
            for load in loads[3:]:
                load.wait()
            prepare(a4, BORDER, ha, BORDER)
            receive(adj_halo)
            sweep(0, groups, free_point, lambda g: mix(ha, g * group + BORDER, blend))
        else:
            receive(samples[k - 1])
            misfits(k - 1, True)
        if k == 2:
            receive(speed_halo)
            square(0, REACH)
            square(REACH + rows, 2 * REACH + rows)
        if shares and k == 2:
            prior.fold_noise()
    if shares:
        prior.send_noise()

    for copies in border_halos:
        sent(copies)
    misfits(STEPS - 1, False)

    @pl.loop(0, groups, unroll=2)
    def _(g):
        drop_point(g, True)

    backward(3, 1, groups - 1, True)
    receive(samples[STEPS - 1])
    misfits(STEPS - 1, True)
    for copies in border_halos:
        receive(copies)
    far = BORDER // group
    for g in range(far):
        drop_point(-1 - g, False)
        drop_point(groups + g, False)
    outer = [g for t in range(far - 1) for g in (-1 - t, groups + t)]
    reached = outer + [0, groups - 1]
    for g in reached[:2]:
        mix(splits[3], g * group + BORDER, blend)
    for n, g in enumerate(reached):
        backward_point(3, g, g not in outer)
        if n + 2 < len(reached):
            mix(splits[3], reached[n + 2] * group + BORDER, blend)
    for g in (-1, groups):
        mix(splits[2], g * group + BORDER, blend)
    for g in (-1, groups):
        backward_point(2, g, False)
    front = groups // 2 + 2
    backward(2, 0, front, True)
    backward(1, 0, groups // 2, True)
    if shares:
        prior.share_first(out)
    backward(2, front, groups, True)
    backward(1, groups // 2, groups, True)
    if shares:
        prior.apply(out)
    for copies in pairs:
        if not any(copies is other for other in border_halos):
            sent(copies)


def shot_gradient(
    velocity,
    prev,
    now,
    later,
    adjoint,
    wavelet,
    source_cells,
    signs,
    record_cells,
    observed,
    noise_field=None,
    step_size=None,
):
    shots, rows, depth, width = now.shape
    receivers = record_cells.shape[1]
    hbm = pl.BlockSpec(memory_space=pl.ANY)
    vmem = pl.BlockSpec(memory_space=pltpu.VMEM)
    smem = pl.BlockSpec(memory_space=pltpu.SMEM)
    f32, bf16 = jnp.float32, jnp.bfloat16
    group = MARGIN
    wide = rows + 2 * REACH
    widest = rows + 2 * BORDER
    exchanges = STEPS * shots + 2 + shots + STEPS
    doms = lax.axis_size("dom")
    shares = 0 if noise_field is None else lax.axis_size("shot")
    more, more_specs, first, last = (), [], [], []
    if shares:
        lines = (doms, rows, width)
        maps = (doms * rows, 3 * doms * rows)
        more = (noise_field.reshape(rows * depth, width), *prior_maps(doms * rows), step_size)
        more_specs = [hbm] * 3 + [smem]
        first = [pltpu.VMEM((rows * depth, width), f32)]
        last = [
            pltpu.VMEM((rows * depth, width), f32),
            pltpu.VMEM(maps, bf16),
            pltpu.VMEM(maps, bf16),
            pltpu.VMEM((shares, *lines), f32),
            pltpu.VMEM((shares, *lines), f32),
            pltpu.VMEM(lines, f32),
            pltpu.VMEM(lines, f32),
            pltpu.VMEM(lines, f32),
            pltpu.VMEM(lines, f32),
            pltpu.VMEM((doms * rows, width), f32),
            pltpu.VMEM(lines, f32),
            pltpu.VMEM(lines, f32),
            pltpu.SemaphoreType.DMA((3,)),
            pltpu.SemaphoreType.DMA((3, doms)),
            pltpu.SemaphoreType.DMA((3, doms)),
            pltpu.SemaphoreType.DMA((3 * shares,)),
            pltpu.SemaphoreType.DMA((3 * shares,)),
        ]
    else:
        first = [pltpu.VMEM((8, width), f32)]
    shape = (rows * depth, width) if shares else (rows, depth, width)
    return pl.pallas_call(
        functools.partial(wave_kernel, doms, shares),
        out_shape=jax.ShapeDtypeStruct(shape, f32),
        in_specs=[hbm] * 10 + more_specs,
        out_specs=vmem,
        scratch_shapes=first
        + [pltpu.VMEM((shots, rows + 2 * MARGIN, depth, width), f32)] * (STEPS + 1)
        + [pltpu.VMEM((shots, widest, depth, width), f32)] * STEPS
        + [
            pltpu.VMEM((shots, rows, depth, width), f32),
            pltpu.VMEM((shots, rows, depth, width), f32),
            pltpu.VMEM((wide, depth, width), f32),
            pltpu.VMEM((wide, depth, width), f32),
            pltpu.VMEM((STEPS, shots, rows, depth, width), f32),
            pltpu.VMEM((shots, rows, depth, 2 * width), bf16),
            pltpu.VMEM((shots, rows, depth, 2 * width), bf16),
            pltpu.VMEM((shots, widest, depth, 2 * width), bf16),
            pltpu.VMEM((shots, widest, depth, 2 * width), bf16),
            pltpu.VMEM((2 * width, width), bf16),
            pltpu.VMEM((shots, rows, depth, width), f32),
            pltpu.VMEM((shots, widest, depth, width), f32),
            pltpu.VMEM((group * depth, 2 * group * depth), bf16),
            pltpu.VMEM((shots, rows, depth, width), f32),
            pltpu.VMEM((shots, receivers, rows * depth), bf16),
            pltpu.VMEM((shots, widest * depth, receivers), bf16),
            pltpu.VMEM((shots, receivers, width), f32),
            pltpu.VMEM((shots, receivers, width), f32),
            pltpu.VMEM((STEPS, 8, width), f32),
            pltpu.VMEM((STEPS, 8, width), f32),
            pltpu.VMEM((STEPS, 2, 8, width), f32),
            pltpu.VMEM((STEPS, shots, receivers, 2 * width), bf16),
            pltpu.VMEM((rows, depth, width), f32),
            pltpu.SemaphoreType.DMA((5,)),
            pltpu.SemaphoreType.DMA((exchanges, 2)),
            pltpu.SemaphoreType.DMA((exchanges, 2)),
            pltpu.SMEM(wavelet.shape, f32),
            pltpu.SMEM(source_cells.shape, jnp.int32),
            pltpu.SMEM(signs.shape, jnp.int32),
            pltpu.VMEM(record_cells.shape, jnp.int32),
            pltpu.VMEM(observed.shape, f32),
            pltpu.SemaphoreType.DMA((5,)),
        ]
        + last,
        compiler_params=pltpu.CompilerParams(
            collective_id=0, has_side_effects=True, vmem_limit_bytes=56 * 1024 * 1024
        ),
    )(
        now,
        adjoint,
        prev,
        later,
        velocity,
        wavelet,
        source_cells,
        signs,
        record_cells,
        observed,
        *more,
    )


def prior_maps(length):
    wave = np.arange(length)[:, None]
    phase = wave * (2 * np.arange(length)[None, :] + 1) % (4 * length)
    factor = np.where(wave == 0, math.sqrt(1.0 / length), math.sqrt(2.0 / length))
    basis = factor * np.cos(math.pi / (2.0 * length) * phase)
    gain = 1.0 / np.sqrt(1.0 + wave / (length // 32))
    maps = []
    for weights in (gain * gain, gain):
        whole = basis.T @ (weights * basis)
        high = whole.astype(jnp.bfloat16)
        low = (whole - high.astype(np.float64)).astype(jnp.bfloat16)
        maps.append(jnp.asarray(np.concatenate([high, high, low], axis=1)))
    return maps


def cosine_basis(length):
    wave_index = jnp.arange(length, dtype=jnp.int32)[:, None]
    position = jnp.arange(length, dtype=jnp.int32)[None, :]
    phase = wave_index * (2 * position + 1) % (4 * length)
    angle = math.pi / (2.0 * length) * phase.astype(jnp.float32)
    factor = jnp.where(wave_index == 0, math.sqrt(1.0 / length), math.sqrt(2.0 / length)).astype(
        jnp.float32
    )
    return factor * jnp.cos(angle)


def prior_gain(length, cutoff):
    scaled = jnp.arange(length, dtype=jnp.float32) / float(cutoff)
    return 1.0 / jnp.sqrt(1.0 + scaled)


def precondition(gradient, noise_cols, rate):
    length = gradient.shape[0]
    basis = cosine_basis(length)
    spectrum = prior_gain(length, length // 32)[:, None]
    highest = lax.Precision.HIGHEST
    grad_hat = jnp.dot(basis, gradient.reshape(length, -1), precision=highest)
    noise_hat = jnp.dot(basis, noise_cols.reshape(length, -1), precision=highest)
    weights = spectrum * (-0.5 * rate * spectrum * grad_hat + jnp.sqrt(rate) * noise_hat)
    update = lax.dot_general(basis, weights, (((0,), (0,)), ((), ())), precision=highest)
    return update.reshape(gradient.shape)


def body(
    velocity,
    noise_field,
    step_size,
    field_prev,
    field_now,
    adjoint_next,
    adjoint_now,
    wavelet,
    source_cells,
    source_signs,
    record_cells,
    observed,
):
    fields = (
        velocity,
        field_prev,
        field_now,
        adjoint_next,
        adjoint_now,
        wavelet,
        source_cells,
        source_signs,
        record_cells,
        observed,
    )
    rate = step_size[0]
    rows, depth, width = velocity.shape
    shares = lax.axis_size("shot")
    shot_rows = width // shares
    start = lax.axis_index("shot") * shot_rows
    if depth == shares * lax.axis_size("dom"):
        moved = shot_gradient(*fields, noise_field, step_size).reshape(velocity.shape)
        return lax.dynamic_slice_in_dim(velocity, start, shot_rows, 2) + moved[:, :, :shot_rows]
    partial_value = shot_gradient(*fields)
    share = lax.psum_scatter(partial_value, "shot", scatter_dimension=2, tiled=True)
    noise_part = lax.dynamic_slice_in_dim(noise_field, start, shot_rows, 2)
    grad_cols, noise_cols = (
        lax.all_to_all(share, "dom", split_axis=2, concat_axis=0, tiled=True),
        lax.all_to_all(noise_part, "dom", split_axis=2, concat_axis=0, tiled=True),
    )
    update = precondition(grad_cols, noise_cols, rate)
    returned = lax.all_to_all(update, "dom", split_axis=0, concat_axis=2, tiled=True)
    result = lax.dynamic_slice_in_dim(velocity, start, shot_rows, 2) + returned
    return result


def solution(mesh):
    placed = (
        P("dom", None, None),
        P("dom", None, None),
        P(),
        P("shot", "dom", None, None),
        P("shot", "dom", None, None),
        P("shot", "dom", None, None),
        P("shot", "dom", None, None),
        P("shot", None),
        P("shot", None),
        P("shot", None),
        P("shot", None),
        P("shot", None, None),
    )
    return jax.shard_map(
        body, mesh=mesh, in_specs=placed, out_specs=P("dom", None, "shot"), check_vma=False
    )
```
